512 devices in a mesh: gx: 8 (over x, core), gy: 8 (over z_hi, y), gz: 8 (over z_lo).
Axes of the slice: x: 4, y: 4, z: 16 (z_hi: 2, z_lo: 8; z = z_hi * 8 + z_lo), core: 2. Of those that a mesh axis runs over, the one named last changes fastest.
Arguments:
- magnet: float32 [3, 32, 256, 2048], P(None, 'gz', 'gx', 'gy'), may hold values from -1 to 1, as said below
- grains: int32 [32, 256, 2048], P('gz', 'gx', 'gy'), may hold values from 0 to 15
- stiffness_table: float32 [16], replicated, may hold values from 0.2 to 1
- saturation_table: float32 [16], replicated, may hold values from 0.6 to 1.4
- kernel_x: bfloat16 [8, 256], replicated, may hold values from -3 to 3
- kernel_y: bfloat16 [8, 2048], replicated, may hold values from -3 to 3
- kernel_z: bfloat16 [8, 32], replicated, may hold values from -3 to 3
- mixing: float32 [8, 3, 3], replicated, may hold values from -1.25 to 1.25
Outputs:
- magnet_next: float32 [3, 32, 256, 2048], P(None, 'gz', 'gx', 'gy')
- demag_field: float32 [16, 3, 128, 1024], P('gz', None, 'gx', 'gy')
The draws below stay inside these ranges and needn't reach their ends.
Inputs may be any that keep to these rules, and one draw needn't show every extreme that they name: `magnet`: every cell's three components form a unit vector.
All inputs are finite; a program needn't handle non-finite values.
Results may differ from the reference program's by a relative error of at most 0.00085.
The reference program's roundings to bfloat16 on the way (of `coarse`, `along_x` and `along_y`) count: a program that leaves them out, or rounds other values in their place, can miss the bound.
Values may be sent and summed in bfloat16 or wider, within the bound.
No kernel may reach another device: no remote copies, remote signals or barrier semaphores. Data moves between devices by JAX's collectives and lax.ppermute only.
A program may use at most 128 MiB of HBM per device.

```python
import math
import jax
import jax.numpy as jnp
from jax import lax

RANK = 8
MATS = 16
SUBSTEPS = 3
NX = 256
NY = 2048
NZ = 32
GX = 128
GY = 1024
GZ = 16


def draw_magnet(key, part):
    key_height, key_angle = jax.random.split(jax.random.fold_in(key, 3))
    height = jax.random.uniform(key_height, (NZ, NX, NY), jnp.float32, -1.0, 1.0)
    angle = jax.random.uniform(key_angle, (NZ, NX, NY), jnp.float32, -math.pi, math.pi)
    radial = jnp.sqrt(jnp.maximum(1.0 - height * height, 0.0))
    return jnp.stack([radial * jnp.cos(angle), radial * jnp.sin(angle), height]).astype(jnp.float32)


def kernel_line(key, extent):
    key_reach, key_values = jax.random.split(key)
    reach_len = extent * jnp.exp(jax.random.uniform(key_reach, (RANK, 1), jnp.float32, math.log(0.15), math.log(0.6)))
    offsets = jnp.arange(2 * extent, dtype=jnp.float32) - extent
    values = jnp.clip(jax.random.normal(key_values, (RANK, 2 * extent), jnp.float32), -4.0, 4.0)
    falloff = jnp.exp(-jnp.abs(offsets)[None] / reach_len) / jnp.sqrt(reach_len)
    centre = jnp.where(offsets == 0.0, 1.0, 0.0)[None]
    return (0.8 * values * falloff + centre).astype(jnp.bfloat16)


def draw_kernel_x(key, part):
    return kernel_line(jax.random.fold_in(key, 11), GX)


def draw_kernel_y(key, part):
    return kernel_line(jax.random.fold_in(key, 12), GY)


def draw_kernel_z(key, part):
    return kernel_line(jax.random.fold_in(key, 13), GZ)


def touch_ends(result, rng, smallest, high):
    dims = result.shape
    place = [jax.random.randint(jax.random.fold_in(rng, axis), (), 0, dims[axis]) for axis in range(len(dims))]
    result = result.at[tuple(place)].set(smallest)
    longest = dims.index(max(dims))
    place[longest] = (place[longest] + 1) % dims[longest]
    return result.at[tuple(place)].set(high)


def scatter_about(key, shape, deviation, reach, held_as=jnp.bfloat16):
    result = jax.random.normal(key, shape, jnp.float32) * deviation
    return jnp.minimum(jnp.maximum(result, -reach), reach).astype(held_as)


def setup_inputs(seed: int = 0) -> dict:
    key_of = jax.random.split(jax.random.key(seed), 9)
    magnet = draw_magnet(jax.random.fold_in(key_of[8], 71), 0)
    grains = touch_ends(jax.random.randint(key_of[1], (NZ, NX, NY), 0, MATS), jax.random.fold_in(key_of[1], 1), 0, MATS - 1).astype(jnp.int32)
    stiffness_table = jnp.clip(jnp.exp(jax.random.uniform(key_of[2], (MATS,), jnp.float32, math.log(0.2), math.log(1.0))), 0.2, 1.0)
    saturation_table = jnp.clip(jax.random.uniform(key_of[3], (MATS,), jnp.float32, 0.6, 1.4), 0.6, 1.4)
    kernel_x = draw_kernel_x(jax.random.fold_in(key_of[8], 71), 0)
    kernel_y = draw_kernel_y(jax.random.fold_in(key_of[8], 71), 0)
    kernel_z = draw_kernel_z(jax.random.fold_in(key_of[8], 71), 0)
    mixing = scatter_about(key_of[7], (RANK, 3, 3), (3 * RANK) ** -0.5, 1.25, jnp.float32)
    return dict(magnet=magnet, grains=grains, stiffness_table=stiffness_table, saturation_table=saturation_table, kernel_x=kernel_x, kernel_y=kernel_y, kernel_z=kernel_z, mixing=mixing)


time_step = 0.02
damping = 0.3

def toeplitz_rows(kernel, offset, extent):
    length = kernel.shape[1] // 2
    flipped = kernel[:, ::-1]
    row_ids = offset + jnp.arange(extent, dtype=jnp.int32)
    picked = jax.vmap(lambda row_index: lax.dynamic_slice_in_dim(flipped, (length - 1 - row_index).astype(jnp.int32), length, 1))(row_ids)
    return jnp.transpose(picked, (1, 0, 2))

def interior(values):
    return values[..., 1:-1, 1:-1, 1:-1]

def shifted(values, along, begin_at):
    slicer = [slice(1, -1), slice(1, -1), slice(1, -1)]
    slicer[along] = slice(begin_at, begin_at + values.shape[along - 3] - 2)
    leading = [slice(None)] * (values.ndim - 3)
    return values[tuple(leading + slicer)]

def cross_product(first_vec, second_vec):
    return jnp.stack([first_vec[1] * second_vec[2] - first_vec[2] * second_vec[1], first_vec[2] * second_vec[0] - first_vec[0] * second_vec[2], first_vec[0] * second_vec[1] - first_vec[1] * second_vec[0]])

def exchange_update(magnet_rim, stiff_rim, saturation, demag_fine):
    centre = interior(magnet_rim)
    stiff_centre = interior(stiff_rim)
    coupled = jnp.zeros_like(centre)
    for along in range(3):
        for begin_at in (0, 2):
            stiff_near = shifted(stiff_rim, along, begin_at)
            denominator = stiff_centre + stiff_near
            weight = 2.0 * stiff_centre * stiff_near / jnp.where(denominator > 0.0, denominator, 1.0)
            coupled = coupled + weight[None] * (shifted(magnet_rim, along, begin_at) - centre)
    inside = saturation > 0.0
    safe_sat = jnp.where(inside, saturation, 1.0)
    field_total = 2.0 * coupled / safe_sat[None] + demag_fine
    torque = cross_product(centre, field_total)
    raw_next = centre - time_step * (torque + damping * cross_product(centre, torque))
    length_sq = jnp.sqrt(lax.optimization_barrier(jnp.sum(raw_next * raw_next, axis=0)))
    safe_len = jnp.where(inside, length_sq, 1.0)
    return jnp.where(inside[None], raw_next / safe_len[None], 0.0)

def coarsen(magnet, saturation):
    weighted = saturation[None] * magnet
    comps, depth, width, height = weighted.shape
    shaped = weighted.reshape(comps, depth // 2, 2, width // 2, 2, height // 2, 2)
    return lax.optimization_barrier(jnp.mean(shaped, axis=(2, 4, 6))).astype(jnp.bfloat16)

def prolong(demag):
    moved = jnp.transpose(demag, (1, 0, 2, 3))
    return jnp.repeat(jnp.repeat(jnp.repeat(moved, 2, axis=1), 2, axis=2), 2, axis=3)

def reference(magnet, grains, stiffness_table, saturation_table, kernel_x, kernel_y, kernel_z, mixing):
    stiffness = stiffness_table[grains]
    saturation = saturation_table[grains]
    coarse = coarsen(magnet, saturation)
    whole_z = toeplitz_rows(kernel_z, 0, kernel_z.shape[1] // 2).astype(jnp.float32)

    def one_rank(running, inputs):
        line_x, line_y, matrix_z, mix_rank = inputs
        matrix_x = toeplitz_rows(line_x[None], 0, line_x.shape[0] // 2)[0].astype(jnp.float32)
        matrix_y = toeplitz_rows(line_y[None], 0, line_y.shape[0] // 2)[0].astype(jnp.float32)
        along_x = jnp.einsum('ab,jzby->jzay', matrix_x, coarse.astype(jnp.float32)).astype(jnp.bfloat16)
        along_y = jnp.einsum('by,jzxy->jzxb', matrix_y, along_x.astype(jnp.float32)).astype(jnp.bfloat16)
        weights = jnp.einsum('ij,az->aijz', mix_rank, matrix_z, precision=lax.Precision.HIGHEST)
        added = jnp.einsum('aijz,jzxy->aixy', weights, along_y.astype(jnp.float32), precision=lax.Precision.HIGHEST)
        return (running + added, None)
    start_field = jnp.zeros((coarse.shape[1], 3, coarse.shape[2], coarse.shape[3]), jnp.float32)
    demag, unused = lax.scan(one_rank, start_field, (kernel_x, kernel_y, whole_z, mixing))
    demag_fine = prolong(demag)
    stiff_rim = jnp.pad(stiffness, 1)
    state = magnet
    for substep in range(SUBSTEPS):
        magnet_rim = jnp.pad(state, ((0, 0), (1, 1), (1, 1), (1, 1)))
        state = exchange_update(magnet_rim, stiff_rim, saturation, demag_fine)
    return (state, demag)
```

```python
import functools

import jax
import jax.numpy as jnp
from jax import lax
from jax.experimental import pallas as pl
from jax.experimental.pallas import tpu as pltpu
from jax.sharding import PartitionSpec as P

f32, bf16, i32 = jnp.float32, jnp.bfloat16, jnp.int32
VM = pl.BlockSpec(memory_space=pltpu.VMEM)
SM = pl.BlockSpec(memory_space=pltpu.SMEM)
TIME_STEP = 0.02
DAMPING = 0.3


def iota(shape, dim):
    return lax.broadcasted_iota(i32, shape, dim)


def one_hot(condition):
    return jnp.where(condition, 1.0, 0.0).astype(bf16)


def dot(a, b, dims=((1,), (0,))):
    return lax.dot_general(a, b, (dims, ((), ())), preferred_element_type=f32)


def lookup(ids, table):
    bits = [(ids & (1 << k)) != 0 for k in range(4)]
    level = [table[k] for k in range(16)]
    for bit in bits:
        level = [jnp.where(bit, level[2 * k + 1], level[2 * k]) for k in range(len(level) // 2)]
    return level[0]


def call(body, out_shape, in_specs, scratch=(), flops=0, nbytes=0):
    outs = out_shape if isinstance(out_shape, list) else [out_shape]
    result = pl.pallas_call(
        body,
        out_shape=outs,
        in_specs=in_specs,
        out_specs=[VM] * len(outs),
        scratch_shapes=list(scratch),
        cost_estimate=pl.CostEstimate(flops=flops, bytes_accessed=nbytes, transcendentals=0),
    )
    return result


def coarse_kernel(mag, grains, sat, out, scr):
    for a in range(2):
        s0 = lookup(grains[2 * a], sat)
        s1 = lookup(grains[2 * a + 1], sat)
        for j in range(3):
            scr[j * 2 + a] = s0 * mag[j, 2 * a] + s1 * mag[j, 2 * a + 1]
    pick = one_hot(iota((256, 128), 0) == 2 * iota((256, 128), 1))
    rows = []
    for p in range(6):
        s = scr[p].reshape(16, 2, 256)
        s = s[:, 0, :] + s[:, 1, :]
        s = s + pltpu.roll(s, 255, 1)
        rows.append((s * 0.125).astype(bf16))
    out[0:96, :] = dot(jnp.concatenate(rows, axis=0), pick).astype(bf16)
    cells = [mag[j].reshape(128, 256).astype(bf16) for j in range(3)]
    cells.append(grains[...].reshape(128, 256).astype(f32).astype(bf16))
    cells = jnp.concatenate(cells, axis=0)
    k, lane = iota((16, 256), 0), iota((16, 256), 1)
    edge = one_hot(((k < 3) & (lane == k)) | ((k >= 8) & (k < 11) & (lane == 245 + k)))
    faces = dot(edge, cells, ((1,), (1,))).astype(bf16)
    for q in range(4):
        out[96 + 16 * q : 112 + 16 * q, :] = faces[:, 128 * q : 128 * (q + 1)]


def toeplitz_kernel(kyp, kxr, strip, kx_out):
    gx = lax.axis_index("gx")

    def one(r, carry):
        row = jnp.broadcast_to(kyp[pl.ds(r, 1), :], (128, 2176))
        strip[pl.ds(r, 1)] = pltpu.roll(row, 0, 1, stride=1, stride_axis=0).astype(bf16)[None]
        return carry

    lax.fori_loop(0, 8, one, 0)
    lane = iota((24, 256), 1)
    for r in range(8):
        row = pltpu.roll(jnp.broadcast_to(kxr[r : r + 1, :], (24, 256)), 0, 1, stride=1, stride_axis=0)
        total = jnp.zeros((24, 256), f32)
        for l in range(8):
            shift = (16 * l + 16 * (gx - (gx ^ l)) + 128 + 512) & 255
            total = jnp.where(lane // 16 == l, pltpu.roll(row, shift, 1), total)
        kx_out[r * 24 : (r + 1) * 24, :] = total[:, :128]


def faces_kernel(own, p7, r1, r2, r3, mag, grains, pay, face_a, rim, scr_a, scr_b):
    gx, gy = lax.axis_index("gx"), lax.axis_index("gy")
    blocks = [own[0:96], r1[0:96], r2[0:96], r3[0:96], r3[96:192], r2[96:192], r1[96:192], p7[0:96]]
    for k in range(8):
        pay[k * 96 : (k + 1) * 96, :] = blocks[k]

    def faces(ref, base):
        return jnp.concatenate([ref[base + 16 * q : base + 16 * (q + 1), :].astype(f32) for q in range(4)], axis=1)

    f1, f3, f7 = faces(r1, 192), faces(r3, 192), faces(p7, 96)
    even = (gy & 1) == 0
    fb = jnp.where((gy == 3) | (gy == 4), f7, f3)
    right, left = jnp.where(even, f1, fb), jnp.where(even, fb, f1)
    sel = jnp.concatenate([right[0:8], left[8:16]], axis=0)
    k, lane = iota((16, 128), 0), iota((16, 128), 1)
    put = one_hot(((k < 3) & (lane == k)) | ((k >= 8) & (k < 11) & (lane == 117 + k)))
    unpacked = dot(sel.astype(bf16), put, ((0,), (0,)))
    rim[...] = unpacked.astype(bf16)
    odd = (gx & 1) == 1
    for c in range(4):
        for z in range(4):
            plane = (c * 4 + z) * 32
            low = mag[c, z, 0:8, :] if c < 3 else grains[z, 0:8, :].astype(f32)
            high = mag[c, z, 24:32, :] if c < 3 else grains[z, 24:32, :].astype(f32)
            low = jnp.concatenate([low, unpacked[plane : plane + 8]], axis=1)[0:3]
            high = jnp.concatenate([high, unpacked[plane + 24 : plane + 32]], axis=1)[5:8]
            to_b, to_a = jnp.where(odd, high, low), jnp.where(odd, low, high)
            for q in range(3):
                at = q * 48 + (c * 4 + z) * 3
                scr_b[at : at + 3, :] = to_b[:, q * 128 : (q + 1) * 128]
                scr_a[at : at + 3, :] = to_a[:, q * 128 : (q + 1) * 128]
    pay[768:912, :] = scr_b[...].astype(bf16)
    face_a[...] = scr_a[...].astype(bf16)


def rims_kernel(mag, grains, rim, rc, r3, r7, low_out, high_out, scr, fa, fb):
    gx = lax.axis_index("gx")
    even = (gx & 1) == 0
    a = rc[3072:3216, :].astype(f32)
    b = jnp.where((gx == 3) | (gx == 4), r7[768:912, :].astype(f32), r3[768:912, :].astype(f32))
    fa[...] = jnp.where(even, a, b)
    fb[...] = jnp.where(even, b, a)
    for z in range(4):
        for c in range(4):
            plane = (c * 4 + z) * 32
            scr[0:32, 0:256] = mag[c, z] if c < 3 else grains[z].astype(f32)
            scr[0:32, 256:384] = rim[plane : plane + 32, :].astype(f32)
            scr[32:40, :] = jnp.zeros((8, 384), f32)
            for q in range(3):
                at = q * 48 + (c * 4 + z) * 3
                scr[32:35, q * 128 : (q + 1) * 128] = fa[at : at + 3, :]
                scr[37:40, q * 128 : (q + 1) * 128] = fb[at : at + 3, :]
            whole = scr[...].astype(bf16)
            if z < 3:
                low_out[z * 4 + c] = whole
            if z > 0:
                high_out[(z - 1) * 4 + c] = whole


def stages_kernel(own, r3, r4, r7, rc, kx, strip, wz, out, ax, ay):
    gy = lax.axis_index("gy")
    kxm = kx[...].astype(bf16)

    def x_stage(n, carry):
        kp, jz = n // 6, n % 6
        halves = []
        for half in range(2):
            at = pl.multiple_of(((2 * kp + half) * 6 + jz) * 16, 16)
            base = lambda g: pl.ds(pl.multiple_of(at + 768 * g, 16), 16)
            parts = [own[base(0)], rc[base(0)], rc[base(1)], r3[base(0)], r4[base(0)], rc[base(2)], rc[base(3)], r7[base(0)]]
            halves.append(jnp.concatenate(parts, axis=0))
        res = dot(kxm, jnp.concatenate(halves, axis=1))
        for r in range(8):
            ax[r, pl.ds(pl.multiple_of(jz * 24, 8), 24), pl.ds(pl.multiple_of(kp * 256, 256), 256)] = res[r * 24 : (r + 1) * 24]
        return carry

    lax.fori_loop(0, 24, x_stage, 0)
    ay[...] = jnp.zeros_like(ay)

    def y_stage(r, carry):
        acc = jnp.zeros((144, 256), f32)
        for kp in range(4):
            tiles = []
            for k in (2 * kp, 2 * kp + 1):
                at = pl.multiple_of(128 * (8 + gy - (gy ^ k)), 128)
                tiles.append(strip[r, :, pl.ds(at, 256)])
            acc = acc + dot(ax[r, :, kp * 256 : (kp + 1) * 256].astype(bf16), jnp.concatenate(tiles, axis=0))
        acc = acc.astype(bf16).astype(f32)
        for jz in range(6):
            for a in range(18):
                ay[a, pl.ds(r * 8 + jz, 1), :] = acc[jz * 24 + a : jz * 24 + a + 1, :]
        return carry

    lax.fori_loop(0, 8, y_stage, 0)
    w = wz[...]
    lane = iota((64, 128), 1)
    rims = jnp.zeros((64, 128), f32)
    for a in range(18):
        o3 = dot(w, ay[a].astype(bf16))
        o = pltpu.roll(o3[0:64] + o3[64:128] + o3[128:192], 192, 1)
        rims = jnp.where(lane // 2 == a, pltpu.roll(o[:, 128:], 2 * a + 1, 1), rims)
        for d in range(8):
            out[d, a * 6 : a * 6 + 6, :] = o[d * 8 : d * 8 + 6, :128]
    for d in range(8):
        out[d, 108:114, :] = rims[d * 8 : d * 8 + 6]
        out[d, 114:120, :] = jnp.zeros((6, 128), f32)


def substeps_kernel(
    mag, grains, own_low, own_high, z_low, z_high, d_own, d_low, d_high, stiff, two_over_sat,
    state_out, demag_out, m0, m1, aa, wx, wy, wz, ss, fz, field, rows, spread,
):
    gx, gy, gz = (lax.axis_index(n) for n in ("gx", "gy", "gz"))
    for q in range(6):
        demag_out[q // 3, q % 3] = d_own[pl.ds(6 + q, 16, stride=6), :]
    lane24 = iota((24, 128), 1)
    row24 = iota((24, 128), 0)
    sources = [(d_low, 3), (d_own, 0), (d_own, 3), (d_high, 0)]
    rows[...] = jnp.zeros_like(rows)
    for level in range(4):
        ref, first = sources[level]
        for i in range(3):
            g = level * 3 + i
            q = first + i
            rows[g * 24 : g * 24 + 18, 0:128] = ref[pl.ds(q, 18, stride=6), :]
            rim = jnp.broadcast_to(ref[108 + q : 109 + q, :], (24, 128))
            rows[g * 24 : g * 24 + 24, 128:256] = jnp.where(lane24 // 2 == row24, rim, 0.0)
    x = rows[...]
    hi = x.astype(bf16)
    lo = (x - hi.astype(f32)).astype(bf16)
    a, b = iota((128, 256), 0), iota((128, 256), 1)
    wide = one_hot(b // 2 == a)
    a, b = iota((128, 128), 0), iota((128, 128), 1)
    ends = one_hot(((a % 2 == 1) & (b < 2)) | ((a % 2 == 0) & (b >= 126)))
    spread[:, 0:256] = dot(hi[:, :128], wide) + dot(lo[:, :128], wide)
    spread[:, 256:384] = dot(hi[:, 128:], ends) + dot(lo[:, 128:], ends)
    r40, c24 = iota((40, 24), 0), iota((40, 24), 1)
    tall = one_hot(((r40 < 32) & (c24 == 1 + r40 // 2)) | ((r40 >= 32) & (r40 < 34) & (c24 == 17)) | ((r40 >= 38) & (c24 == 0)))
    for g in range(12):
        v = spread[g * 24 : (g + 1) * 24, :]
        hi = v.astype(bf16)
        lo = (v - hi.astype(f32)).astype(bf16)
        field[g] = dot(tall, hi) + dot(tall, lo)
    row, col = iota((40, 384), 0), iota((40, 384), 1)
    inside = ((row < 32) | ((row < 36) & (gx < 7)) | ((row >= 36) & (gx > 0))) & (
        (col < 256) | ((col < 320) & (gy < 7)) | ((col >= 320) & (gy > 0))
    )
    for p in range(10):
        z = p - 3
        if z < 0:
            whole = [z_low[p * 4 + c].astype(f32) for c in range(4)]
            ok = gz > 0
        elif z > 3:
            whole = [z_high[(z - 4) * 4 + c].astype(f32) for c in range(4)]
            ok = gz < 7
        else:
            ref, at = (own_low, z * 4) if z < 3 else (own_high, 8)
            whole = [ref[at + c].astype(f32) for c in range(4)]
            ok = gz >= 0
        for c in range(3):
            m0[c, p] = whole[c]
            if 0 <= z < 4:
                m0[c, p, 0:32, 0:256] = mag[c, z]
        ids = whole[3].astype(i32)
        aa[p] = jnp.where(inside & ok, lookup(ids, stiff), 0.0)
        ss[p] = lookup(ids, two_over_sat)

    def weight(u, v):
        den = u + v
        return 2.0 * u * v / jnp.where(den > 0.0, den, 1.0)

    for p in range(10):
        here = aa[p]
        if 1 <= p <= 8:
            wx[p] = weight(here, pltpu.roll(here, 39, 0))
            wy[p] = weight(here, pltpu.roll(here, 383, 1))
        if p < 9:
            wz[p] = weight(here, aa[p + 1])
    for step in range(3):
        src, dst = (m0, m1) if step % 2 == 0 else (m1, m0)
        first, last = step + 1, 8 - step

        def plane(p, carry):
            m = [src[c, p] for c in range(3)]
            w_up = wz[p]
            sat = ss[p]
            level = (p - 1) // 2
            h = []
            for c in range(3):
                flux = wx[p] * (pltpu.roll(m[c], 39, 0) - m[c])
                total = flux - pltpu.roll(flux, 1, 0)
                flux = wy[p] * (pltpu.roll(m[c], 383, 1) - m[c])
                total = total + (flux - pltpu.roll(flux, 1, 1))
                up = w_up * (src[c, p + 1] - m[c])
                total = total + (up - fz[c])
                fz[c] = up
                h.append(total * sat + field[level * 3 + c])
            t = [m[1] * h[2] - m[2] * h[1], m[2] * h[0] - m[0] * h[2], m[0] * h[1] - m[1] * h[0]]
            u = [m[1] * t[2] - m[2] * t[1], m[2] * t[0] - m[0] * t[2], m[0] * t[1] - m[1] * t[0]]
            raw = [m[c] - TIME_STEP * (t[c] + DAMPING * u[c]) for c in range(3)]
            scale = lax.rsqrt(jnp.maximum(raw[0] * raw[0] + raw[1] * raw[1] + raw[2] * raw[2], 1e-30))
            for c in range(3):
                if step < 2:
                    dst[c, p] = raw[c] * scale
                else:
                    state_out[c, p - 3] = (raw[c] * scale)[0:32, 0:256]
            return carry

        for c in range(3):
            fz[c] = wz[first - 1] * (src[c, first] - src[c, first - 1])
        lax.fori_loop(first, last + 1, plane, 0)


def swap(value, axis, bit):
    return lax.ppermute(value, axis, [(i, i ^ bit) for i in range(8)])


def z_weights(kernel_z, mixing):
    gz = lax.axis_index("gz")
    kz = kernel_z.astype(f32)
    own = jnp.stack([lax.dynamic_slice_in_dim(kz, 16 - 2 * gz - zl, 16, 1) for zl in range(2)])
    own = own.reshape(2, 8, 8, 2)
    w = jnp.einsum("rij,zrda->dairjz", mixing, own, precision=lax.Precision.HIGHEST).reshape(8, 6, 8, 6)
    w = jnp.pad(w, ((0, 0), (0, 2), (0, 0), (0, 2))).reshape(64, 64)
    hi = lax.reduce_precision(w, 8, 7)
    mid = lax.reduce_precision(w - hi, 8, 7)
    return jnp.concatenate([hi, mid, w - hi - mid], axis=0).astype(bf16)


def local(magnet, grains, stiffness_table, saturation_table, kernel_x, kernel_y, kernel_z, mixing):
    shape = jax.ShapeDtypeStruct
    (pay0,) = call(
        coarse_kernel, shape((160, 128), bf16), [VM, VM, SM], [pltpu.VMEM((6, 32, 256), f32)], 20_000_000, 600_000
    )(magnet, grains, saturation_table)
    kyp = jnp.pad(kernel_y.astype(f32), ((0, 0), (64, 64)))
    strip, kx = call(
        toeplitz_kernel, [shape((8, 128, 2176), bf16), shape((192, 128), f32)], [VM, VM], (), 20_000_000, 5_000_000
    )(kyp, kernel_x[:, ::-1].astype(f32))
    wz = z_weights(kernel_z, mixing)
    p7 = swap(pay0, "gy", 7)
    pay_y = jnp.concatenate([pay0[:96], p7[:96], pay0[96:]], axis=0)
    r1, r2, r3 = (swap(pay_y, "gy", k) for k in (1, 2, 3))
    pay_x, face_a, rim = call(
        faces_kernel,
        [shape((912, 128), bf16), shape((144, 128), bf16), shape((512, 128), bf16)],
        [VM] * 7,
        [pltpu.VMEM((144, 128), f32)] * 2,
        1_000_000,
        1_000_000,
    )(pay0, p7, r1, r2, r3, magnet, grains)
    x3, x4, x7 = (swap(pay_x, "gx", k) for k in (3, 4, 7))
    pay_c = jnp.concatenate([pay_x[:768], x3[:768], x4[:768], x7[:768], face_a], axis=0)
    rc = swap(pay_c, "gx", 1)
    own_low, own_high = call(
        rims_kernel,
        [shape((12, 40, 384), bf16)] * 2,
        [VM] * 6,
        [pltpu.VMEM((40, 384), f32), pltpu.VMEM((144, 128), f32), pltpu.VMEM((144, 128), f32)],
        1_000_000,
        2_000_000,
    )(magnet, grains, rim, rc, x3, x7)
    up = [(i, i + 1) for i in range(7)]
    down = [(i + 1, i) for i in range(7)]
    z_low = lax.ppermute(own_high, "gz", up)
    z_high = lax.ppermute(own_low, "gz", down)
    (parts,) = call(
        stages_kernel,
        shape((8, 120, 128), f32),
        [VM] * 8,
        [pltpu.VMEM((8, 144, 1024), f32), pltpu.VMEM((18, 64, 256), f32)],
        2_000_000_000,
        10_000_000,
    )(pay_x, x3, x4, x7, rc, kx, strip, wz)
    d_own = jnp.sum(lax.all_to_all(parts, "gz", 0, 0, tiled=True), axis=0)
    d_low = lax.ppermute(d_own, "gz", up)
    d_high = lax.ppermute(d_own, "gz", down)
    big = (10, 40, 384)
    state, demag = call(
        substeps_kernel,
        [shape((3, 4, 32, 256), f32), shape((2, 3, 16, 128), f32)],
        [VM] * 9 + [SM] * 2,
        [pltpu.VMEM((3,) + big, f32)] * 2
        + [pltpu.VMEM(big, f32)] * 5
        + [pltpu.VMEM((3, 40, 384), f32), pltpu.VMEM((12, 40, 384), f32)]
        + [pltpu.VMEM((288, 256), f32), pltpu.VMEM((288, 384), f32)],
        50_000_000,
        5_000_000,
    )(magnet, grains, own_low, own_high, z_low, z_high, d_own, d_low, d_high, stiffness_table, 2.0 / saturation_table)
    return (state, demag)


def solution(mesh):
    in_specs = (P(None, "gz", "gx", "gy"), P("gz", "gx", "gy"), P(), P(), P(), P(), P(), P())
    out_specs = (P(None, "gz", "gx", "gy"), P("gz", None, "gx", "gy"))
    return jax.shard_map(local, mesh=mesh, in_specs=in_specs, out_specs=out_specs, check_vma=False)
```

```python
import jax
import jax.numpy as jnp
from jax import lax
from jax.experimental import pallas as pl
from jax.experimental.pallas import tpu as pltpu
from jax.sharding import PartitionSpec as P


f32, bf16, i32 = jnp.float32, jnp.bfloat16, jnp.int32
VM = pl.BlockSpec(memory_space=pltpu.VMEM)
SM = pl.BlockSpec(memory_space=pltpu.SMEM)
TIME_STEP = 0.02
DAMPING = 0.3
SCALE = 32000.0


def iota(shape, dim):
    return lax.broadcasted_iota(i32, shape, dim)


def one_hot(condition):
    return jnp.where(condition, 1.0, 0.0).astype(bf16)


def dot(a, b, dims=((1,), (0,))):
    return lax.dot_general(a, b, (dims, ((), ())), preferred_element_type=f32)


def lookup(ids, table):
    bits = [(ids & (1 << k)) != 0 for k in range(4)]
    level = [table[k] for k in range(16)]
    for bit in bits:
        level = [jnp.where(bit, level[2 * k + 1], level[2 * k]) for k in range(len(level) // 2)]
    return level[0]


def call(body, out_shape, in_specs, scratch=(), flops=0, nbytes=0, vmem=24):
    outs = out_shape if isinstance(out_shape, list) else [out_shape]
    result = pl.pallas_call(
        body,
        out_shape=outs,
        in_specs=in_specs,
        out_specs=[VM] * len(outs),
        scratch_shapes=list(scratch),
        compiler_params=pltpu.CompilerParams(vmem_limit_bytes=vmem << 20),
        cost_estimate=pl.CostEstimate(flops=flops, bytes_accessed=nbytes, transcendentals=0),
    )
    return result


def coarse_kernel(mag, grains, sat, out, scr):
    for a in range(2):
        s0 = lookup(grains[2 * a], sat)
        s1 = lookup(grains[2 * a + 1], sat)
        for j in range(3):
            scr[j * 2 + a] = s0 * mag[j, 2 * a] + s1 * mag[j, 2 * a + 1]
    pick = one_hot(iota((256, 128), 0) == 2 * iota((256, 128), 1))
    rows = []
    for p in range(6):
        s = scr[p].reshape(16, 2, 256)
        s = s[:, 0, :] + s[:, 1, :]
        s = s + pltpu.roll(s, 255, 1)
        rows.append((s * 0.125).astype(bf16))
    coarse = dot(jnp.concatenate(rows, axis=0), pick).astype(bf16)
    cells = [mag[j].reshape(128, 256).astype(bf16) for j in range(3)]
    cells.append(grains[...].reshape(128, 256).astype(f32).astype(bf16))
    cells = jnp.concatenate(cells, axis=0)
    k, lane = iota((8, 256), 0), iota((8, 256), 1)
    edge = one_hot(((k < 3) & (lane == k)) | ((k >= 4) & (k < 7) & (lane == 249 + k)))
    faces = dot(edge, cells, ((1,), (1,)))
    faces = jnp.concatenate([faces[:, 128 * q : 128 * (q + 1)] for q in range(4)], axis=0).astype(bf16)
    for d in range(8):
        out[d, 0:96, :] = coarse
        out[d, 96:128, :] = faces


def toeplitz_kernel(kernel_x, kernel_y, kernel_z, mixing, strip, kx_out, wz_out, kyp):
    gx, gz = lax.axis_index("gx"), lax.axis_index("gz")
    kyp[...] = jnp.zeros_like(kyp)
    kyp[:, 0:2048] = kernel_y[...].astype(f32)
    kyp[...] = pltpu.roll(kyp[...], 64, 1)
    mirror = one_hot(iota((256, 256), 0) + iota((256, 256), 1) == 255)
    kxr = dot(kernel_x[...], mirror)
    row, col = iota((64, 32), 0), iota((64, 32), 1)
    level = 2 * (row // 8) + jnp.where(row % 8 >= 3, 1, 0) + 16 - 2 * gz
    row, col8 = iota((8, 64), 0), iota((8, 64), 1)
    total = jnp.zeros((64, 64), f32)
    for zl in range(2):
        per_rank = dot(one_hot(col == level - zl), kernel_z[...], ((1,), (1,)))
        total = total + dot(per_rank.astype(bf16), one_hot((col8 // 8 == row) & (col8 % 8 < 6) & (col8 % 2 == zl)))
    row, col = iota((64, 64), 0), iota((64, 64), 1)
    i_of = jnp.where(row % 8 < 6, row % 8 % 3, 3)
    rj_of = col // 2
    mix = jnp.zeros((64, 64), f32)
    for i in range(3):
        line = jnp.zeros((1, 64), f32)
        for r in range(8):
            for j in range(3):
                line = jnp.where(rj_of[0:1] == r * 4 + j, mixing[r, i * 3 + j], line)
        mix = jnp.where(i_of == i, line, mix)
    w = mix * total
    hi = w.astype(bf16)
    rest = w - hi.astype(f32)
    mid = rest.astype(bf16)
    wz_out[0:64] = hi
    wz_out[64:128] = mid
    wz_out[128:192] = (rest - mid.astype(f32)).astype(bf16)

    def one(r, carry):
        row = jnp.broadcast_to(kyp[pl.ds(r, 1), :], (128, 2176))
        strip[pl.ds(r, 1)] = pltpu.roll(row, 0, 1, stride=1, stride_axis=0).astype(bf16)[None]
        return carry

    lax.fori_loop(0, 8, one, 0)
    lane = iota((24, 256), 1)
    for r in range(8):
        row = pltpu.roll(jnp.broadcast_to(kxr[r : r + 1, :], (24, 256)), 0, 1, stride=1, stride_axis=0)
        total = jnp.zeros((24, 256), f32)
        for l in range(8):
            shift = (16 * l + 16 * (gx - (gx ^ l)) + 128 + 512) & 255
            total = jnp.where(lane // 16 == l, pltpu.roll(row, shift, 1), total)
        kx_out[r * 24 : (r + 1) * 24, :] = total[:, :128]


def faces_kernel(gathered, mag, grains, pay, face_a, rim, scr_a, scr_b):
    gx, gy = lax.axis_index("gx"), lax.axis_index("gy")
    for k in range(8):
        pay[k * 96 : (k + 1) * 96, :] = gathered[k, 0:96, :]

    def faces(q):
        rows = gathered[q, 96:128, :].astype(f32)
        return jnp.concatenate([rows[8 * n : 8 * (n + 1)] for n in range(4)], axis=1)

    right, left = faces(jnp.minimum(gy + 1, 7)), faces(jnp.maximum(gy - 1, 0))
    sel = jnp.where(iota((8, 512), 0) < 4, right, left)
    k, lane = iota((8, 128), 0), iota((8, 128), 1)
    put = one_hot(((k < 3) & (lane == k)) | ((k >= 4) & (k < 7) & (lane == 121 + k)))
    unpacked = dot(sel.astype(bf16), put, ((0,), (0,)))
    rim[...] = unpacked.astype(bf16)
    odd = (gx & 1) == 1
    for c in range(4):
        for z in range(4):
            plane = (c * 4 + z) * 32
            low = mag[c, z, 0:8, :] if c < 3 else grains[z, 0:8, :].astype(f32)
            high = mag[c, z, 24:32, :] if c < 3 else grains[z, 24:32, :].astype(f32)
            low = jnp.concatenate([low, unpacked[plane : plane + 8]], axis=1)[0:3]
            high = jnp.concatenate([high, unpacked[plane + 24 : plane + 32]], axis=1)[5:8]
            to_b, to_a = jnp.where(odd, high, low), jnp.where(odd, low, high)
            for q in range(3):
                at = q * 48 + (c * 4 + z) * 3
                scr_b[at : at + 3, :] = to_b[:, q * 128 : (q + 1) * 128]
                scr_a[at : at + 3, :] = to_a[:, q * 128 : (q + 1) * 128]
    pay[768:912, :] = scr_b[...].astype(bf16)
    face_a[...] = scr_a[...].astype(bf16)


def rims_kernel(mag, grains, rim, rc, r3, r7, low_out, high_out, scr, fa, fb):
    gx = lax.axis_index("gx")
    even = (gx & 1) == 0
    a = rc[3072:3216, :].astype(f32)
    b = jnp.where((gx == 3) | (gx == 4), r7[768:912, :].astype(f32), r3[768:912, :].astype(f32))
    fa[...] = jnp.where(even, a, b)
    fb[...] = jnp.where(even, b, a)
    for z in range(4):
        for c in range(4):
            plane = (c * 4 + z) * 32
            scr[0:32, 0:256] = mag[c, z] if c < 3 else grains[z].astype(f32)
            scr[0:32, 256:384] = rim[plane : plane + 32, :].astype(f32)
            scr[32:40, :] = jnp.zeros((8, 384), f32)
            for q in range(3):
                at = q * 48 + (c * 4 + z) * 3
                scr[32:35, q * 128 : (q + 1) * 128] = fa[at : at + 3, :]
                scr[37:40, q * 128 : (q + 1) * 128] = fb[at : at + 3, :]
            whole = scr[...].astype(bf16)
            if z < 3:
                low_out[z * 4 + c] = whole
            if z > 0:
                high_out[(z - 1) * 4 + c] = whole


def stages_kernel(own, r3, r4, r7, rc, kx, strip, wz, packed, ax, ay, out):
    gy = lax.axis_index("gy")
    kxm = kx[...].astype(bf16)

    def x_stage(n, carry):
        kp, jz = n // 6, n % 6
        halves = []
        for half in range(2):
            at = pl.multiple_of(((2 * kp + half) * 6 + jz) * 16, 16)
            base = lambda g: pl.ds(pl.multiple_of(at + 768 * g, 16), 16)
            parts = [own[base(0)], rc[base(0)], rc[base(1)], r3[base(0)], r4[base(0)], rc[base(2)], rc[base(3)], r7[base(0)]]
            halves.append(jnp.concatenate(parts, axis=0))
        res = dot(kxm, jnp.concatenate(halves, axis=1))
        for r in range(8):
            ax[r, pl.ds(pl.multiple_of(jz * 24, 8), 24), pl.ds(pl.multiple_of(kp * 256, 256), 256)] = res[r * 24 : (r + 1) * 24]
        return carry

    lax.fori_loop(0, 24, x_stage, 0)
    ay[...] = jnp.zeros_like(ay)

    def y_stage(r, carry):
        acc = jnp.zeros((144, 256), f32)
        for kp in range(4):
            tiles = []
            for k in (2 * kp, 2 * kp + 1):
                at = pl.multiple_of(128 * (8 + gy - k), 128)
                tiles.append(strip[r, :, pl.ds(at, 256)])
            acc = acc + dot(ax[r, :, kp * 256 : (kp + 1) * 256].astype(bf16), jnp.concatenate(tiles, axis=0))
        acc = acc.astype(bf16).astype(f32)
        for jz in range(6):
            for a in range(18):
                ay[a, pl.ds(r * 8 + jz, 1), :] = acc[jz * 24 + a : jz * 24 + a + 1, :]
        return carry

    lax.fori_loop(0, 8, y_stage, 0)
    w = wz[...]
    lane = iota((64, 128), 1)
    rims = jnp.zeros((64, 128), f32)
    for a in range(18):
        o3 = dot(w, ay[a].astype(bf16))
        o = pltpu.roll(o3[0:64] + o3[64:128] + o3[128:192], 192, 1)
        rims = jnp.where(lane // 2 == a, pltpu.roll(o[:, 128:], 2 * a + 1, 1), rims)
        for d in range(8):
            out[d, a * 6 : a * 6 + 6, :] = o[d * 8 : d * 8 + 6, :128]
    for d in range(8):
        out[d, 108:114, :] = rims[d * 8 : d * 8 + 6]
        values = out[d, 0:114, :]
        peak = jnp.max(jnp.abs(values), axis=0, keepdims=True)
        code = jnp.ceil(16.0 * jnp.log2(jnp.maximum(peak, 1e-30)))
        scaled = values * (SCALE * jnp.exp2(code * -0.0625))
        scaled = jnp.concatenate([scaled, jnp.broadcast_to(code, (6, 128))], axis=0)
        packed[d] = jnp.round(scaled).astype(i32).astype(jnp.int16)


def sum_kernel(parts, out):
    total = jnp.zeros((114, 128), f32)
    for d in range(8):
        values = parts[d].astype(i32).astype(f32)
        total = total + values[0:114] * (jnp.exp2(values[114:115] * 0.0625) * (1.0 / SCALE))
    out[0:114] = total
    out[114:120] = jnp.zeros((6, 128), f32)


def weights_kernel(mag, grains, own_low, own_high, z_low, z_high, stiff, sat, m0, hh, wx, wy, wz, ss, aa):
    gx, gy, gz = (lax.axis_index(n) for n in ("gx", "gy", "gz"))
    row, col = iota((40, 384), 0), iota((40, 384), 1)
    inside = ((row < 32) | ((row < 36) & (gx < 7)) | ((row >= 36) & (gx > 0))) & (
        (col < 256) | ((col < 320) & (gy < 7)) | ((col >= 320) & (gy > 0))
    )
    for p in range(10):
        z = p - 3
        if z < 0:
            whole = [z_low[p * 4 + c].astype(f32) for c in range(4)]
            ok = gz > 0
        elif z > 3:
            whole = [z_high[(z - 4) * 4 + c].astype(f32) for c in range(4)]
            ok = gz < 7
        else:
            ref, at = (own_low, z * 4) if z < 3 else (own_high, 8)
            whole = [ref[at + c].astype(f32) for c in range(4)]
            ok = gz >= 0
        for c in range(3):
            m0[c, p] = whole[c]
            if 0 <= z < 4:
                m0[c, p, 0:32, 0:256] = mag[c, z]
        ids = whole[3].astype(i32)
        aa[p] = jnp.where(inside & ok, lookup(ids, stiff), 0.0)
        ss[p] = 2.0 / lookup(ids, sat)

    def weight(u, v):
        den = u + v
        return 2.0 * u * v / jnp.where(den > 0.0, den, 1.0)

    for p in range(10):
        here = aa[p]
        if 1 <= p <= 8:
            wx[p] = weight(here, pltpu.roll(here, 39, 0))
            wy[p] = weight(here, pltpu.roll(here, 383, 1))
        if p < 9:
            wz[p] = weight(here, aa[p + 1])

    fz = [wz[0] * (m0[c, 1] - m0[c, 0]) for c in range(3)]
    for p in range(1, 9):
        for c in range(3):
            total, fz[c] = exchange(m0, wx, wy, wz, c, p, fz[c])
            hh[c, p - 1] = total * ss[p]


def exchange(src, wx, wy, wz, c, p, below):
    m = src[c, p]
    flux = wx[p] * (pltpu.roll(m, 39, 0) - m)
    total = flux - pltpu.roll(flux, 1, 0)
    flux = wy[p] * (pltpu.roll(m, 383, 1) - m)
    total = total + (flux - pltpu.roll(flux, 1, 1))
    up = wz[p] * (src[c, p + 1] - m)
    return total + (up - below), up


def substeps_kernel(
    m0, hh, wx, wy, wz, ss, d_own, d_low, d_high, state_out, demag_out, m1, m2, fz, field, rows, spread
):
    for q in range(6):
        demag_out[q // 3, q % 3] = d_own[pl.ds(6 + q, 16, stride=6), :]
    lane24 = iota((24, 128), 1)
    row24 = iota((24, 128), 0)
    sources = [(d_low, 3), (d_own, 0), (d_own, 3), (d_high, 0)]
    rows[...] = jnp.zeros_like(rows)
    for level in range(4):
        ref, first = sources[level]
        for i in range(3):
            g = level * 3 + i
            q = first + i
            rows[g * 24 : g * 24 + 18, 0:128] = ref[pl.ds(q, 18, stride=6), :]
            rim = jnp.broadcast_to(ref[108 + q : 109 + q, :], (24, 128))
            rows[g * 24 : g * 24 + 24, 128:256] = jnp.where(lane24 // 2 == row24, rim, 0.0)
    x = rows[...]
    hi = x.astype(bf16)
    lo = (x - hi.astype(f32)).astype(bf16)
    a, b = iota((128, 256), 0), iota((128, 256), 1)
    wide = one_hot(b // 2 == a)
    a, b = iota((128, 128), 0), iota((128, 128), 1)
    ends = one_hot(((a % 2 == 1) & (b < 2)) | ((a % 2 == 0) & (b >= 126)))
    spread[:, 0:256] = dot(hi[:, :128], wide) + dot(lo[:, :128], wide)
    spread[:, 256:384] = dot(hi[:, 128:], ends) + dot(lo[:, 128:], ends)
    r40, c24 = iota((40, 24), 0), iota((40, 24), 1)
    tall = one_hot(((r40 < 32) & (c24 == 1 + r40 // 2)) | ((r40 >= 32) & (r40 < 34) & (c24 == 17)) | ((r40 >= 38) & (c24 == 0)))
    for g in range(12):
        v = spread[g * 24 : (g + 1) * 24, :]
        hi = v.astype(bf16)
        lo = (v - hi.astype(f32)).astype(bf16)
        field[g] = dot(tall, hi) + dot(tall, lo)
    for step in range(3):
        src, dst = ((m0, m1), (m1, m2), (m2, None))[step]
        first, last = step + 1, 8 - step

        def plane(p, carry):
            m = [src[c, p] for c in range(3)]
            level = (p - 1) // 2
            h = []
            for c in range(3):
                if step == 0:
                    total = hh[c, p - 1]
                else:
                    total, up = exchange(src, wx, wy, wz, c, p, fz[c])
                    fz[c] = up
                    total = total * ss[p]
                h.append(total + field[level * 3 + c])
            t = [m[1] * h[2] - m[2] * h[1], m[2] * h[0] - m[0] * h[2], m[0] * h[1] - m[1] * h[0]]
            u = [m[1] * t[2] - m[2] * t[1], m[2] * t[0] - m[0] * t[2], m[0] * t[1] - m[1] * t[0]]
            raw = [m[c] - TIME_STEP * (t[c] + DAMPING * u[c]) for c in range(3)]
            scale = lax.rsqrt(jnp.maximum(raw[0] * raw[0] + raw[1] * raw[1] + raw[2] * raw[2], 1e-30))
            for c in range(3):
                if step < 2:
                    dst[c, p] = raw[c] * scale
                else:
                    state_out[c, p - 3] = (raw[c] * scale)[0:32, 0:256]
            return carry

        if step:
            for c in range(3):
                fz[c] = wz[first - 1] * (src[c, first] - src[c, first - 1])
        lax.fori_loop(first, last + 1, plane, 0)


def swap(value, axis, bit):
    return lax.ppermute(value, axis, [(i, i ^ bit) for i in range(8)])


def local(magnet, grains, stiffness_table, saturation_table, kernel_x, kernel_y, kernel_z, mixing):
    shape = jax.ShapeDtypeStruct
    (pay_y,) = call(
        coarse_kernel, shape((8, 128, 128), bf16), [VM, VM, SM], [pltpu.VMEM((6, 32, 256), f32)], 20_000_000, 600_000
    )(magnet, grains, saturation_table)
    gathered = lax.all_to_all(pay_y, "gy", 0, 0, tiled=True)
    strip, kx, wz = call(
        toeplitz_kernel,
        [shape((8, 128, 2176), bf16), shape((192, 128), f32), shape((192, 64), bf16)],
        [VM, VM, VM, SM],
        [pltpu.VMEM((8, 2176), f32)],
        20_000_000,
        5_000_000,
    )(kernel_x, kernel_y, kernel_z, mixing.reshape(8, 9))
    pay_x, face_a, rim = call(
        faces_kernel,
        [shape((912, 128), bf16), shape((144, 128), bf16), shape((512, 128), bf16)],
        [VM] * 3,
        [pltpu.VMEM((144, 128), f32)] * 2,
        1_000_000,
        1_000_000,
    )(gathered, magnet, grains)
    x3, x4, x7 = (swap(pay_x, "gx", k) for k in (3, 4, 7))
    pay_c = jnp.concatenate([pay_x[:768], x3[:768], x4[:768], x7[:768], face_a], axis=0)
    rc = swap(pay_c, "gx", 1)
    own_low, own_high = call(
        rims_kernel,
        [shape((12, 40, 384), bf16)] * 2,
        [VM] * 6,
        [pltpu.VMEM((40, 384), f32), pltpu.VMEM((144, 128), f32), pltpu.VMEM((144, 128), f32)],
        1_000_000,
        2_000_000,
    )(magnet, grains, rim, rc, x3, x7)
    up = [(i, i + 1) for i in range(7)]
    down = [(i + 1, i) for i in range(7)]
    z_low = lax.ppermute(own_high, "gz", up)
    z_high = lax.ppermute(own_low, "gz", down)
    (parts,) = call(
        stages_kernel,
        shape((8, 120, 128), jnp.int16),
        [VM] * 8,
        [pltpu.VMEM((8, 144, 1024), f32), pltpu.VMEM((18, 64, 256), f32), pltpu.VMEM((8, 120, 128), f32)],
        2_000_000_000,
        10_000_000,
    )(pay_x, x3, x4, x7, rc, kx, strip, wz)
    parts = lax.all_to_all(parts, "gz", 0, 0, tiled=True)
    big = (10, 40, 384)
    m0, hh, wx, wy, wz, ss = call(
        weights_kernel,
        [shape((3,) + big, f32), shape((3, 8, 40, 384), f32)] + [shape(big, f32)] * 4,
        [VM] * 6 + [SM] * 2,
        [pltpu.VMEM(big, f32)],
        20_000_000,
        5_000_000,
    )(magnet, grains, own_low, own_high, z_low, z_high, stiffness_table, saturation_table)
    (d_own,) = call(sum_kernel, shape((120, 128), f32), [VM], (), 100_000, 300_000)(parts)
    d_low = lax.ppermute(d_own, "gz", up)
    d_high = lax.ppermute(d_own, "gz", down)
    state, demag = call(
        substeps_kernel,
        [shape((3, 4, 32, 256), f32), shape((2, 3, 16, 128), f32)],
        [VM] * 9,
        [pltpu.VMEM((3,) + big, f32)] * 2
        + [pltpu.VMEM((3, 40, 384), f32), pltpu.VMEM((12, 40, 384), f32)]
        + [pltpu.VMEM((288, 256), f32), pltpu.VMEM((288, 384), f32)],
        50_000_000,
        5_000_000,
    )(m0, hh, wx, wy, wz, ss, d_own, d_low, d_high)
    return (state, demag)


def solution(mesh):
    in_specs = (P(None, "gz", "gx", "gy"), P("gz", "gx", "gy"), P(), P(), P(), P(), P(), P())
    out_specs = (P(None, "gz", "gx", "gy"), P("gz", None, "gx", "gy"))
    return jax.shard_map(local, mesh=mesh, in_specs=in_specs, out_specs=out_specs, check_vma=False)
```

```python
import jax
import jax.numpy as jnp
from jax import lax
from jax.experimental import pallas as pl
from jax.experimental.pallas import tpu as pltpu
from jax.sharding import PartitionSpec as P


f32, bf16, i32 = jnp.float32, jnp.bfloat16, jnp.int32
VM = pl.BlockSpec(memory_space=pltpu.VMEM)
SM = pl.BlockSpec(memory_space=pltpu.SMEM)
HB = pl.BlockSpec(memory_space=pltpu.MemorySpace.HBM)
TIME_STEP = 0.02
DAMPING = 0.3
SCALE = 32000.0
FULL = 67_043_328


def iota(shape, dim):
    return lax.broadcasted_iota(i32, shape, dim)


def one_hot(condition):
    return jnp.where(condition, 1.0, 0.0).astype(bf16)


def dot(a, b, dims=((1,), (0,))):
    return lax.dot_general(a, b, (dims, ((), ())), preferred_element_type=f32)


def lookup(ids, table):
    bits = [(ids & (1 << k)) != 0 for k in range(4)]
    level = [table[k] for k in range(16)]
    for bit in bits:
        level = [jnp.where(bit, level[2 * k + 1], level[2 * k]) for k in range(len(level) // 2)]
    return level[0]


def call(body, out_shape, in_specs, scratch=(), flops=0, nbytes=0, vmem=None):
    outs = out_shape if isinstance(out_shape, list) else [out_shape]
    result = pl.pallas_call(
        body,
        out_shape=outs,
        in_specs=in_specs,
        out_specs=[VM] * len(outs),
        scratch_shapes=list(scratch),
        compiler_params=pltpu.CompilerParams(vmem_limit_bytes=vmem),
        cost_estimate=pl.CostEstimate(flops=flops, bytes_accessed=nbytes, transcendentals=0),
    )
    return result


def coarse_kernel(mag, grains, sat, out, edges, cells_out, scr):
    for a in range(2):
        s0 = lookup(grains[2 * a], sat)
        s1 = lookup(grains[2 * a + 1], sat)
        for j in range(3):
            scr[j * 2 + a] = s0 * mag[j, 2 * a] + s1 * mag[j, 2 * a + 1]
    pick = one_hot(iota((256, 128), 0) == 2 * iota((256, 128), 1))
    rows = []
    for p in range(6):
        s = scr[p].reshape(16, 2, 256)
        s = s[:, 0, :] + s[:, 1, :]
        s = s + pltpu.roll(s, 255, 1)
        rows.append((s * 0.125).astype(bf16))
    coarse = dot(jnp.concatenate(rows, axis=0), pick).astype(bf16)
    cells = [mag[j].reshape(128, 256).astype(bf16) for j in range(3)]
    cells.append(grains[...].reshape(128, 256).astype(f32).astype(bf16))
    cells = jnp.concatenate(cells, axis=0)
    k, lane = iota((8, 256), 0), iota((8, 256), 1)
    edge = one_hot(((k < 3) & (lane == k)) | ((k >= 4) & (k < 7) & (lane == 249 + k)))
    faces = dot(edge, cells, ((1,), (1,)))
    faces = jnp.concatenate([faces[:, 128 * q : 128 * (q + 1)] for q in range(4)], axis=0).astype(bf16)
    out[0:96, :] = coarse
    out[96:128, :] = faces
    cells_out[...] = cells
    for c in range(4):
        for z in range(4):
            at = (c * 4 + z) * 3
            plane = mag[c, z] if c < 3 else grains[z].astype(f32)
            edges[0, at : at + 3, :] = plane[0:3]
            edges[1, at : at + 3, :] = plane[29:32]


def pair_kernel(own, other, out):
    for n in range(4):
        out[n, 0:96, :] = own[0:96]
        out[n, 96:192, :] = other[0:96]
        out[n, 192:224, :] = own[96:128]


def toeplitz_kernel(kernel_x, kernel_y, kernel_z, mixing, strip, kx_out, wz_out, kyp):
    gx, gz = lax.axis_index("gx"), lax.axis_index("gz")
    kyp[...] = jnp.zeros_like(kyp)
    kyp[:, 0:2048] = kernel_y[...].astype(f32)
    kyp[...] = pltpu.roll(kyp[...], 64, 1)
    mirror = one_hot(iota((256, 256), 0) + iota((256, 256), 1) == 255)
    kxr = dot(kernel_x[...], mirror)
    row, col = iota((64, 32), 0), iota((64, 32), 1)
    level = 2 * (row // 8) + jnp.where(row % 8 >= 3, 1, 0) + 16 - 2 * gz
    row, col8 = iota((8, 64), 0), iota((8, 64), 1)
    total = jnp.zeros((64, 64), f32)
    for zl in range(2):
        per_rank = dot(one_hot(col == level - zl), kernel_z[...], ((1,), (1,)))
        total = total + dot(per_rank.astype(bf16), one_hot((col8 // 8 == row) & (col8 % 8 < 6) & (col8 % 2 == zl)))
    row, col = iota((64, 64), 0), iota((64, 64), 1)
    i_of = jnp.where(row % 8 < 6, row % 8 % 3, 3)
    rj_of = col // 2
    mix = jnp.zeros((64, 64), f32)
    for i in range(3):
        line = jnp.zeros((1, 64), f32)
        for r in range(8):
            for j in range(3):
                line = jnp.where(rj_of[0:1] == r * 4 + j, mixing[r, i * 3 + j], line)
        mix = jnp.where(i_of == i, line, mix)
    w = mix * total
    hi = w.astype(bf16)
    rest = w - hi.astype(f32)
    mid = rest.astype(bf16)
    wz_out[0:64] = hi
    wz_out[64:128] = mid
    wz_out[128:192] = (rest - mid.astype(f32)).astype(bf16)

    def one(r, carry):
        row = jnp.broadcast_to(kyp[pl.ds(r, 1), :], (128, 2176))
        strip[pl.ds(r, 1)] = pltpu.roll(row, 0, 1, stride=1, stride_axis=0).astype(bf16)[None]
        return carry

    lax.fori_loop(0, 8, one, 0)
    lane = iota((24, 256), 1)
    for r in range(8):
        row = pltpu.roll(jnp.broadcast_to(kxr[r : r + 1, :], (24, 256)), 0, 1, stride=1, stride_axis=0)
        total = jnp.zeros((24, 256), f32)
        for l in range(8):
            block = 2 * (l % 4) + ((gx & 1) if l < 4 else 1 - (gx & 1))
            shift = (16 * l + 16 * (gx - block) + 128 + 512) & 255
            total = jnp.where(lane // 16 == l, pltpu.roll(row, shift, 1), total)
        kx_out[r * 24 : (r + 1) * 24, :] = total[:, :128]


def faces_kernel(gathered, other, edges, pay, face_a, rim, low, high):
    gx, gy = lax.axis_index("gx"), lax.axis_index("gy")
    y = gy & 3

    def faces(rows):
        return jnp.concatenate([rows[8 * n : 8 * (n + 1)] for n in range(4)], axis=1)

    across = faces(other[96:128, :].astype(f32))
    right = faces(gathered[jnp.minimum(y + 1, 3), 192:224, :].astype(f32))
    left = faces(gathered[jnp.maximum(y - 1, 0), 192:224, :].astype(f32))
    right = jnp.where(gy == 3, across, right)
    left = jnp.where(gy == 4, across, left)
    sel = jnp.where(iota((8, 512), 0) < 4, right, left)
    k, lane = iota((8, 128), 0), iota((8, 128), 1)
    put = one_hot(((k < 3) & (lane == k)) | ((k >= 4) & (k < 7) & (lane == 121 + k)))
    unpacked = dot(sel.astype(bf16), put, ((0,), (0,)))
    rim[...] = unpacked.astype(bf16)
    for n in range(16):
        low[3 * n : 3 * n + 3] = unpacked[32 * n : 32 * n + 3]
        high[3 * n : 3 * n + 3] = unpacked[32 * n + 29 : 32 * n + 32]
    odd = (gx & 1) == 1
    to_b = [jnp.where(odd, edges[1], edges[0]).astype(bf16), jnp.where(odd, high[...], low[...]).astype(bf16)]
    to_a = [jnp.where(odd, edges[0], edges[1]).astype(bf16), jnp.where(odd, low[...], high[...]).astype(bf16)]
    face_a[0:48, :] = to_a[0][:, :128]
    face_a[48:96, :] = to_a[0][:, 128:]
    face_a[96:144, :] = to_a[1]
    for n in range(4):
        for k in range(4):
            pay[n, k * 96 : (k + 1) * 96, :] = gathered[k, 0:96, :]
            pay[n, (k + 4) * 96 : (k + 5) * 96, :] = gathered[k, 96:192, :]
        pay[n, 768:816, :] = to_b[0][:, :128]
        pay[n, 816:864, :] = to_b[0][:, 128:]
        pay[n, 864:912, :] = to_b[1]


def rims_kernel(cells, rim, near, rc, low_out, high_out, scr, fa, fb):
    gx = lax.axis_index("gx")
    even = (gx & 1) == 0
    chip = gx // 2
    a = near[...].astype(f32)
    b = rc[jnp.where(even, jnp.maximum(chip - 1, 0), jnp.minimum(chip + 1, 3)), 768:912, :].astype(f32)
    fa[...] = jnp.where(even, a, b)
    fb[...] = jnp.where(even, b, a)
    for z in range(4):
        for c in range(4):
            plane = (c * 4 + z) * 32
            scr[0:32, 0:256] = cells[plane : plane + 32, :].astype(f32)
            scr[0:32, 256:384] = rim[plane : plane + 32, :].astype(f32)
            scr[32:40, :] = jnp.zeros((8, 384), f32)
            for q in range(3):
                at = q * 48 + (c * 4 + z) * 3
                scr[32:35, q * 128 : (q + 1) * 128] = fa[at : at + 3, :]
                scr[37:40, q * 128 : (q + 1) * 128] = fb[at : at + 3, :]
            whole = scr[...].astype(bf16)
            if z < 3:
                low_out[z * 4 + c] = whole
            if z > 0:
                high_out[(z - 1) * 4 + c] = whole


def stages_kernel(own, rc, kx, strip_hbm, wz, packed, ax, ay, out, strip, sem):
    gy = lax.axis_index("gy")
    kxm = kx[...].astype(bf16)
    fetch = pltpu.make_async_copy(strip_hbm, strip, sem)
    fetch.start()

    def x_stage(n, carry):
        kp, jz = n // 6, n % 6
        halves = []
        for half in range(2):
            at = pl.multiple_of(((2 * kp + half) * 6 + jz) * 16, 16)
            parts = [ref[n, pl.ds(at, 16), :] for ref in (own, rc) for n in range(4)]
            halves.append(jnp.concatenate(parts, axis=0))
        res = dot(kxm, jnp.concatenate(halves, axis=1))
        for r in range(8):
            ax[r, pl.ds(pl.multiple_of(jz * 24, 8), 24), pl.ds(pl.multiple_of(kp * 256, 256), 256)] = res[r * 24 : (r + 1) * 24]
        return carry

    lax.fori_loop(0, 24, x_stage, 0)
    ay[...] = jnp.zeros_like(ay)
    fetch.wait()

    def y_stage(r, carry):
        acc = jnp.zeros((144, 256), f32)
        for kp in range(4):
            tiles = []
            for k in (2 * kp, 2 * kp + 1):
                block = (gy & 4) + k if k < 4 else 11 - (gy & 4) - k
                at = pl.multiple_of(128 * (8 + gy - block), 128)
                tiles.append(strip[r, :, pl.ds(at, 256)])
            acc = acc + dot(ax[r, :, kp * 256 : (kp + 1) * 256].astype(bf16), jnp.concatenate(tiles, axis=0))
        acc = acc.astype(bf16).astype(f32)
        for jz in range(6):
            for a in range(18):
                ay[a, pl.ds(r * 8 + jz, 1), :] = acc[jz * 24 + a : jz * 24 + a + 1, :]
        return carry

    lax.fori_loop(0, 8, y_stage, 0)
    w = wz[...]
    lane = iota((64, 128), 1)
    rims = jnp.zeros((64, 128), f32)
    for a in range(18):
        o3 = dot(w, ay[a].astype(bf16))
        o = pltpu.roll(o3[0:64] + o3[64:128] + o3[128:192], 192, 1)
        rims = jnp.where(lane // 2 == a, pltpu.roll(o[:, 128:], 2 * a + 1, 1), rims)
        for d in range(8):
            out[d, a * 6 : a * 6 + 6, :] = o[d * 8 : d * 8 + 6, :128]
    for d in range(8):
        out[d, 108:114, :] = rims[d * 8 : d * 8 + 6]
        values = out[d, 0:114, :]
        peak = jnp.max(jnp.abs(values), axis=0, keepdims=True)
        code = jnp.ceil(16.0 * jnp.log2(jnp.maximum(peak, 1e-30)))
        scaled = values * (SCALE * jnp.exp2(code * -0.0625))
        scaled = jnp.concatenate([scaled, jnp.broadcast_to(code, (6, 128))], axis=0)
        packed[d] = jnp.round(scaled).astype(i32).astype(jnp.int16)


def sum_kernel(parts, out):
    total = jnp.zeros((114, 128), f32)
    for d in range(8):
        values = parts[d].astype(i32).astype(f32)
        total = total + values[0:114] * (jnp.exp2(values[114:115] * 0.0625) * (1.0 / SCALE))
    out[0:114] = total
    out[114:120] = jnp.zeros((6, 128), f32)


def weights_kernel(mag, own_low, own_high, z_low, z_high, stiff, sat, m0, hh, wx, wy, wz, ss, aa):
    gx, gy, gz = (lax.axis_index(n) for n in ("gx", "gy", "gz"))
    row, col = iota((40, 384), 0), iota((40, 384), 1)
    inside = ((row < 32) | ((row < 36) & (gx < 7)) | ((row >= 36) & (gx > 0))) & (
        (col < 256) | ((col < 320) & (gy < 7)) | ((col >= 320) & (gy > 0))
    )
    for p in range(10):
        z = p - 3
        if z < 0:
            whole = [z_low[p * 4 + c].astype(f32) for c in range(4)]
            ok = gz > 0
        elif z > 3:
            whole = [z_high[(z - 4) * 4 + c].astype(f32) for c in range(4)]
            ok = gz < 7
        else:
            ref, at = (own_low, z * 4) if z < 3 else (own_high, 8)
            whole = [ref[at + c].astype(f32) for c in range(4)]
            ok = gz >= 0
        for c in range(3):
            m0[c, p] = whole[c]
            if 0 <= z < 4:
                m0[c, p, 0:32, 0:256] = mag[c, z]
        ids = whole[3].astype(i32)
        aa[p] = jnp.where(inside & ok, lookup(ids, stiff), 0.0)
        ss[p] = 2.0 / lookup(ids, sat)

    def weight(u, v):
        den = u + v
        return 2.0 * u * v / jnp.where(den > 0.0, den, 1.0)

    for p in range(10):
        here = aa[p]
        if 1 <= p <= 8:
            wx[p] = weight(here, pltpu.roll(here, 39, 0))
            wy[p] = weight(here, pltpu.roll(here, 383, 1))
        if p < 9:
            wz[p] = weight(here, aa[p + 1])

    fz = [wz[0] * (m0[c, 1] - m0[c, 0]) for c in range(3)]
    for p in range(1, 9):
        for c in range(3):
            total, fz[c] = exchange(m0, wx, wy, wz, c, p, fz[c])
            hh[c, p - 1] = total * ss[p]


def exchange(src, wx, wy, wz, c, p, below):
    m = src[c, p]
    flux = wx[p] * (pltpu.roll(m, 39, 0) - m)
    total = flux - pltpu.roll(flux, 1, 0)
    flux = wy[p] * (pltpu.roll(m, 383, 1) - m)
    total = total + (flux - pltpu.roll(flux, 1, 1))
    up = wz[p] * (src[c, p + 1] - m)
    return total + (up - below), up


def substeps_kernel(
    m0_hbm, hh_hbm, wx_hbm, wy_hbm, wz_hbm, ss_hbm, d_own, d_low, d_high, state_out, demag_out,
    m0, hh, wx, wy, wz, ss, m1, m2, fz, field, rows, spread, sems,
):
    pairs = ((m0_hbm, m0), (hh_hbm, hh), (wx_hbm, wx), (wy_hbm, wy), (wz_hbm, wz), (ss_hbm, ss))
    fetches = [pltpu.make_async_copy(a, b, sems.at[n]) for n, (a, b) in enumerate(pairs)]
    for fetch in fetches:
        fetch.start()
    for q in range(6):
        demag_out[q // 3, q % 3] = d_own[pl.ds(6 + q, 16, stride=6), :]
    lane24 = iota((24, 128), 1)
    row24 = iota((24, 128), 0)
    sources = [(d_low, 3), (d_own, 0), (d_own, 3), (d_high, 0)]
    rows[...] = jnp.zeros_like(rows)
    for level in range(4):
        ref, first = sources[level]
        for i in range(3):
            g = level * 3 + i
            q = first + i
            rows[g * 24 : g * 24 + 18, 0:128] = ref[pl.ds(q, 18, stride=6), :]
            rim = jnp.broadcast_to(ref[108 + q : 109 + q, :], (24, 128))
            rows[g * 24 : g * 24 + 24, 128:256] = jnp.where(lane24 // 2 == row24, rim, 0.0)
    x = rows[...]
    hi = x.astype(bf16)
    lo = (x - hi.astype(f32)).astype(bf16)
    a, b = iota((128, 256), 0), iota((128, 256), 1)
    wide = one_hot(b // 2 == a)
    a, b = iota((128, 128), 0), iota((128, 128), 1)
    ends = one_hot(((a % 2 == 1) & (b < 2)) | ((a % 2 == 0) & (b >= 126)))
    spread[:, 0:256] = dot(hi[:, :128], wide) + dot(lo[:, :128], wide)
    spread[:, 256:384] = dot(hi[:, 128:], ends) + dot(lo[:, 128:], ends)
    r40, c24 = iota((40, 24), 0), iota((40, 24), 1)
    tall = one_hot(((r40 < 32) & (c24 == 1 + r40 // 2)) | ((r40 >= 32) & (r40 < 34) & (c24 == 17)) | ((r40 >= 38) & (c24 == 0)))
    for g in range(12):
        v = spread[g * 24 : (g + 1) * 24, :]
        hi = v.astype(bf16)
        lo = (v - hi.astype(f32)).astype(bf16)
        field[g] = dot(tall, hi) + dot(tall, lo)
    for step in range(3):
        src, dst = ((m0, m1), (m1, m2), (m2, None))[step]
        for fetch in (fetches[:2], fetches[2:], ())[step]:
            fetch.wait()
        first, last = step + 1, 8 - step

        def plane(p, carry):
            m = [src[c, p] for c in range(3)]
            level = (p - 1) // 2
            h = []
            for c in range(3):
                if step == 0:
                    total = hh[c, p - 1]
                else:
                    total, up = exchange(src, wx, wy, wz, c, p, fz[c])
                    fz[c] = up
                    total = total * ss[p]
                h.append(total + field[level * 3 + c])
            t = [m[1] * h[2] - m[2] * h[1], m[2] * h[0] - m[0] * h[2], m[0] * h[1] - m[1] * h[0]]
            u = [m[1] * t[2] - m[2] * t[1], m[2] * t[0] - m[0] * t[2], m[0] * t[1] - m[1] * t[0]]
            raw = [m[c] - TIME_STEP * (t[c] + DAMPING * u[c]) for c in range(3)]
            scale = lax.rsqrt(jnp.maximum(raw[0] * raw[0] + raw[1] * raw[1] + raw[2] * raw[2], 1e-30))
            for c in range(3):
                if step < 2:
                    dst[c, p] = raw[c] * scale
                else:
                    state_out[c, p - 3] = (raw[c] * scale)[0:32, 0:256]
            return carry

        if step:
            for c in range(3):
                fz[c] = wz[first - 1] * (src[c, first] - src[c, first - 1])
        lax.fori_loop(first, last + 1, plane, 0)


def swap(value, axis, bit):
    return lax.ppermute(value, axis, [(i, i ^ bit) for i in range(8)])


def step(magnet, grains, stiffness_table, saturation_table, kernel_x, kernel_y, kernel_z, mixing):
    shape = jax.ShapeDtypeStruct
    up = [(i, i + 1) for i in range(7)]
    down = [(i + 1, i) for i in range(7)]
    big = (10, 40, 384)
    pay, edges, cells = call(
        coarse_kernel,
        [shape((128, 128), bf16), shape((2, 48, 256), f32), shape((512, 256), bf16)],
        [VM, VM, SM],
        [pltpu.VMEM((6, 32, 256), f32)],
        20_000_000,
        600_000,
        FULL - 520_000,
    )(magnet, grains, saturation_table)
    other = swap(pay, "gy", 7)
    strip, kx, wz = call(
        toeplitz_kernel,
        [shape((8, 128, 2176), bf16), shape((192, 128), f32), shape((192, 64), bf16)],
        [VM, VM, VM, SM],
        [pltpu.VMEM((8, 2176), f32)],
        20_000_000,
        5_000_000,
    )(kernel_x, kernel_y, kernel_z, mixing.reshape(8, 9))
    (pay,) = call(pair_kernel, shape((4, 224, 128), bf16), [VM] * 2, (), 1000, 400_000, 8 << 20)(pay, other)
    groups = [[0, 1, 2, 3], [4, 5, 6, 7]]
    gathered = lax.all_to_all(pay, "gy", 0, 0, tiled=True, axis_index_groups=groups)
    pay, face_a, rim = call(
        faces_kernel,
        [shape((4, 912, 128), bf16), shape((144, 128), bf16), shape((512, 128), bf16)],
        [VM] * 3,
        [pltpu.VMEM((48, 128), f32)] * 2,
        1_000_000,
        1_000_000,
        8 << 20,
    )(gathered, other, edges)
    groups = [[0, 2, 4, 6], [1, 3, 5, 7]]
    gathered = lax.all_to_all(pay, "gx", 0, 0, tiled=True, axis_index_groups=groups)
    near = swap(face_a, "gx", 1)
    rc = swap(gathered, "gx", 1)
    own_low, own_high = call(
        rims_kernel,
        [shape((12, 40, 384), bf16)] * 2,
        [VM] * 4,
        [pltpu.VMEM((40, 384), f32), pltpu.VMEM((144, 128), f32), pltpu.VMEM((144, 128), f32)],
        1_000_000,
        2_000_000,
        12 << 20,
    )(cells, rim, near, rc)
    z_low = lax.ppermute(own_high, "gz", up)
    z_high = lax.ppermute(own_low, "gz", down)
    (parts,) = call(
        stages_kernel,
        shape((8, 120, 128), jnp.int16),
        [VM, VM, VM, HB, VM],
        [pltpu.VMEM((8, 144, 1024), f32), pltpu.VMEM((18, 64, 256), f32), pltpu.VMEM((8, 120, 128), f32)]
        + [pltpu.VMEM((8, 128, 2176), bf16), pltpu.SemaphoreType.DMA],
        2_000_000_000,
        10_000_000,
        FULL - (4 << 20),
    )(gathered, rc, kx, strip, wz)
    parts = lax.all_to_all(parts, "gz", 0, 0, tiled=True)
    fields = call(
        weights_kernel,
        [shape((3,) + big, f32), shape((3, 8, 40, 384), f32)] + [shape(big, f32)] * 4,
        [VM] * 5 + [SM] * 2,
        [pltpu.VMEM(big, f32)],
        20_000_000,
        5_000_000,
    )(magnet, own_low, own_high, z_low, z_high, stiffness_table, saturation_table)
    (d_own,) = call(sum_kernel, shape((120, 128), f32), [VM], (), 100_000, 300_000, 8 << 20)(parts)
    d_low = lax.ppermute(d_own, "gz", up)
    d_high = lax.ppermute(d_own, "gz", down)
    state, demag = call(
        substeps_kernel,
        [shape((3, 4, 32, 256), f32), shape((2, 3, 16, 128), f32)],
        [HB] * 6 + [VM] * 3,
        [pltpu.VMEM((3,) + big, f32), pltpu.VMEM((3, 8, 40, 384), f32)]
        + [pltpu.VMEM(big, f32)] * 4
        + [pltpu.VMEM((3,) + big, f32)] * 2
        + [pltpu.VMEM((3, 40, 384), f32), pltpu.VMEM((12, 40, 384), f32)]
        + [pltpu.VMEM((288, 256), f32), pltpu.VMEM((288, 384), f32), pltpu.SemaphoreType.DMA((6,))],
        50_000_000,
        5_000_000,
        FULL - 300_000,
    )(*fields, d_own, d_low, d_high)
    return (state, demag)


def solution(mesh):
    in_specs = (P(None, "gz", "gx", "gy"), P("gz", "gx", "gy"), P(), P(), P(), P(), P(), P())
    out_specs = (P(None, "gz", "gx", "gy"), P("gz", None, "gx", "gy"))
    return jax.shard_map(step, mesh=mesh, in_specs=in_specs, out_specs=out_specs, check_vma=False)
```

```python
import jax
import jax.numpy as jnp
from jax import lax
from jax.experimental import pallas as pl
from jax.experimental.pallas import tpu as pltpu
from jax.sharding import PartitionSpec as P


f32, bf16, i32 = jnp.float32, jnp.bfloat16, jnp.int32
VM = pl.BlockSpec(memory_space=pltpu.VMEM)
SM = pl.BlockSpec(memory_space=pltpu.SMEM)
HB = pl.BlockSpec(memory_space=pltpu.MemorySpace.HBM)
TIME_STEP = 0.02
DAMPING = 0.3
SCALE = 32000.0
FULL = 67_043_328


def iota(shape, dim):
    return lax.broadcasted_iota(i32, shape, dim)


def one_hot(condition):
    return jnp.where(condition, 1.0, 0.0).astype(bf16)


def dot(a, b, dims=((1,), (0,))):
    return lax.dot_general(a, b, (dims, ((), ())), preferred_element_type=f32)


def lookup(ids, table):
    bits = [(ids & (1 << k)) != 0 for k in range(4)]
    level = [table[k] for k in range(16)]
    for bit in bits:
        level = [jnp.where(bit, level[2 * k + 1], level[2 * k]) for k in range(len(level) // 2)]
    return level[0]


def call(body, out_shape, in_specs, scratch=(), flops=0, nbytes=0, vmem=None):
    outs = out_shape if isinstance(out_shape, list) else [out_shape]
    result = pl.pallas_call(
        body,
        out_shape=outs,
        in_specs=in_specs,
        out_specs=[VM] * len(outs),
        scratch_shapes=list(scratch),
        compiler_params=pltpu.CompilerParams(vmem_limit_bytes=vmem),
        cost_estimate=pl.CostEstimate(flops=flops, bytes_accessed=nbytes, transcendentals=0),
    )
    return result


def coarse_kernel(mag, grains, sat, out, edges, cells_out, scr):
    for a in range(2):
        s0 = lookup(grains[2 * a], sat)
        s1 = lookup(grains[2 * a + 1], sat)
        for j in range(3):
            scr[j * 2 + a] = s0 * mag[j, 2 * a] + s1 * mag[j, 2 * a + 1]
    pick = one_hot(iota((256, 128), 0) == 2 * iota((256, 128), 1))
    rows = []
    for p in range(6):
        s = scr[p].reshape(16, 2, 256)
        s = s[:, 0, :] + s[:, 1, :]
        s = s + pltpu.roll(s, 255, 1)
        rows.append((s * 0.125).astype(bf16))
    coarse = dot(jnp.concatenate(rows, axis=0), pick).astype(bf16)
    cells = [mag[j].reshape(128, 256).astype(bf16) for j in range(3)]
    cells.append(grains[...].reshape(128, 256).astype(f32).astype(bf16))
    cells = jnp.concatenate(cells, axis=0)
    k, lane = iota((8, 256), 0), iota((8, 256), 1)
    edge = one_hot(((k < 3) & (lane == k)) | ((k >= 4) & (k < 7) & (lane == 249 + k)))
    faces = dot(edge, cells, ((1,), (1,)))
    faces = jnp.concatenate([faces[:, 128 * q : 128 * (q + 1)] for q in range(4)], axis=0).astype(bf16)
    out[0:96, :] = coarse
    out[96:128, :] = faces
    cells_out[...] = cells
    for c in range(4):
        for z in range(4):
            at = (c * 4 + z) * 3
            plane = mag[c, z] if c < 3 else grains[z].astype(f32)
            edges[0, at : at + 3, :] = plane[0:3]
            edges[1, at : at + 3, :] = plane[29:32]


def pair_kernel(own, other, out):
    for n in range(4):
        out[n, 0:96, :] = own[0:96]
        out[n, 96:192, :] = other[0:96]
        out[n, 192:224, :] = own[96:128]


def toeplitz_kernel(kernel_x, kernel_y, kernel_z, mixing, strip, kx_out, wz_out, kyp):
    gx, gz = lax.axis_index("gx"), lax.axis_index("gz")
    kyp[...] = jnp.zeros_like(kyp)
    kyp[:, 0:2048] = kernel_y[...].astype(f32)
    mirror = one_hot(iota((256, 256), 0) + iota((256, 256), 1) == 255)
    kxr = dot(kernel_x[...], mirror)
    row, col = iota((64, 32), 0), iota((64, 32), 1)
    level = 2 * (row // 8) + jnp.where(row % 8 >= 3, 1, 0) + 16 - 2 * gz
    row, col8 = iota((8, 64), 0), iota((8, 64), 1)
    total = jnp.zeros((64, 64), f32)
    for zl in range(2):
        per_rank = dot(one_hot(col == level - zl), kernel_z[...], ((1,), (1,)))
        total = total + dot(per_rank.astype(bf16), one_hot((col8 // 8 == row) & (col8 % 8 < 6) & (col8 % 2 == zl)))
    row, col = iota((64, 64), 0), iota((64, 64), 1)
    i_of = jnp.where(row % 8 < 6, row % 8 % 3, 3)
    rj_of = col // 2
    mix = jnp.zeros((64, 64), f32)
    for i in range(3):
        line = jnp.zeros((1, 64), f32)
        for r in range(8):
            for j in range(3):
                line = jnp.where(rj_of[0:1] == r * 4 + j, mixing[i, j, r], line)
        mix = jnp.where(i_of == i, line, mix)
    w = mix * total
    hi = w.astype(bf16)
    rest = w - hi.astype(f32)
    mid = rest.astype(bf16)
    wz_out[:, 0:64] = hi
    wz_out[:, 64:128] = mid
    wz_out[:, 128:192] = (rest - mid.astype(f32)).astype(bf16)

    def one(r, carry):
        row = jnp.broadcast_to(kyp[pl.ds(r, 1), :], (128, 2176))
        strip[pl.ds(r, 1)] = pltpu.roll(row, 0, 1, stride=1, stride_axis=0).astype(bf16)[None]
        return carry

    lax.fori_loop(0, 8, one, 0)
    lane = iota((24, 256), 1)
    for r in range(8):
        row = pltpu.roll(jnp.broadcast_to(kxr[r : r + 1, :], (24, 256)), 0, 1, stride=1, stride_axis=0)
        total = jnp.zeros((24, 256), f32)
        for l in range(8):
            block = 2 * (l % 4) + ((gx & 1) if l < 4 else 1 - (gx & 1))
            shift = (16 * l + 16 * (gx - block) + 128 + 512) & 255
            total = jnp.where(lane // 16 == l, pltpu.roll(row, shift, 1), total)
        kx_out[r * 24 : (r + 1) * 24, :] = total[:, :128]


def faces_kernel(gathered, other, edges, pay, face_a, rim, low, high):
    gx, gy = lax.axis_index("gx"), lax.axis_index("gy")
    y = gy & 3

    def faces(rows):
        return jnp.concatenate([rows[8 * n : 8 * (n + 1)] for n in range(4)], axis=1)

    across = faces(other[96:128, :].astype(f32))
    right = faces(gathered[jnp.minimum(y + 1, 3), 192:224, :].astype(f32))
    left = faces(gathered[jnp.maximum(y - 1, 0), 192:224, :].astype(f32))
    right = jnp.where(gy == 3, across, right)
    left = jnp.where(gy == 4, across, left)
    sel = jnp.where(iota((8, 512), 0) < 4, right, left)
    k, lane = iota((8, 128), 0), iota((8, 128), 1)
    put = one_hot(((k < 3) & (lane == k)) | ((k >= 4) & (k < 7) & (lane == 121 + k)))
    unpacked = dot(sel.astype(bf16), put, ((0,), (0,)))
    rim[...] = unpacked.astype(bf16)
    for n in range(16):
        low[3 * n : 3 * n + 3] = unpacked[32 * n : 32 * n + 3]
        high[3 * n : 3 * n + 3] = unpacked[32 * n + 29 : 32 * n + 32]
    odd = (gx & 1) == 1
    to_b = [jnp.where(odd, edges[1], edges[0]).astype(bf16), jnp.where(odd, high[...], low[...]).astype(bf16)]
    to_a = [jnp.where(odd, edges[0], edges[1]).astype(bf16), jnp.where(odd, low[...], high[...]).astype(bf16)]
    face_a[0:48, :] = to_a[0][:, :128]
    face_a[48:96, :] = to_a[0][:, 128:]
    face_a[96:144, :] = to_a[1]
    for n in range(4):
        for k in range(4):
            pay[n, k * 96 : (k + 1) * 96, :] = gathered[k, 0:96, :]
            pay[n, (k + 4) * 96 : (k + 5) * 96, :] = gathered[k, 96:192, :]
        pay[n, 768:816, :] = to_b[0][:, :128]
        pay[n, 816:864, :] = to_b[0][:, 128:]
        pay[n, 864:912, :] = to_b[1]


def rims_kernel(cells, rim, near, rc, low_out, high_out, scr, fa, fb):
    gx = lax.axis_index("gx")
    even = (gx & 1) == 0
    chip = gx // 2
    a = near[...].astype(f32)
    b = rc[jnp.where(even, jnp.maximum(chip - 1, 0), jnp.minimum(chip + 1, 3)), 768:912, :].astype(f32)
    fa[...] = jnp.where(even, a, b)
    fb[...] = jnp.where(even, b, a)
    for z in range(4):
        for c in range(4):
            plane = (c * 4 + z) * 32
            scr[0:32, 0:256] = cells[plane : plane + 32, :].astype(f32)
            scr[0:32, 256:384] = rim[plane : plane + 32, :].astype(f32)
            scr[32:40, :] = jnp.zeros((8, 384), f32)
            for q in range(3):
                at = q * 48 + (c * 4 + z) * 3
                scr[32:35, q * 128 : (q + 1) * 128] = fa[at : at + 3, :]
                scr[37:40, q * 128 : (q + 1) * 128] = fb[at : at + 3, :]
            whole = scr[...].astype(bf16)
            if z < 3:
                low_out[z * 4 + c] = whole
            if z > 0:
                high_out[(z - 1) * 4 + c] = whole


def stages_kernel(own, rc, kx, strip_hbm, wz, packed, ax, ay, out, strip, sem):
    gy = lax.axis_index("gy")
    kxm = kx[...].astype(bf16)
    fetch = pltpu.make_async_copy(strip_hbm, strip, sem)
    fetch.start()

    def x_stage(kp, carry):
        for pair in range(3):
            res = []
            for jz in range(2):
                halves = []
                for half in range(2):
                    at = pl.multiple_of(((2 * kp + half) * 6 + 2 * pair + jz) * 16, 16)
                    parts = [ref[n, pl.ds(at, 16), :] for ref in (own, rc) for n in range(4)]
                    halves.append(jnp.concatenate(parts, axis=0))
                res.append(dot(kxm, jnp.concatenate(halves, axis=1)))
            for r in range(8):
                both = jnp.concatenate([res[0][r * 24 : (r + 1) * 24], res[1][r * 24 : (r + 1) * 24]], axis=0)
                ax[r, pair * 48 : pair * 48 + 48, pl.ds(pl.multiple_of(kp * 256, 256), 256)] = both.astype(bf16)
        return carry

    lax.fori_loop(0, 4, x_stage, 0)
    for r in range(8):
        for half in range(2):
            ay[r, half, 144:192, :] = jnp.zeros((48, 128), f32)
    fetch.wait()

    first_half = iota((128, 128), 1) < 64

    def y_stage(r, carry):
        acc = jnp.zeros((144, 256), f32)
        for kp in range(4):
            tiles = []
            for k in (2 * kp, 2 * kp + 1):
                block = (gy & 4) + k if k < 4 else 11 - (gy & 4) - k
                at = pl.multiple_of(128 * (8 + gy - block), 128)
                after, before = strip[r, :, pl.ds(at + 128, 128)], strip[r, :, pl.ds(at - 128, 128)]
                ends = jnp.where(first_half, after, before)
                tiles.append(jnp.concatenate([strip[r, :, pl.ds(at, 128)], ends], axis=1))
            acc = acc + dot(ax[r, :, kp * 256 : (kp + 1) * 256], jnp.concatenate(tiles, axis=0))
        for half in range(2):
            ay[r, half, 0:144, :] = acc[:, 128 * half : 128 * half + 128]
        return carry

    lax.fori_loop(0, 8, y_stage, 0, unroll=2)
    w = wz[...]
    lane = iota((64, 128), 1)
    rims = jnp.zeros((64, 128), f32)
    for a in range(18):
        halves = [
            jnp.concatenate([ay[r, half, pl.ds(a, 8, stride=24), :] for r in range(8)], axis=0).astype(bf16)
            for half in range(2)
        ]
        col = jnp.concatenate(halves, axis=1)
        o = dot(w, jnp.concatenate([col, col, col], axis=0))
        rims = jnp.where(lane // 2 == a, pltpu.roll(o[:, 128:], 2 * a + 1, 1), rims)
        for d in range(8):
            out[d, a * 6 : a * 6 + 6, :] = o[d * 8 : d * 8 + 6, :128]
    for d in range(8):
        out[d, 108:114, :] = rims[d * 8 : d * 8 + 6]
        values = out[d, 0:114, :]
        peak = jnp.max(jnp.abs(values), axis=0, keepdims=True)
        code = jnp.ceil(16.0 * jnp.log2(jnp.maximum(peak, 1e-30)))
        scaled = values * (SCALE * jnp.exp2(code * -0.0625))
        scaled = jnp.concatenate([scaled, jnp.broadcast_to(code, (6, 128))], axis=0)
        packed[d] = jnp.round(scaled).astype(i32).astype(jnp.int16)


def sum_kernel(parts, out):
    total = jnp.zeros((114, 128), f32)
    for d in range(8):
        values = parts[d].astype(i32).astype(f32)
        total = total + values[0:114] * (jnp.exp2(values[114:115] * 0.0625) * (1.0 / SCALE))
    out[0:114] = total
    out[114:120] = jnp.zeros((6, 128), f32)


def weights_kernel(mag, own_low, own_high, z_low, z_high, stiff, sat, m0, hh, wx, wy, wz, ss, aa):
    gx, gy, gz = (lax.axis_index(n) for n in ("gx", "gy", "gz"))
    row, col = iota((40, 384), 0), iota((40, 384), 1)
    inside = ((row < 32) | ((row < 36) & (gx < 7)) | ((row >= 36) & (gx > 0))) & (
        (col < 256) | ((col < 320) & (gy < 7)) | ((col >= 320) & (gy > 0))
    )
    for p in range(10):
        z = p - 3
        if z < 0:
            whole = [z_low[p * 4 + c].astype(f32) for c in range(4)]
            ok = gz > 0
        elif z > 3:
            whole = [z_high[(z - 4) * 4 + c].astype(f32) for c in range(4)]
            ok = gz < 7
        else:
            ref, at = (own_low, z * 4) if z < 3 else (own_high, 8)
            whole = [ref[at + c].astype(f32) for c in range(4)]
            ok = gz >= 0
        for c in range(3):
            m0[c, p] = whole[c]
            if 0 <= z < 4:
                m0[c, p, 0:32, 0:256] = mag[c, z]
        ids = whole[3].astype(i32)
        aa[p] = jnp.where(inside & ok, lookup(ids, stiff), 0.0)
        ss[p] = 2.0 / lookup(ids, sat)

    def weight(u, v):
        den = u + v
        return 2.0 * u * v / jnp.where(den > 0.0, den, 1.0)

    for p in range(10):
        here = aa[p]
        if 1 <= p <= 8:
            wx[p] = weight(here, pltpu.roll(here, 39, 0))
            wy[p] = weight(here, pltpu.roll(here, 383, 1))
        if p < 9:
            wz[p] = weight(here, aa[p + 1])

    fz = [wz[0] * (m0[c, 1] - m0[c, 0]) for c in range(3)]
    for p in range(1, 9):
        for c in range(3):
            total, fz[c] = exchange(m0, wx, wy, wz, c, p, fz[c])
            hh[c, p - 1] = total * ss[p]


def exchange(src, wx, wy, wz, c, p, below):
    m = src[c, p]
    flux = wx[p] * (pltpu.roll(m, 39, 0) - m)
    total = flux - pltpu.roll(flux, 1, 0)
    flux = wy[p] * (pltpu.roll(m, 383, 1) - m)
    total = total + (flux - pltpu.roll(flux, 1, 1))
    up = wz[p] * (src[c, p + 1] - m)
    return total + (up - below), up


def substeps_kernel(
    m0_hbm, hh_hbm, wx_hbm, wy_hbm, wz_hbm, ss_hbm, d_own, d_low, d_high, state_out, demag_out,
    m0, hh, wx, wy, wz, ss, m1, m2, fz, field, rows, spread, sems,
):
    pairs = ((m0_hbm, m0), (hh_hbm, hh), (wx_hbm, wx), (wy_hbm, wy), (wz_hbm, wz), (ss_hbm, ss))
    fetches = [pltpu.make_async_copy(a, b, sems.at[n]) for n, (a, b) in enumerate(pairs)]
    for fetch in fetches[:2]:
        fetch.start()
    for q in range(6):
        demag_out[q // 3, q % 3] = d_own[pl.ds(6 + q, 16, stride=6), :]
    lane24 = iota((24, 128), 1)
    row24 = iota((24, 128), 0)
    sources = [(d_low, 3), (d_own, 0), (d_own, 3), (d_high, 0)]
    rows[...] = jnp.zeros_like(rows)
    for level in range(4):
        ref, first = sources[level]
        for i in range(3):
            g = level * 3 + i
            q = first + i
            rows[g * 24 : g * 24 + 18, 0:128] = ref[pl.ds(q, 18, stride=6), :]
            rim = jnp.broadcast_to(ref[108 + q : 109 + q, :], (24, 128))
            rows[g * 24 : g * 24 + 24, 128:256] = jnp.where(lane24 // 2 == row24, rim, 0.0)
    x = rows[...]
    hi = x.astype(bf16)
    lo = (x - hi.astype(f32)).astype(bf16)
    a, b = iota((128, 256), 0), iota((128, 256), 1)
    wide = one_hot(b // 2 == a)
    a, b = iota((128, 128), 0), iota((128, 128), 1)
    ends = one_hot(((a % 2 == 1) & (b < 2)) | ((a % 2 == 0) & (b >= 126)))
    spread[:, 0:256] = dot(hi[:, :128], wide) + dot(lo[:, :128], wide)
    spread[:, 256:384] = dot(hi[:, 128:], ends) + dot(lo[:, 128:], ends)
    r40, c24 = iota((40, 24), 0), iota((40, 24), 1)
    tall = one_hot(((r40 < 32) & (c24 == 1 + r40 // 2)) | ((r40 >= 32) & (r40 < 34) & (c24 == 17)) | ((r40 >= 38) & (c24 == 0)))
    for g in range(12):
        v = spread[g * 24 : (g + 1) * 24, :]
        hi = v.astype(bf16)
        lo = (v - hi.astype(f32)).astype(bf16)
        field[g] = dot(tall, hi) + dot(tall, lo)
    for step in range(3):
        src, dst = ((m0, m1), (m1, m2), (m2, None))[step]
        for fetch in (fetches[:2], fetches[2:], ())[step]:
            fetch.wait()
        if step == 0:
            for fetch in fetches[2:]:
                fetch.start()
        first, last = step + 1, 8 - step

        def plane(p, carry):
            m = [src[c, p] for c in range(3)]
            level = (p - 1) // 2
            h = []
            for c in range(3):
                if step == 0:
                    total = hh[c, p - 1]
                else:
                    total, up = exchange(src, wx, wy, wz, c, p, fz[c])
                    fz[c] = up
                    total = total * ss[p]
                h.append(total + field[level * 3 + c])
            t = [m[1] * h[2] - m[2] * h[1], m[2] * h[0] - m[0] * h[2], m[0] * h[1] - m[1] * h[0]]
            u = [m[1] * t[2] - m[2] * t[1], m[2] * t[0] - m[0] * t[2], m[0] * t[1] - m[1] * t[0]]
            raw = [m[c] - TIME_STEP * (t[c] + DAMPING * u[c]) for c in range(3)]
            scale = lax.rsqrt(jnp.maximum(raw[0] * raw[0] + raw[1] * raw[1] + raw[2] * raw[2], 1e-30))
            for c in range(3):
                if step < 2:
                    dst[c, p] = raw[c] * scale
                else:
                    state_out[c, p - 3] = (raw[c] * scale)[0:32, 0:256]
            return carry

        if step:
            for c in range(3):
                fz[c] = wz[first - 1] * (src[c, first] - src[c, first - 1])
        lax.fori_loop(first, last + 1, plane, 0)


def swap(value, axis, bit):
    return lax.ppermute(value, axis, [(i, i ^ bit) for i in range(8)])


def step(magnet, grains, stiffness_table, saturation_table, kernel_x, kernel_y, kernel_z, mixing):
    shape = jax.ShapeDtypeStruct
    up = [(i, i + 1) for i in range(7)]
    down = [(i + 1, i) for i in range(7)]
    big = (10, 40, 384)
    pay, edges, cells = call(
        coarse_kernel,
        [shape((128, 128), bf16), shape((2, 48, 256), f32), shape((512, 256), bf16)],
        [VM, VM, SM],
        [pltpu.VMEM((6, 32, 256), f32)],
        20_000_000,
        600_000,
        FULL - 520_000,
    )(magnet, grains, saturation_table)
    other = swap(pay, "gy", 7)
    strip, kx, wz = call(
        toeplitz_kernel,
        [shape((8, 128, 2176), bf16), shape((192, 128), f32), shape((64, 192), bf16)],
        [VM, VM, VM, SM],
        [pltpu.VMEM((8, 2176), f32)],
        20_000_000,
        5_000_000,
    )(kernel_x, kernel_y, kernel_z, mixing.transpose(1, 2, 0))
    (pay,) = call(pair_kernel, shape((4, 224, 128), bf16), [VM] * 2, (), 1000, 400_000, 8 << 20)(pay, other)
    groups = [[0, 1, 2, 3], [4, 5, 6, 7]]
    gathered = lax.all_to_all(pay, "gy", 0, 0, tiled=True, axis_index_groups=groups)
    pay, face_a, rim = call(
        faces_kernel,
        [shape((4, 912, 128), bf16), shape((144, 128), bf16), shape((512, 128), bf16)],
        [VM] * 3,
        [pltpu.VMEM((48, 128), f32)] * 2,
        1_000_000,
        1_000_000,
        8 << 20,
    )(gathered, other, edges)
    groups = [[0, 2, 4, 6], [1, 3, 5, 7]]
    gathered = lax.all_to_all(pay, "gx", 0, 0, tiled=True, axis_index_groups=groups)
    near = swap(face_a, "gx", 1)
    rc = swap(gathered, "gx", 1)
    own_low, own_high = call(
        rims_kernel,
        [shape((12, 40, 384), bf16)] * 2,
        [VM] * 4,
        [pltpu.VMEM((40, 384), f32), pltpu.VMEM((144, 128), f32), pltpu.VMEM((144, 128), f32)],
        1_000_000,
        2_000_000,
        12 << 20,
    )(cells, rim, near, rc)
    z_low = lax.ppermute(own_high, "gz", up)
    z_high = lax.ppermute(own_low, "gz", down)
    (parts,) = call(
        stages_kernel,
        shape((8, 120, 128), jnp.int16),
        [VM, VM, VM, HB, VM],
        [pltpu.VMEM((8, 144, 1024), bf16), pltpu.VMEM((8, 2, 192, 128), f32), pltpu.VMEM((8, 120, 128), f32)]
        + [pltpu.VMEM((8, 128, 2176), bf16), pltpu.SemaphoreType.DMA],
        2_000_000_000,
        10_000_000,
        FULL - (4 << 20),
    )(gathered, rc, kx, strip, wz)
    parts = lax.all_to_all(parts, "gz", 0, 0, tiled=True)
    fields = call(
        weights_kernel,
        [shape((3,) + big, f32), shape((3, 8, 40, 384), f32)] + [shape(big, f32)] * 4,
        [VM] * 5 + [SM] * 2,
        [pltpu.VMEM(big, f32)],
        20_000_000,
        5_000_000,
    )(magnet, own_low, own_high, z_low, z_high, stiffness_table, saturation_table)
    (d_own,) = call(sum_kernel, shape((120, 128), f32), [VM], (), 100_000, 300_000, 8 << 20)(parts)
    d_low = lax.ppermute(d_own, "gz", up)
    d_high = lax.ppermute(d_own, "gz", down)
    state, demag = call(
        substeps_kernel,
        [shape((3, 4, 32, 256), f32), shape((2, 3, 16, 128), f32)],
        [HB] * 6 + [VM] * 3,
        [pltpu.VMEM((3,) + big, f32), pltpu.VMEM((3, 8, 40, 384), f32)]
        + [pltpu.VMEM(big, f32)] * 4
        + [pltpu.VMEM((3,) + big, f32)] * 2
        + [pltpu.VMEM((3, 40, 384), f32), pltpu.VMEM((12, 40, 384), f32)]
        + [pltpu.VMEM((288, 256), f32), pltpu.VMEM((288, 384), f32), pltpu.SemaphoreType.DMA((6,))],
        50_000_000,
        5_000_000,
        FULL - 300_000,
    )(*fields, d_own, d_low, d_high)
    return (state, demag)


def solution(mesh):
    in_specs = (P(None, "gz", "gx", "gy"), P("gz", "gx", "gy"), P(), P(), P(), P(), P(), P())
    out_specs = (P(None, "gz", "gx", "gy"), P("gz", None, "gx", "gy"))
    return jax.shard_map(step, mesh=mesh, in_specs=in_specs, out_specs=out_specs, check_vma=False)
```

```python
import jax
import jax.numpy as jnp
from jax import lax
from jax.experimental import pallas as pl
from jax.experimental.pallas import tpu as pltpu
from jax.sharding import PartitionSpec as P


f32, bf16, i32 = jnp.float32, jnp.bfloat16, jnp.int32
VM = pl.BlockSpec(memory_space=pltpu.VMEM)
SM = pl.BlockSpec(memory_space=pltpu.SMEM)
HB = pl.BlockSpec(memory_space=pltpu.MemorySpace.HBM)
TIME_STEP = 0.02
DAMPING = 0.3
SCALE = 32000.0
FULL = 67_043_328


def iota(shape, dim):
    return lax.broadcasted_iota(i32, shape, dim)


def one_hot(condition):
    return jnp.where(condition, 1.0, 0.0).astype(bf16)


def dot(a, b, dims=((1,), (0,))):
    return lax.dot_general(a, b, (dims, ((), ())), preferred_element_type=f32)


class Planes:
    def __init__(self, ref, base, inner=0):
        self.ref, self.base, self.inner = ref, base, inner

    def key(self, k):
        k = k if isinstance(k, tuple) else (k,)
        if self.inner:
            return (self.base + k[0] * self.inner + k[1],) + k[2:]
        return (self.base + k[0],) + k[1:]

    def __getitem__(self, k):
        return self.ref[self.key(k)]

    def __setitem__(self, k, value):
        self.ref[self.key(k)] = value


def parts_of(ref):
    layout = ((0, 10), (30, 8), (54, 0), (64, 0), (74, 0), (84, 0))
    return [Planes(ref, base, inner) for base, inner in layout]


def lookup(ids, table):
    bits = [(ids & (1 << k)) != 0 for k in range(4)]
    level = [table[k] for k in range(16)]
    for bit in bits:
        level = [jnp.where(bit, level[2 * k + 1], level[2 * k]) for k in range(len(level) // 2)]
    return level[0]


def call(body, out_shape, in_specs, scratch=(), flops=0, nbytes=0, vmem=None, alias={}):
    outs = out_shape if isinstance(out_shape, list) else [out_shape]
    result = pl.pallas_call(
        body,
        out_shape=outs,
        in_specs=in_specs,
        out_specs=[VM] * len(outs),
        scratch_shapes=list(scratch),
        input_output_aliases=alias,
        compiler_params=pltpu.CompilerParams(vmem_limit_bytes=vmem),
        cost_estimate=pl.CostEstimate(flops=flops, bytes_accessed=nbytes, transcendentals=0),
    )
    return result


def coarse_kernel(mag, grains, sat, out, scr):
    for a in range(2):
        s0 = lookup(grains[2 * a], sat)
        s1 = lookup(grains[2 * a + 1], sat)
        for j in range(3):
            scr[j * 2 + a] = s0 * mag[j, 2 * a] + s1 * mag[j, 2 * a + 1]
    pick = one_hot(iota((256, 128), 0) == 2 * iota((256, 128), 1))
    rows = []
    for p in range(6):
        s = scr[p].reshape(16, 2, 256)
        s = s[:, 0, :] + s[:, 1, :]
        s = s + pltpu.roll(s, 255, 1)
        rows.append((s * 0.125).astype(bf16))
    coarse = dot(jnp.concatenate(rows, axis=0), pick).astype(bf16)
    cells = [mag[j].reshape(128, 256).astype(bf16) for j in range(3)]
    cells.append(grains[...].reshape(128, 256).astype(f32).astype(bf16))
    cells = jnp.concatenate(cells, axis=0)
    k, lane = iota((8, 256), 0), iota((8, 256), 1)
    edge = one_hot(((k < 3) & (lane == k)) | ((k >= 4) & (k < 7) & (lane == 249 + k)))
    faces = dot(edge, cells, ((1,), (1,)))
    faces = jnp.concatenate([faces[:, 128 * q : 128 * (q + 1)] for q in range(4)], axis=0).astype(bf16)
    out[0:96, :] = coarse
    out[96:128, :] = faces


def block_kernel(mag, grains, own, edges, cells, out):
    for n in range(4):
        out[n, 0:128, :] = own[...]
        out[n, 128:256, :] = own[...]
    for c in range(4):
        for z in range(4):
            at = c * 4 + z
            plane = mag[c, z] if c < 3 else grains[z].astype(f32)
            edges[0, 3 * at : 3 * at + 3, :] = plane[0:3]
            edges[1, 3 * at : 3 * at + 3, :] = plane[29:32]
            cells[32 * at : 32 * at + 32, :] = plane.astype(bf16)


def pair_kernel(block, other, out):
    for n in range(4):
        out[n, 128:256, :] = other[...]


def toeplitz_kernel(kernel_x, kernel_y, kernel_z, mixing, strip, kx_out, wz_out, kyp):
    gx, gz = lax.axis_index("gx"), lax.axis_index("gz")
    kyp[...] = jnp.zeros_like(kyp)
    kyp[:, 0:2048] = kernel_y[...].astype(f32)
    mirror = one_hot(iota((256, 256), 0) + iota((256, 256), 1) == 255)
    kxr = dot(kernel_x[...], mirror)
    row, col = iota((64, 32), 0), iota((64, 32), 1)
    level = 2 * (row // 8) + jnp.where(row % 8 >= 3, 1, 0) + 16 - 2 * gz
    row, col8 = iota((8, 64), 0), iota((8, 64), 1)
    total = jnp.zeros((64, 64), f32)
    for zl in range(2):
        per_rank = dot(one_hot(col == level - zl), kernel_z[...], ((1,), (1,)))
        total = total + dot(per_rank.astype(bf16), one_hot((col8 // 8 == row) & (col8 % 8 < 6) & (col8 % 2 == zl)))
    row, col = iota((64, 64), 0), iota((64, 64), 1)
    i_of = jnp.where(row % 8 < 6, row % 8 % 3, 3)
    rj_of = col // 2
    mix = jnp.zeros((64, 64), f32)
    for i in range(3):
        line = jnp.zeros((1, 64), f32)
        for r in range(8):
            for j in range(3):
                line = jnp.where(rj_of[0:1] == r * 4 + j, mixing[i, j, r], line)
        mix = jnp.where(i_of == i, line, mix)
    w = mix * total
    hi = w.astype(bf16)
    rest = w - hi.astype(f32)
    mid = rest.astype(bf16)
    wz_out[:, 0:64] = hi
    wz_out[:, 64:128] = mid
    wz_out[:, 128:192] = (rest - mid.astype(f32)).astype(bf16)

    def one(r, carry):
        row = jnp.broadcast_to(kyp[pl.ds(r, 1), :], (128, 2176))
        strip[pl.ds(r, 1)] = pltpu.roll(row, 0, 1, stride=1, stride_axis=0).astype(bf16)[None]
        return carry

    lax.fori_loop(0, 8, one, 0)
    lane = iota((24, 256), 1)
    for r in range(8):
        row = pltpu.roll(jnp.broadcast_to(kxr[r : r + 1, :], (24, 256)), 0, 1, stride=1, stride_axis=0)
        total = jnp.zeros((24, 256), f32)
        for l in range(8):
            block = 2 * (l % 4) + ((gx & 1) if l < 4 else 1 - (gx & 1))
            shift = (16 * l + 16 * (gx - block) + 128 + 512) & 255
            total = jnp.where(lane // 16 == l, pltpu.roll(row, shift, 1), total)
        kx_out[r * 24 : (r + 1) * 24, :] = total[:, :128]


def faces_kernel(gathered, edges, pay, face_a, rim, low, high):
    gx, gy = lax.axis_index("gx"), lax.axis_index("gy")
    y = gy & 3

    def faces(n, row):
        rows = gathered[n, row : row + 32, :].astype(f32)
        return jnp.concatenate([rows[8 * q : 8 * (q + 1)] for q in range(4)], axis=1)

    right = jnp.where(gy == 3, faces(0, 224), faces(jnp.minimum(y + 1, 3), 96))
    left = jnp.where(gy == 4, faces(3, 224), faces(jnp.maximum(y - 1, 0), 96))
    sel = jnp.where(iota((8, 512), 0) < 4, right, left)
    k, lane = iota((8, 128), 0), iota((8, 128), 1)
    put = one_hot(((k < 3) & (lane == k)) | ((k >= 4) & (k < 7) & (lane == 121 + k)))
    unpacked = dot(sel.astype(bf16), put, ((0,), (0,)))
    rim[...] = unpacked.astype(bf16)
    for n in range(16):
        low[3 * n : 3 * n + 3] = unpacked[32 * n : 32 * n + 3]
        high[3 * n : 3 * n + 3] = unpacked[32 * n + 29 : 32 * n + 32]
    odd = (gx & 1) == 1
    to_b = [jnp.where(odd, edges[1], edges[0]).astype(bf16), jnp.where(odd, high[...], low[...]).astype(bf16)]
    to_a = [jnp.where(odd, edges[0], edges[1]).astype(bf16), jnp.where(odd, low[...], high[...]).astype(bf16)]
    face_a[0:48, :] = to_a[0][:, :128]
    face_a[48:96, :] = to_a[0][:, 128:]
    face_a[96:144, :] = to_a[1]
    for n in range(4):
        for k in range(4):
            pay[n, k * 96 : (k + 1) * 96, :] = gathered[k, 0:96, :]
            pay[n, (k + 4) * 96 : (k + 5) * 96, :] = gathered[k, 128:224, :]
        pay[n, 768:816, :] = to_b[0][:, :128]
        pay[n, 816:864, :] = to_b[0][:, 128:]
        pay[n, 864:912, :] = to_b[1]


def rims_kernel(cells, rim, near, rc, low_out, high_out, scr, fa, fb):
    gx = lax.axis_index("gx")
    even = (gx & 1) == 0
    chip = gx // 2
    a = near[...].astype(f32)
    b = rc[jnp.where(even, jnp.maximum(chip - 1, 0), jnp.minimum(chip + 1, 3)), 768:912, :].astype(f32)
    fa[...] = jnp.where(even, a, b)
    fb[...] = jnp.where(even, b, a)
    for z in range(4):
        for c in range(4):
            plane = (c * 4 + z) * 32
            scr[0:32, 0:256] = cells[plane : plane + 32, :].astype(f32)
            scr[0:32, 256:384] = rim[plane : plane + 32, :].astype(f32)
            scr[32:40, :] = jnp.zeros((8, 384), f32)
            for q in range(3):
                at = q * 48 + (c * 4 + z) * 3
                scr[32:35, q * 128 : (q + 1) * 128] = fa[at : at + 3, :]
                scr[37:40, q * 128 : (q + 1) * 128] = fb[at : at + 3, :]
            whole = scr[...].astype(bf16)
            if z < 3:
                low_out[z * 4 + c] = whole
            if z > 0:
                high_out[(z - 1) * 4 + c] = whole


def stages_kernel(own, rc, kx, strip_hbm, wz, packed, ax, ay, out, strip, sem):
    gy = lax.axis_index("gy")
    kxm = kx[...].astype(bf16)
    fetch = pltpu.make_async_copy(strip_hbm, strip, sem)
    fetch.start()

    def x_stage(kp, carry):
        for pair in range(3):
            res = []
            for jz in range(2):
                halves = []
                for half in range(2):
                    at = pl.multiple_of(((2 * kp + half) * 6 + 2 * pair + jz) * 16, 16)
                    parts = [ref[n, pl.ds(at, 16), :] for ref in (own, rc) for n in range(4)]
                    halves.append(jnp.concatenate(parts, axis=0))
                res.append(dot(kxm, jnp.concatenate(halves, axis=1)))
            for r in range(8):
                both = jnp.concatenate([res[0][r * 24 : (r + 1) * 24], res[1][r * 24 : (r + 1) * 24]], axis=0)
                ax[r, pair * 48 : pair * 48 + 48, pl.ds(pl.multiple_of(kp * 256, 256), 256)] = both.astype(bf16)
        return carry

    lax.fori_loop(0, 4, x_stage, 0)
    for r in range(8):
        for half in range(2):
            ay[r, half, 144:192, :] = jnp.zeros((48, 128), f32)
    fetch.wait()

    first_half = iota((128, 128), 1) < 64

    def y_stage(r, carry):
        acc = jnp.zeros((144, 256), f32)
        for kp in range(4):
            tiles = []
            for k in (2 * kp, 2 * kp + 1):
                block = (gy & 4) + k if k < 4 else k - (gy & 4)
                at = pl.multiple_of(128 * (8 + gy - block), 128)
                after, before = strip[r, :, pl.ds(at + 128, 128)], strip[r, :, pl.ds(at - 128, 128)]
                ends = jnp.where(first_half, after, before)
                tiles.append(jnp.concatenate([strip[r, :, pl.ds(at, 128)], ends], axis=1))
            acc = acc + dot(ax[r, :, kp * 256 : (kp + 1) * 256], jnp.concatenate(tiles, axis=0))
        for half in range(2):
            ay[r, half, 0:144, :] = acc[:, 128 * half : 128 * half + 128]
        return carry

    lax.fori_loop(0, 8, y_stage, 0, unroll=2)
    w = wz[...]
    lane = iota((64, 128), 1)
    rims = jnp.zeros((64, 128), f32)
    for a in range(18):
        halves = [
            jnp.concatenate([ay[r, half, pl.ds(a, 8, stride=24), :] for r in range(8)], axis=0).astype(bf16)
            for half in range(2)
        ]
        col = jnp.concatenate(halves, axis=1)
        o = dot(w, jnp.concatenate([col, col, col], axis=0))
        rims = jnp.where(lane // 2 == a, pltpu.roll(o[:, 128:], 2 * a + 1, 1), rims)
        for d in range(8):
            out[d, a * 6 : a * 6 + 6, :] = o[d * 8 : d * 8 + 6, :128]
    for d in range(8):
        out[d, 108:114, :] = rims[d * 8 : d * 8 + 6]
        values = out[d, 0:114, :]
        peak = jnp.max(jnp.abs(values), axis=0, keepdims=True)
        code = jnp.ceil(16.0 * jnp.log2(jnp.maximum(peak, 1e-30)))
        scaled = values * (SCALE * jnp.exp2(code * -0.0625))
        scaled = jnp.concatenate([scaled, jnp.broadcast_to(code, (6, 128))], axis=0)
        packed[d] = jnp.round(scaled).astype(i32).astype(jnp.int16)


def sum_kernel(parts, out):
    total = jnp.zeros((114, 128), f32)
    for d in range(8):
        values = parts[d].astype(i32).astype(f32)
        total = total + values[0:114] * (jnp.exp2(values[114:115] * 0.0625) * (1.0 / SCALE))
    out[0:114] = total
    out[114:120] = jnp.zeros((6, 128), f32)


def weights_kernel(mag, own_low, own_high, z_low, z_high, stiff, sat, fields, aa):
    m0, hh, wx, wy, wz, ss = parts_of(fields)
    gx, gy, gz = (lax.axis_index(n) for n in ("gx", "gy", "gz"))
    row, col = iota((40, 384), 0), iota((40, 384), 1)
    inside = ((row < 32) | ((row < 36) & (gx < 7)) | ((row >= 36) & (gx > 0))) & (
        (col < 256) | ((col < 320) & (gy < 7)) | ((col >= 320) & (gy > 0))
    )
    for p in range(10):
        z = p - 3
        if z < 0:
            whole = [z_low[p * 4 + c].astype(f32) for c in range(4)]
            ok = gz > 0
        elif z > 3:
            whole = [z_high[(z - 4) * 4 + c].astype(f32) for c in range(4)]
            ok = gz < 7
        else:
            ref, at = (own_low, z * 4) if z < 3 else (own_high, 8)
            whole = [ref[at + c].astype(f32) for c in range(4)]
            ok = gz >= 0
        for c in range(3):
            m0[c, p] = whole[c]
            if 0 <= z < 4:
                m0[c, p, 0:32, 0:256] = mag[c, z]
        ids = whole[3].astype(i32)
        aa[p] = jnp.where(inside & ok, lookup(ids, stiff), 0.0)
        ss[p] = 2.0 / lookup(ids, sat)

    def weight(u, v):
        den = u + v
        return 2.0 * u * v / jnp.where(den > 0.0, den, 1.0)

    for p in range(10):
        here = aa[p]
        if 1 <= p <= 8:
            wx[p] = weight(here, pltpu.roll(here, 39, 0))
            wy[p] = weight(here, pltpu.roll(here, 383, 1))
        if p < 9:
            wz[p] = weight(here, aa[p + 1])

    fz = [wz[0] * (m0[c, 1] - m0[c, 0]) for c in range(3)]
    for p in range(1, 9):
        for c in range(3):
            total, fz[c] = exchange(m0, wx, wy, wz, c, p, fz[c])
            hh[c, p - 1] = total * ss[p]


def exchange(src, wx, wy, wz, c, p, below):
    m = src[c, p]
    flux = wx[p] * (pltpu.roll(m, 39, 0) - m)
    total = flux - pltpu.roll(flux, 1, 0)
    flux = wy[p] * (pltpu.roll(m, 383, 1) - m)
    total = total + (flux - pltpu.roll(flux, 1, 1))
    up = wz[p] * (src[c, p + 1] - m)
    return total + (up - below), up


def substeps_kernel(
    fields_hbm, d_own, d_low, d_high, state_out, demag_out, fields, m1, m2, fz, field, rows, spread, sems
):
    m0, hh, wx, wy, wz, ss = parts_of(fields)
    cuts = (pl.ds(0, 54), pl.ds(54, 40))
    fetches = [pltpu.make_async_copy(fields_hbm.at[c], fields.at[c], sems.at[n]) for n, c in enumerate(cuts)]
    for fetch in fetches:
        fetch.start()
    for q in range(6):
        demag_out[q // 3, q % 3] = d_own[pl.ds(6 + q, 16, stride=6), :]
    lane24 = iota((24, 128), 1)
    row24 = iota((24, 128), 0)
    sources = [(d_low, 3), (d_own, 0), (d_own, 3), (d_high, 0)]
    rows[...] = jnp.zeros_like(rows)
    for level in range(4):
        ref, first = sources[level]
        for i in range(3):
            g = level * 3 + i
            q = first + i
            rows[g * 24 : g * 24 + 18, 0:128] = ref[pl.ds(q, 18, stride=6), :]
            rim = jnp.broadcast_to(ref[108 + q : 109 + q, :], (24, 128))
            rows[g * 24 : g * 24 + 24, 128:256] = jnp.where(lane24 // 2 == row24, rim, 0.0)
    x = rows[...]
    hi = x.astype(bf16)
    lo = (x - hi.astype(f32)).astype(bf16)
    a, b = iota((128, 256), 0), iota((128, 256), 1)
    wide = one_hot(b // 2 == a)
    a, b = iota((128, 128), 0), iota((128, 128), 1)
    ends = one_hot(((a % 2 == 1) & (b < 2)) | ((a % 2 == 0) & (b >= 126)))
    spread[:, 0:256] = dot(hi[:, :128], wide) + dot(lo[:, :128], wide)
    spread[:, 256:384] = dot(hi[:, 128:], ends) + dot(lo[:, 128:], ends)
    r40, c24 = iota((40, 24), 0), iota((40, 24), 1)
    tall = one_hot(((r40 < 32) & (c24 == 1 + r40 // 2)) | ((r40 >= 32) & (r40 < 34) & (c24 == 17)) | ((r40 >= 38) & (c24 == 0)))
    for g in range(12):
        v = spread[g * 24 : (g + 1) * 24, :]
        hi = v.astype(bf16)
        lo = (v - hi.astype(f32)).astype(bf16)
        field[g] = dot(tall, hi) + dot(tall, lo)
    for step in range(3):
        src, dst = ((m0, m1), (m1, m2), (m2, None))[step]
        if step < 2:
            fetches[step].wait()
        first, last = step + 1, 8 - step

        def plane(p, carry):
            m = [src[c, p] for c in range(3)]
            level = (p - 1) // 2
            h = []
            for c in range(3):
                if step == 0:
                    total = hh[c, p - 1]
                else:
                    total, up = exchange(src, wx, wy, wz, c, p, fz[c])
                    fz[c] = up
                    total = total * ss[p]
                h.append(total + field[level * 3 + c])
            t = [m[1] * h[2] - m[2] * h[1], m[2] * h[0] - m[0] * h[2], m[0] * h[1] - m[1] * h[0]]
            u = [m[1] * t[2] - m[2] * t[1], m[2] * t[0] - m[0] * t[2], m[0] * t[1] - m[1] * t[0]]
            raw = [m[c] - TIME_STEP * (t[c] + DAMPING * u[c]) for c in range(3)]
            scale = lax.rsqrt(jnp.maximum(raw[0] * raw[0] + raw[1] * raw[1] + raw[2] * raw[2], 1e-30))
            for c in range(3):
                if step < 2:
                    dst[c, p] = raw[c] * scale
                else:
                    state_out[c, p - 3] = (raw[c] * scale)[0:32, 0:256]
            return carry

        if step:
            for c in range(3):
                fz[c] = wz[first - 1] * (src[c, first] - src[c, first - 1])
        lax.fori_loop(first, last + 1, plane, 0)


def swap(value, axis, bit):
    return lax.ppermute(value, axis, [(i, i ^ bit) for i in range(8)])


def step(magnet, grains, stiffness_table, saturation_table, kernel_x, kernel_y, kernel_z, mixing):
    shape = jax.ShapeDtypeStruct
    up = [(i, i + 1) for i in range(7)]
    down = [(i + 1, i) for i in range(7)]
    big = (10, 40, 384)
    (pay,) = call(
        coarse_kernel,
        shape((128, 128), bf16),
        [VM, VM, SM],
        [pltpu.VMEM((6, 32, 256), f32)],
        20_000_000,
        600_000,
    )(magnet, grains, saturation_table)
    other = swap(pay, "gy", 4)
    edges, cells, block = call(
        block_kernel,
        [shape((2, 48, 256), f32), shape((512, 256), bf16), shape((4, 256, 128), bf16)],
        [VM] * 3,
        (),
        1_000_000,
        1_500_000,
        16 << 20,
    )(magnet, grains, pay)
    strip, kx, wz = call(
        toeplitz_kernel,
        [shape((8, 128, 2176), bf16), shape((192, 128), f32), shape((64, 192), bf16)],
        [VM, VM, VM, SM],
        [pltpu.VMEM((8, 2176), f32)],
        20_000_000,
        5_000_000,
        FULL - 14_000_000,
    )(kernel_x, kernel_y, kernel_z, mixing.transpose(1, 2, 0))
    (pay,) = call(pair_kernel, shape((4, 256, 128), bf16), [VM] * 2, (), 1000, 400_000, 8 << 20, {0: 0})(block, other)
    groups = [[0, 1, 2, 3], [4, 5, 6, 7]]
    gathered = lax.all_to_all(pay, "gy", 0, 0, tiled=True, axis_index_groups=groups)
    pay, face_a, rim = call(
        faces_kernel,
        [shape((4, 912, 128), bf16), shape((144, 128), bf16), shape((512, 128), bf16)],
        [VM] * 2,
        [pltpu.VMEM((48, 128), f32)] * 2,
        1_000_000,
        1_000_000,
        8 << 20,
    )(gathered, edges)
    groups = [[0, 2, 4, 6], [1, 3, 5, 7]]
    gathered = lax.all_to_all(pay, "gx", 0, 0, tiled=True, axis_index_groups=groups)
    near = swap(face_a, "gx", 1)
    rc = swap(gathered, "gx", 1)
    own_low, own_high = call(
        rims_kernel,
        [shape((12, 40, 384), bf16)] * 2,
        [VM] * 4,
        [pltpu.VMEM((40, 384), f32), pltpu.VMEM((144, 128), f32), pltpu.VMEM((144, 128), f32)],
        1_000_000,
        2_000_000,
        12 << 20,
    )(cells, rim, near, rc)
    z_low = lax.ppermute(own_high, "gz", up)
    z_high = lax.ppermute(own_low, "gz", down)
    (parts,) = call(
        stages_kernel,
        shape((8, 120, 128), jnp.int16),
        [VM, VM, VM, HB, VM],
        [pltpu.VMEM((8, 144, 1024), bf16), pltpu.VMEM((8, 2, 192, 128), f32), pltpu.VMEM((8, 120, 128), f32)]
        + [pltpu.VMEM((8, 128, 2176), bf16), pltpu.SemaphoreType.DMA],
        2_000_000_000,
        10_000_000,
        FULL - (16 << 20),
    )(gathered, rc, kx, strip, wz)
    parts = lax.all_to_all(parts, "gz", 0, 0, tiled=True)
    (fields,) = call(
        weights_kernel,
        shape((94, 40, 384), f32),
        [VM] * 5 + [SM] * 2,
        [pltpu.VMEM(big, f32)],
        20_000_000,
        5_000_000,
    )(magnet, own_low, own_high, z_low, z_high, stiffness_table, saturation_table)
    (d_own,) = call(sum_kernel, shape((120, 128), f32), [VM], (), 100_000, 300_000, 8 << 20)(parts)
    d_low = lax.ppermute(d_own, "gz", up)
    d_high = lax.ppermute(d_own, "gz", down)
    state, demag = call(
        substeps_kernel,
        [shape((3, 4, 32, 256), f32), shape((2, 3, 16, 128), f32)],
        [HB] + [VM] * 3,
        [pltpu.VMEM((94, 40, 384), f32)]
        + [pltpu.VMEM((3,) + big, f32)] * 2
        + [pltpu.VMEM((3, 40, 384), f32), pltpu.VMEM((12, 40, 384), f32)]
        + [pltpu.VMEM((288, 256), f32), pltpu.VMEM((288, 384), f32), pltpu.SemaphoreType.DMA((2,))],
        50_000_000,
        5_000_000,
        FULL - 14_000_000,
    )(fields, d_own, d_low, d_high)
    return (state, demag)


def solution(mesh):
    in_specs = (P(None, "gz", "gx", "gy"), P("gz", "gx", "gy"), P(), P(), P(), P(), P(), P())
    out_specs = (P(None, "gz", "gx", "gy"), P("gz", None, "gx", "gy"))
    return jax.shard_map(step, mesh=mesh, in_specs=in_specs, out_specs=out_specs, check_vma=False)
```

```python
import jax
import jax.numpy as jnp
from jax import lax
from jax.experimental import pallas as pl
from jax.experimental.pallas import tpu as pltpu
from jax.sharding import PartitionSpec as P


f32, bf16, i32 = jnp.float32, jnp.bfloat16, jnp.int32
VM = pl.BlockSpec(memory_space=pltpu.VMEM)
SM = pl.BlockSpec(memory_space=pltpu.SMEM)
HB = pl.BlockSpec(memory_space=pltpu.MemorySpace.HBM)
TIME_STEP = 0.02
DAMPING = 0.3
SCALE = 32000.0
FULL = 67_043_328


def iota(shape, dim):
    return lax.broadcasted_iota(i32, shape, dim)


def one_hot(condition):
    return jnp.where(condition, 1.0, 0.0).astype(bf16)


def dot(a, b, dims=((1,), (0,))):
    return lax.dot_general(a, b, (dims, ((), ())), preferred_element_type=f32)


class Planes:
    def __init__(self, ref, base, inner=0):
        self.ref, self.base, self.inner = ref, base, inner

    def key(self, k):
        k = k if isinstance(k, tuple) else (k,)
        if self.inner:
            return (self.base + k[0] * self.inner + k[1],) + k[2:]
        return (self.base + k[0],) + k[1:]

    def __getitem__(self, k):
        return self.ref[self.key(k)]

    def __setitem__(self, k, value):
        self.ref[self.key(k)] = value


def parts_of(ref):
    layout = ((0, 10), (30, 8), (54, 0), (64, 0), (74, 0), (84, 0))
    return [Planes(ref, base, inner) for base, inner in layout]


def lookup(ids, table):
    bits = [(ids & (1 << k)) != 0 for k in range(4)]
    level = [table[k] for k in range(16)]
    for bit in bits:
        level = [jnp.where(bit, level[2 * k + 1], level[2 * k]) for k in range(len(level) // 2)]
    return level[0]


def call(body, out_shape, in_specs, scratch=(), flops=0, nbytes=0, vmem=None, out_specs=None, alias={}):
    outs = out_shape if isinstance(out_shape, list) else [out_shape]
    result = pl.pallas_call(
        body,
        out_shape=outs,
        in_specs=in_specs,
        out_specs=out_specs or [VM] * len(outs),
        scratch_shapes=list(scratch),
        input_output_aliases=alias,
        compiler_params=pltpu.CompilerParams(vmem_limit_bytes=vmem),
        cost_estimate=pl.CostEstimate(flops=flops, bytes_accessed=nbytes, transcendentals=0),
    )
    return result


def coarse_kernel(mag, grains, sat, out, scr):
    for a in range(2):
        s0 = lookup(grains[2 * a], sat)
        s1 = lookup(grains[2 * a + 1], sat)
        for j in range(3):
            scr[j * 2 + a] = s0 * mag[j, 2 * a] + s1 * mag[j, 2 * a + 1]
    pick = one_hot(iota((256, 128), 0) == 2 * iota((256, 128), 1))
    rows = []
    for p in range(6):
        s = scr[p].reshape(16, 2, 256)
        s = s[:, 0, :] + s[:, 1, :]
        s = s + pltpu.roll(s, 255, 1)
        rows.append((s * 0.125).astype(bf16))
    coarse = dot(jnp.concatenate(rows, axis=0), pick).astype(bf16)
    cells = [mag[j].reshape(128, 256).astype(bf16) for j in range(3)]
    cells.append(grains[...].reshape(128, 256).astype(f32).astype(bf16))
    cells = jnp.concatenate(cells, axis=0)
    k, lane = iota((8, 256), 0), iota((8, 256), 1)
    edge = one_hot(((k < 3) & (lane == k)) | ((k >= 4) & (k < 7) & (lane == 249 + k)))
    faces = dot(edge, cells, ((1,), (1,)))
    faces = jnp.concatenate([faces[:, 128 * q : 128 * (q + 1)] for q in range(4)], axis=0).astype(bf16)
    out[0:96, :] = coarse
    out[96:128, :] = faces


def block_kernel(mag, grains, own, edges, cells, out):
    for n in range(4):
        out[n, 0:128, :] = own[...]
        out[n, 128:256, :] = own[...]
    for c in range(4):
        for z in range(4):
            at = c * 4 + z
            plane = mag[c, z] if c < 3 else grains[z].astype(f32)
            edges[0, 3 * at : 3 * at + 3, :] = plane[0:3]
            edges[1, 3 * at : 3 * at + 3, :] = plane[29:32]
            cells[32 * at : 32 * at + 32, :] = plane.astype(bf16)


def pair_kernel(block, other, out):
    for n in range(4):
        out[n, 128:256, :] = other[...]


def toeplitz_kernel(kernel_x, kernel_y, kernel_z, mixing, strip_hbm, kx_out, wz_out, kyp, strip, sems):
    gx, gz = lax.axis_index("gx"), lax.axis_index("gz")
    kyp[...] = jnp.zeros_like(kyp)
    kyp[:, 0:2048] = kernel_y[...].astype(f32)

    def send(r):
        return pltpu.make_async_copy(strip.at[r], strip_hbm.at[r], sems.at[r])

    def one(r, carry):
        row = jnp.broadcast_to(kyp[pl.ds(r, 1), :], (128, 2176))
        strip[pl.ds(r, 1)] = pltpu.roll(row, 0, 1, stride=1, stride_axis=0).astype(bf16)[None]
        send(r).start()
        return carry

    lax.fori_loop(0, 8, one, 0)
    mirror = one_hot(iota((256, 256), 0) + iota((256, 256), 1) == 255)
    kxr = dot(kernel_x[...], mirror)
    row, col = iota((64, 32), 0), iota((64, 32), 1)
    level = 2 * (row // 8) + jnp.where(row % 8 >= 3, 1, 0) + 16 - 2 * gz
    row, col8 = iota((8, 64), 0), iota((8, 64), 1)
    total = jnp.zeros((64, 64), f32)
    for zl in range(2):
        per_rank = dot(one_hot(col == level - zl), kernel_z[...], ((1,), (1,)))
        total = total + dot(per_rank.astype(bf16), one_hot((col8 // 8 == row) & (col8 % 8 < 6) & (col8 % 2 == zl)))
    row, col = iota((64, 64), 0), iota((64, 64), 1)
    i_of = jnp.where(row % 8 < 6, row % 8 % 3, 3)
    rj_of = col // 2
    mix = jnp.zeros((64, 64), f32)
    for i in range(3):
        line = jnp.zeros((1, 64), f32)
        for r in range(8):
            for j in range(3):
                line = jnp.where(rj_of[0:1] == r * 4 + j, mixing[i, j, r], line)
        mix = jnp.where(i_of == i, line, mix)
    w = mix * total
    hi = w.astype(bf16)
    rest = w - hi.astype(f32)
    mid = rest.astype(bf16)
    wz_out[:, 0:64] = hi
    wz_out[:, 64:128] = mid
    wz_out[:, 128:192] = (rest - mid.astype(f32)).astype(bf16)

    lane = iota((24, 256), 1)
    for r in range(8):
        row = pltpu.roll(jnp.broadcast_to(kxr[r : r + 1, :], (24, 256)), 0, 1, stride=1, stride_axis=0)
        total = jnp.zeros((24, 256), f32)
        for l in range(8):
            block = 2 * (l % 4) + ((gx & 1) if l < 4 else 1 - (gx & 1))
            shift = (16 * l + 16 * (gx - block) + 128 + 512) & 255
            total = jnp.where(lane // 16 == l, pltpu.roll(row, shift, 1), total)
        kx_out[r * 24 : (r + 1) * 24, :] = total[:, :128]
    for r in range(8):
        send(r).wait()


def faces_kernel(gathered, edges, pay, face_a, rim, low, high):
    gx, gy = lax.axis_index("gx"), lax.axis_index("gy")
    y = gy & 3

    def faces(n, row):
        rows = gathered[n, row : row + 32, :].astype(f32)
        return jnp.concatenate([rows[8 * q : 8 * (q + 1)] for q in range(4)], axis=1)

    right = jnp.where(gy == 3, faces(0, 224), faces(jnp.minimum(y + 1, 3), 96))
    left = jnp.where(gy == 4, faces(3, 224), faces(jnp.maximum(y - 1, 0), 96))
    sel = jnp.where(iota((8, 512), 0) < 4, right, left)
    k, lane = iota((8, 128), 0), iota((8, 128), 1)
    put = one_hot(((k < 3) & (lane == k)) | ((k >= 4) & (k < 7) & (lane == 121 + k)))
    unpacked = dot(sel.astype(bf16), put, ((0,), (0,)))
    rim[...] = unpacked.astype(bf16)
    for n in range(16):
        low[3 * n : 3 * n + 3] = unpacked[32 * n : 32 * n + 3]
        high[3 * n : 3 * n + 3] = unpacked[32 * n + 29 : 32 * n + 32]
    odd = (gx & 1) == 1
    to_b = [jnp.where(odd, edges[1], edges[0]).astype(bf16), jnp.where(odd, high[...], low[...]).astype(bf16)]
    to_a = [jnp.where(odd, edges[0], edges[1]).astype(bf16), jnp.where(odd, low[...], high[...]).astype(bf16)]
    face_a[0:48, :] = to_a[0][:, :128]
    face_a[48:96, :] = to_a[0][:, 128:]
    face_a[96:144, :] = to_a[1]
    for n in range(4):
        for k in range(4):
            pay[n, k * 96 : (k + 1) * 96, :] = gathered[k, 0:96, :]
            pay[n, (k + 4) * 96 : (k + 5) * 96, :] = gathered[k, 128:224, :]
        pay[n, 768:816, :] = to_b[0][:, :128]
        pay[n, 816:864, :] = to_b[0][:, 128:]
        pay[n, 864:912, :] = to_b[1]


def rims_kernel(cells, rim, near, rc, low_out, high_out, scr, fa, fb):
    gx = lax.axis_index("gx")
    even = (gx & 1) == 0
    chip = gx // 2
    a = near[...].astype(f32)
    b = rc[jnp.where(even, jnp.maximum(chip - 1, 0), jnp.minimum(chip + 1, 3)), 768:912, :].astype(f32)
    fa[...] = jnp.where(even, a, b)
    fb[...] = jnp.where(even, b, a)
    scr[2, 640:672, :] = jnp.zeros((32, 128), f32)
    for z in range(4):
        for c in range(4):
            plane, top, at = (c * 4 + z) * 32, (z * 4 + c) * 40, (c * 4 + z) * 3
            for q in range(3):
                if q < 2:
                    scr[q, top : top + 32] = cells[plane : plane + 32, q * 128 : (q + 1) * 128].astype(f32)
                else:
                    scr[q, top : top + 32] = rim[plane : plane + 32, :].astype(f32)
                scr[q, top + 32 : top + 40] = jnp.zeros((8, 128), f32)
                scr[q, top + 32 : top + 35] = fa[q * 48 + at : q * 48 + at + 3, :]
                scr[q, top + 37 : top + 40] = fb[q * 48 + at : q * 48 + at + 3, :]
    for out, first in ((low_out, 0), (high_out, 160)):
        for q in range(2):
            out[q * 480 : (q + 1) * 480, :] = scr[q, first : first + 480].astype(bf16)
        ends = dot(rim_lanes(), scr[2, first : first + 512].astype(bf16), ((1,), (1,)))
        ends = jnp.concatenate([ends[:, 128 * n : 128 * (n + 1)] for n in range(4)], axis=0)
        out[960:992, :] = ends.astype(bf16)


def rim_lanes():
    k, lane = iota((8, 128), 0), iota((8, 128), 1)
    return one_hot(((k < 3) & (lane == k)) | ((k >= 4) & (k < 7) & (lane == 121 + k)))


def unpack_rims(ref):
    ends = ref[960:992, :].astype(f32)
    ends = jnp.concatenate([ends[8 * n : 8 * (n + 1)] for n in range(4)], axis=1)
    ends = dot(ends.astype(bf16), rim_lanes(), ((0,), (0,)))
    return [ref[0:480, :].astype(f32), ref[480:960, :].astype(f32), ends]


def stages_kernel(own, rc, kx, strip_hbm, wz, packed, ax, ay, out, strip, sem):
    gy = lax.axis_index("gy")
    kxm = kx[...].astype(bf16)
    fetch = pltpu.make_async_copy(strip_hbm, strip, sem)
    fetch.start()

    def x_stage(kp, carry):
        for pair in range(3):
            res = []
            for jz in range(2):
                halves = []
                for half in range(2):
                    at = pl.multiple_of(((2 * kp + half) * 6 + 2 * pair + jz) * 16, 16)
                    parts = [ref[n, pl.ds(at, 16), :] for ref in (own, rc) for n in range(4)]
                    halves.append(jnp.concatenate(parts, axis=0))
                res.append(dot(kxm, jnp.concatenate(halves, axis=1)))
            for r in range(8):
                both = jnp.concatenate([res[0][r * 24 : (r + 1) * 24], res[1][r * 24 : (r + 1) * 24]], axis=0)
                ax[r, pair * 48 : pair * 48 + 48, pl.ds(pl.multiple_of(kp * 256, 256), 256)] = both.astype(bf16)
        return carry

    lax.fori_loop(0, 4, x_stage, 0)
    for r in range(8):
        for half in range(2):
            ay[r, half, 144:192, :] = jnp.zeros((48, 128), f32)
    fetch.wait()

    first_half = iota((128, 128), 1) < 64

    def y_stage(r, carry):
        acc = jnp.zeros((144, 256), f32)
        for kp in range(4):
            tiles = []
            for k in (2 * kp, 2 * kp + 1):
                block = (gy & 4) + k if k < 4 else k - (gy & 4)
                at = pl.multiple_of(128 * (8 + gy - block), 128)
                after, before = strip[r, :, pl.ds(at + 128, 128)], strip[r, :, pl.ds(at - 128, 128)]
                ends = jnp.where(first_half, after, before)
                tiles.append(jnp.concatenate([strip[r, :, pl.ds(at, 128)], ends], axis=1))
            acc = acc + dot(ax[r, :, kp * 256 : (kp + 1) * 256], jnp.concatenate(tiles, axis=0))
        for half in range(2):
            ay[r, half, 0:144, :] = acc[:, 128 * half : 128 * half + 128]
        return carry

    lax.fori_loop(0, 8, y_stage, 0, unroll=2)
    w = wz[...]
    lane = iota((64, 128), 1)
    rims = jnp.zeros((64, 128), f32)
    for a in range(18):
        halves = [
            jnp.concatenate([ay[r, half, pl.ds(a, 8, stride=24), :] for r in range(8)], axis=0).astype(bf16)
            for half in range(2)
        ]
        col = jnp.concatenate(halves, axis=1)
        o = dot(w, jnp.concatenate([col, col, col], axis=0))
        rims = jnp.where(lane // 2 == a, pltpu.roll(o[:, 128:], 2 * a + 1, 1), rims)
        for d in range(8):
            out[d, a * 6 : a * 6 + 6, :] = o[d * 8 : d * 8 + 6, :128]
    for d in range(8):
        out[d, 108:114, :] = rims[d * 8 : d * 8 + 6]
        values = out[d, 0:114, :]
        peak = jnp.max(jnp.abs(values), axis=0, keepdims=True)
        code = jnp.ceil(16.0 * jnp.log2(jnp.maximum(peak, 1e-30)))
        scaled = values * (SCALE * jnp.exp2(code * -0.0625))
        scaled = jnp.concatenate([scaled, jnp.broadcast_to(code, (6, 128))], axis=0)
        packed[d] = jnp.round(scaled).astype(i32).astype(jnp.int16)


def sum_kernel(parts, out):
    total = jnp.zeros((114, 128), f32)
    for d in range(8):
        values = parts[d].astype(i32).astype(f32)
        total = total + values[0:114] * (jnp.exp2(values[114:115] * 0.0625) * (1.0 / SCALE))
    out[0:114] = total
    out[114:120] = jnp.zeros((6, 128), f32)


def weights_kernel(mag, own_low, own_high, z_low, z_high, stiff, sat, fields, aa):
    m0, hh, wx, wy, wz, ss = parts_of(fields)
    gx, gy, gz = (lax.axis_index(n) for n in ("gx", "gy", "gz"))
    row, col = iota((40, 384), 0), iota((40, 384), 1)
    inside = ((row < 32) | ((row < 36) & (gx < 7)) | ((row >= 36) & (gx > 0))) & (
        (col < 256) | ((col < 320) & (gy < 7)) | ((col >= 320) & (gy > 0))
    )
    unpacked = [unpack_rims(ref) for ref in (z_low, own_low, own_high, z_high)]
    for p in range(10):
        z = p - 3
        if z < 0:
            chunks, at, ok = unpacked[0], p * 4, gz > 0
        elif z > 3:
            chunks, at, ok = unpacked[3], (z - 4) * 4, gz < 7
        elif z < 3:
            chunks, at, ok = unpacked[1], z * 4, gz >= 0
        else:
            chunks, at, ok = unpacked[2], 8, gz >= 0
        whole = [jnp.concatenate([v[40 * (at + c) : 40 * (at + c) + 40] for v in chunks], axis=1) for c in range(4)]
        for c in range(3):
            m0[c, p] = whole[c]
            if 0 <= z < 4:
                m0[c, p, 0:32, 0:256] = mag[c, z]
        ids = whole[3].astype(i32)
        aa[p] = jnp.where(inside & ok, lookup(ids, stiff), 0.0)
        ss[p] = 2.0 / lookup(ids, sat)

    def weight(u, v):
        den = u + v
        return 2.0 * u * v / jnp.where(den > 0.0, den, 1.0)

    for p in range(10):
        here = aa[p]
        if 1 <= p <= 8:
            wx[p] = weight(here, pltpu.roll(here, 39, 0))
            wy[p] = weight(here, pltpu.roll(here, 383, 1))
        if p < 9:
            wz[p] = weight(here, aa[p + 1])

    fz = [wz[0] * (m0[c, 1] - m0[c, 0]) for c in range(3)]
    for p in range(1, 9):
        for c in range(3):
            total, fz[c] = exchange(m0, wx, wy, wz, c, p, fz[c])
            hh[c, p - 1] = total * ss[p]


def exchange(src, wx, wy, wz, c, p, below):
    m = src[c, p]
    flux = wx[p] * (pltpu.roll(m, 39, 0) - m)
    total = flux - pltpu.roll(flux, 1, 0)
    flux = wy[p] * (pltpu.roll(m, 383, 1) - m)
    total = total + (flux - pltpu.roll(flux, 1, 1))
    up = wz[p] * (src[c, p + 1] - m)
    return total + (up - below), up


def substeps_kernel(
    fields_hbm, d_own, d_low, d_high, state_out, demag_out, fields, m1, m2, fz, field, rows, spread, sems
):
    m0, hh, wx, wy, wz, ss = parts_of(fields)
    cuts = (pl.ds(0, 54), pl.ds(54, 40))
    fetches = [pltpu.make_async_copy(fields_hbm.at[c], fields.at[c], sems.at[n]) for n, c in enumerate(cuts)]
    for fetch in fetches:
        fetch.start()
    for q in range(6):
        demag_out[q // 3, q % 3] = d_own[pl.ds(6 + q, 16, stride=6), :]
    lane24 = iota((24, 128), 1)
    row24 = iota((24, 128), 0)
    sources = [(d_low, 3), (d_own, 0), (d_own, 3), (d_high, 0)]
    rows[...] = jnp.zeros_like(rows)
    for level in range(4):
        ref, first = sources[level]
        for i in range(3):
            g = level * 3 + i
            q = first + i
            rows[g * 24 : g * 24 + 18, 0:128] = ref[pl.ds(q, 18, stride=6), :]
            rim = jnp.broadcast_to(ref[108 + q : 109 + q, :], (24, 128))
            rows[g * 24 : g * 24 + 24, 128:256] = jnp.where(lane24 // 2 == row24, rim, 0.0)
    x = rows[...]
    hi = x.astype(bf16)
    lo = (x - hi.astype(f32)).astype(bf16)
    a, b = iota((128, 256), 0), iota((128, 256), 1)
    wide = one_hot(b // 2 == a)
    a, b = iota((128, 128), 0), iota((128, 128), 1)
    ends = one_hot(((a % 2 == 1) & (b < 2)) | ((a % 2 == 0) & (b >= 126)))
    spread[:, 0:256] = dot(hi[:, :128], wide) + dot(lo[:, :128], wide)
    spread[:, 256:384] = dot(hi[:, 128:], ends) + dot(lo[:, 128:], ends)
    r40, c24 = iota((40, 24), 0), iota((40, 24), 1)
    tall = one_hot(((r40 < 32) & (c24 == 1 + r40 // 2)) | ((r40 >= 32) & (r40 < 34) & (c24 == 17)) | ((r40 >= 38) & (c24 == 0)))
    for g in range(12):
        v = spread[g * 24 : (g + 1) * 24, :]
        hi = v.astype(bf16)
        lo = (v - hi.astype(f32)).astype(bf16)
        field[g] = dot(tall, hi) + dot(tall, lo)
    for step in range(3):
        src, dst = ((m0, m1), (m1, m2), (m2, None))[step]
        if step < 2:
            fetches[step].wait()
        first, last = step + 1, 8 - step

        def plane(p, carry):
            m = [src[c, p] for c in range(3)]
            level = (p - 1) // 2
            h = []
            for c in range(3):
                if step == 0:
                    total = hh[c, p - 1]
                else:
                    total, up = exchange(src, wx, wy, wz, c, p, fz[c])
                    fz[c] = up
                    total = total * ss[p]
                h.append(total + field[level * 3 + c])
            t = [m[1] * h[2] - m[2] * h[1], m[2] * h[0] - m[0] * h[2], m[0] * h[1] - m[1] * h[0]]
            u = [m[1] * t[2] - m[2] * t[1], m[2] * t[0] - m[0] * t[2], m[0] * t[1] - m[1] * t[0]]
            raw = [m[c] - TIME_STEP * (t[c] + DAMPING * u[c]) for c in range(3)]
            scale = lax.rsqrt(jnp.maximum(raw[0] * raw[0] + raw[1] * raw[1] + raw[2] * raw[2], 1e-30))
            for c in range(3):
                if step < 2:
                    dst[c, p] = raw[c] * scale
                else:
                    state_out[c, p - 3] = (raw[c] * scale)[0:32, 0:256]
            return carry

        if step:
            for c in range(3):
                fz[c] = wz[first - 1] * (src[c, first] - src[c, first - 1])
        lax.fori_loop(first, last + 1, plane, 0)


def swap(value, axis, bit):
    return lax.ppermute(value, axis, [(i, i ^ bit) for i in range(8)])


def step(magnet, grains, stiffness_table, saturation_table, kernel_x, kernel_y, kernel_z, mixing):
    shape = jax.ShapeDtypeStruct
    up = [(i, i + 1) for i in range(7)]
    down = [(i + 1, i) for i in range(7)]
    big = (10, 40, 384)
    (pay,) = call(
        coarse_kernel,
        shape((128, 128), bf16),
        [VM, VM, SM],
        [pltpu.VMEM((6, 32, 256), f32)],
        20_000_000,
        600_000,
    )(magnet, grains, saturation_table)
    other = swap(pay, "gy", 4)
    edges, cells, block = call(
        block_kernel,
        [shape((2, 48, 256), f32), shape((512, 256), bf16), shape((4, 256, 128), bf16)],
        [VM] * 3,
        (),
        1_000_000,
        1_500_000,
        16 << 20,
    )(magnet, grains, pay)
    strip, kx, wz = call(
        toeplitz_kernel,
        [shape((8, 128, 2176), bf16), shape((192, 128), f32), shape((64, 192), bf16)],
        [VM, VM, VM, SM],
        [pltpu.VMEM((8, 2176), f32), pltpu.VMEM((8, 128, 2176), bf16), pltpu.SemaphoreType.DMA((8,))],
        20_000_000,
        5_000_000,
        FULL - 14_000_000,
        [HB, VM, VM],
    )(kernel_x, kernel_y, kernel_z, mixing.transpose(1, 2, 0))
    (pay,) = call(pair_kernel, shape((4, 256, 128), bf16), [VM] * 2, (), 1000, 400_000, 8 << 20, None, {0: 0})(block, other)
    groups = [[0, 1, 2, 3], [4, 5, 6, 7]]
    gathered = lax.all_to_all(pay, "gy", 0, 0, tiled=True, axis_index_groups=groups)
    pay, face_a, rim = call(
        faces_kernel,
        [shape((4, 912, 128), bf16), shape((144, 128), bf16), shape((512, 128), bf16)],
        [VM] * 2,
        [pltpu.VMEM((48, 128), f32)] * 2,
        1_000_000,
        1_000_000,
        8 << 20,
    )(gathered, edges)
    groups = [[0, 2, 4, 6], [1, 3, 5, 7]]
    gathered = lax.all_to_all(pay, "gx", 0, 0, tiled=True, axis_index_groups=groups)
    near = swap(face_a, "gx", 1)
    rc = swap(gathered, "gx", 1)
    own_low, own_high = call(
        rims_kernel,
        [shape((992, 128), bf16)] * 2,
        [VM] * 4,
        [pltpu.VMEM((3, 672, 128), f32), pltpu.VMEM((144, 128), f32), pltpu.VMEM((144, 128), f32)],
        1_000_000,
        2_000_000,
        12 << 20,
    )(cells, rim, near, rc)
    z_low = lax.ppermute(own_high, "gz", up)
    z_high = lax.ppermute(own_low, "gz", down)
    (parts,) = call(
        stages_kernel,
        shape((8, 120, 128), jnp.int16),
        [VM, VM, VM, HB, VM],
        [pltpu.VMEM((8, 144, 1024), bf16), pltpu.VMEM((8, 2, 192, 128), f32), pltpu.VMEM((8, 120, 128), f32)]
        + [pltpu.VMEM((8, 128, 2176), bf16), pltpu.SemaphoreType.DMA],
        2_000_000_000,
        10_000_000,
        FULL - (16 << 20),
    )(gathered, rc, kx, strip, wz)
    parts = lax.all_to_all(parts, "gz", 0, 0, tiled=True)
    (fields,) = call(
        weights_kernel,
        shape((94, 40, 384), f32),
        [VM] * 5 + [SM] * 2,
        [pltpu.VMEM(big, f32)],
        20_000_000,
        5_000_000,
    )(magnet, own_low, own_high, z_low, z_high, stiffness_table, saturation_table)
    (d_own,) = call(sum_kernel, shape((120, 128), f32), [VM], (), 100_000, 300_000, 8 << 20)(parts)
    d_low = lax.ppermute(d_own, "gz", up)
    d_high = lax.ppermute(d_own, "gz", down)
    state, demag = call(
        substeps_kernel,
        [shape((3, 4, 32, 256), f32), shape((2, 3, 16, 128), f32)],
        [HB] + [VM] * 3,
        [pltpu.VMEM((94, 40, 384), f32)]
        + [pltpu.VMEM((3,) + big, f32)] * 2
        + [pltpu.VMEM((3, 40, 384), f32), pltpu.VMEM((12, 40, 384), f32)]
        + [pltpu.VMEM((288, 256), f32), pltpu.VMEM((288, 384), f32), pltpu.SemaphoreType.DMA((2,))],
        50_000_000,
        5_000_000,
        FULL - 14_000_000,
    )(fields, d_own, d_low, d_high)
    return (state, demag)


def solution(mesh):
    in_specs = (P(None, "gz", "gx", "gy"), P("gz", "gx", "gy"), P(), P(), P(), P(), P(), P())
    out_specs = (P(None, "gz", "gx", "gy"), P("gz", None, "gx", "gy"))
    return jax.shard_map(step, mesh=mesh, in_specs=in_specs, out_specs=out_specs, check_vma=False)
```

```python
import jax
import jax.numpy as jnp
from jax import lax
from jax.experimental import pallas as pl
from jax.experimental.pallas import tpu as pltpu
from jax.sharding import PartitionSpec as P


f32, bf16, i32 = jnp.float32, jnp.bfloat16, jnp.int32
VM = pl.BlockSpec(memory_space=pltpu.VMEM)
SM = pl.BlockSpec(memory_space=pltpu.SMEM)
HB = pl.BlockSpec(memory_space=pltpu.MemorySpace.HBM)
TIME_STEP = 0.02
DAMPING = 0.3
SCALE = 32000.0
FULL = 67_043_328


def iota(shape, dim):
    return lax.broadcasted_iota(i32, shape, dim)


def one_hot(condition):
    return jnp.where(condition, 1.0, 0.0).astype(bf16)


def dot(a, b, dims=((1,), (0,))):
    return lax.dot_general(a, b, (dims, ((), ())), preferred_element_type=f32)


class Planes:
    def __init__(self, ref, base, inner=0):
        self.ref, self.base, self.inner = ref, base, inner

    def key(self, k):
        k = k if isinstance(k, tuple) else (k,)
        if self.inner:
            return (self.base + k[0] * self.inner + k[1],) + k[2:]
        return (self.base + k[0],) + k[1:]

    def __getitem__(self, k):
        return self.ref[self.key(k)]

    def __setitem__(self, k, value):
        self.ref[self.key(k)] = value


def parts_of(ref):
    layout = ((0, 10), (30, 8), (54, 0), (64, 0), (74, 0), (84, 0))
    return [Planes(ref, base, inner) for base, inner in layout]


def lookup(ids, table):
    bits = [(ids & (1 << k)) != 0 for k in range(4)]
    level = [table[k] for k in range(16)]
    for bit in bits:
        level = [jnp.where(bit, level[2 * k + 1], level[2 * k]) for k in range(len(level) // 2)]
    return level[0]


def call(body, out_shape, in_specs, scratch=(), flops=0, nbytes=0, vmem=None, out_specs=None, alias={}):
    outs = out_shape if isinstance(out_shape, list) else [out_shape]
    result = pl.pallas_call(
        body,
        out_shape=outs,
        in_specs=in_specs,
        out_specs=out_specs or [VM] * len(outs),
        scratch_shapes=list(scratch),
        input_output_aliases=alias,
        compiler_params=pltpu.CompilerParams(vmem_limit_bytes=vmem),
        cost_estimate=pl.CostEstimate(flops=flops, bytes_accessed=nbytes, transcendentals=0),
    )
    return result


def coarse_kernel(mag, grains, sat, out, scr):
    for a in range(2):
        s0 = lookup(grains[2 * a], sat)
        s1 = lookup(grains[2 * a + 1], sat)
        for j in range(3):
            scr[j * 2 + a] = s0 * mag[j, 2 * a] + s1 * mag[j, 2 * a + 1]
    pick = one_hot(iota((256, 128), 0) == 2 * iota((256, 128), 1))
    rows = []
    for p in range(6):
        s = scr[p].reshape(16, 2, 256)
        s = s[:, 0, :] + s[:, 1, :]
        s = s + pltpu.roll(s, 255, 1)
        rows.append((s * 0.125).astype(bf16))
    coarse = dot(jnp.concatenate(rows, axis=0), pick).astype(bf16)
    cells = [mag[j].reshape(128, 256).astype(bf16) for j in range(3)]
    cells.append(grains[...].reshape(128, 256).astype(f32).astype(bf16))
    cells = jnp.concatenate(cells, axis=0)
    k, lane = iota((8, 256), 0), iota((8, 256), 1)
    edge = one_hot(((k < 3) & (lane == k)) | ((k >= 4) & (k < 7) & (lane == 249 + k)))
    faces = dot(edge, cells, ((1,), (1,)))
    faces = jnp.concatenate([faces[:, 128 * q : 128 * (q + 1)] for q in range(4)], axis=0).astype(bf16)
    out[0:96, :] = coarse
    out[96:128, :] = faces


def block_kernel(mag, grains, own, edges, cells, out):
    for n in range(4):
        out[n, 0:128, :] = own[...]
        out[n, 128:256, :] = own[...]
    for c in range(4):
        for z in range(4):
            at = c * 4 + z
            plane = mag[c, z] if c < 3 else grains[z].astype(f32)
            edges[0, 3 * at : 3 * at + 3, :] = plane[0:3]
            edges[1, 3 * at : 3 * at + 3, :] = plane[29:32]
            cells[32 * at : 32 * at + 32, :] = plane.astype(bf16)


def pair_kernel(block, other, out):
    for n in range(4):
        out[n, 128:256, :] = other[...]


def toeplitz_kernel(kernel_x, kernel_y, kernel_z, mixing, strip_hbm, kx_out, wz_out, kyp, strip, sems):
    gx, gz = lax.axis_index("gx"), lax.axis_index("gz")
    kyp[...] = jnp.zeros_like(kyp)
    kyp[:, 0:2048] = kernel_y[...].astype(f32)

    def send(r):
        return pltpu.make_async_copy(strip.at[r], strip_hbm.at[r], sems.at[r])

    def one(r, carry):
        row = jnp.broadcast_to(kyp[pl.ds(r, 1), :], (128, 2176))
        strip[pl.ds(r, 1)] = pltpu.roll(row, 0, 1, stride=1, stride_axis=0).astype(bf16)[None]
        send(r).start()
        return carry

    lax.fori_loop(0, 8, one, 0)
    mirror = one_hot(iota((256, 256), 0) + iota((256, 256), 1) == 255)
    kxr = dot(kernel_x[...], mirror)
    row, col = iota((64, 32), 0), iota((64, 32), 1)
    level = 2 * (row // 8) + jnp.where(row % 8 >= 3, 1, 0) + 16 - 2 * gz
    row, col8 = iota((8, 64), 0), iota((8, 64), 1)
    total = jnp.zeros((64, 64), f32)
    for zl in range(2):
        per_rank = dot(one_hot(col == level - zl), kernel_z[...], ((1,), (1,)))
        total = total + dot(per_rank.astype(bf16), one_hot((col8 // 8 == row) & (col8 % 8 < 6) & (col8 % 2 == zl)))
    row, col = iota((64, 64), 0), iota((64, 64), 1)
    i_of = jnp.where(row % 8 < 6, row % 8 % 3, 3)
    rj_of = col // 2
    mix = jnp.zeros((64, 64), f32)
    for i in range(3):
        line = jnp.zeros((1, 64), f32)
        for r in range(8):
            for j in range(3):
                line = jnp.where(rj_of[0:1] == r * 4 + j, mixing[i, j, r], line)
        mix = jnp.where(i_of == i, line, mix)
    w = mix * total
    hi = w.astype(bf16)
    rest = w - hi.astype(f32)
    mid = rest.astype(bf16)
    wz_out[:, 0:64] = hi
    wz_out[:, 64:128] = mid
    wz_out[:, 128:192] = (rest - mid.astype(f32)).astype(bf16)

    lane = iota((24, 256), 1)
    for r in range(8):
        row = pltpu.roll(jnp.broadcast_to(kxr[r : r + 1, :], (24, 256)), 0, 1, stride=1, stride_axis=0)
        total = jnp.zeros((24, 256), f32)
        for l in range(8):
            block = 2 * (l % 4) + ((gx & 1) if l < 4 else 1 - (gx & 1))
            shift = (16 * l + 16 * (gx - block) + 128 + 512) & 255
            total = jnp.where(lane // 16 == l, pltpu.roll(row, shift, 1), total)
        kx_out[r * 24 : (r + 1) * 24, :] = total[:, :128]
    for r in range(8):
        send(r).wait()


def faces_kernel(gathered, edges, pay, face_a, rim, low, high):
    gx, gy = lax.axis_index("gx"), lax.axis_index("gy")
    y = gy & 3

    def faces(n, row):
        rows = gathered[n, row : row + 32, :].astype(f32)
        return jnp.concatenate([rows[8 * q : 8 * (q + 1)] for q in range(4)], axis=1)

    right = jnp.where(gy == 3, faces(0, 224), faces(jnp.minimum(y + 1, 3), 96))
    left = jnp.where(gy == 4, faces(3, 224), faces(jnp.maximum(y - 1, 0), 96))
    sel = jnp.where(iota((8, 512), 0) < 4, right, left)
    k, lane = iota((8, 128), 0), iota((8, 128), 1)
    put = one_hot(((k < 3) & (lane == k)) | ((k >= 4) & (k < 7) & (lane == 121 + k)))
    unpacked = dot(sel.astype(bf16), put, ((0,), (0,)))
    rim[...] = unpacked.astype(bf16)
    for n in range(16):
        low[3 * n : 3 * n + 3] = unpacked[32 * n : 32 * n + 3]
        high[3 * n : 3 * n + 3] = unpacked[32 * n + 29 : 32 * n + 32]
    odd = (gx & 1) == 1
    to_b = [jnp.where(odd, edges[1], edges[0]).astype(bf16), jnp.where(odd, high[...], low[...]).astype(bf16)]
    to_a = [jnp.where(odd, edges[0], edges[1]).astype(bf16), jnp.where(odd, low[...], high[...]).astype(bf16)]
    face_a[0:48, :] = to_a[0][:, :128]
    face_a[48:96, :] = to_a[0][:, 128:]
    face_a[96:144, :] = to_a[1]
    for n in range(4):
        for k in range(4):
            pay[n, k * 96 : (k + 1) * 96, :] = gathered[k, 0:96, :]
            pay[n, (k + 4) * 96 : (k + 5) * 96, :] = gathered[k, 128:224, :]
        pay[n, 768:816, :] = to_b[0][:, :128]
        pay[n, 816:864, :] = to_b[0][:, 128:]
        pay[n, 864:912, :] = to_b[1]


def rims_kernel(cells, rim, near, rc, low_out, high_out, scr, fa, fb):
    gx = lax.axis_index("gx")
    even = (gx & 1) == 0
    chip = gx // 2
    a = near[...].astype(f32)
    b = rc[jnp.where(even, jnp.maximum(chip - 1, 0), jnp.minimum(chip + 1, 3)), 768:912, :].astype(f32)
    fa[...] = jnp.where(even, a, b)
    fb[...] = jnp.where(even, b, a)
    scr[2, 640:672, :] = jnp.zeros((32, 128), f32)
    for z in range(4):
        for c in range(4):
            plane, top, at = (c * 4 + z) * 32, (z * 4 + c) * 40, (c * 4 + z) * 3
            for q in range(3):
                if q < 2:
                    scr[q, top : top + 32] = cells[plane : plane + 32, q * 128 : (q + 1) * 128].astype(f32)
                else:
                    scr[q, top : top + 32] = rim[plane : plane + 32, :].astype(f32)
                scr[q, top + 32 : top + 40] = jnp.zeros((8, 128), f32)
                scr[q, top + 32 : top + 35] = fa[q * 48 + at : q * 48 + at + 3, :]
                scr[q, top + 37 : top + 40] = fb[q * 48 + at : q * 48 + at + 3, :]
    for out, first in ((low_out, 0), (high_out, 160)):
        for q in range(2):
            out[q * 480 : (q + 1) * 480, :] = scr[q, first : first + 480].astype(bf16)
        ends = dot(rim_lanes(), scr[2, first : first + 512].astype(bf16), ((1,), (1,)))
        ends = jnp.concatenate([ends[:, 128 * n : 128 * (n + 1)] for n in range(4)], axis=0)
        out[960:992, :] = ends.astype(bf16)


def rim_lanes():
    k, lane = iota((8, 128), 0), iota((8, 128), 1)
    return one_hot(((k < 3) & (lane == k)) | ((k >= 4) & (k < 7) & (lane == 121 + k)))


def unpack_rims(ref):
    ends = ref[960:992, :].astype(f32)
    ends = jnp.concatenate([ends[8 * n : 8 * (n + 1)] for n in range(4)], axis=1)
    ends = dot(ends.astype(bf16), rim_lanes(), ((0,), (0,)))
    return [ref[0:480, :].astype(f32), ref[480:960, :].astype(f32), ends]


def stages_kernel(own, rc, kx, strip_hbm, wz, packed, ax, ay, out, strip, sem):
    gy = lax.axis_index("gy")
    kxm = kx[...].astype(bf16)
    fetch = pltpu.make_async_copy(strip_hbm, strip, sem)
    fetch.start()

    def x_stage(kp, carry):
        for pair in range(3):
            res = []
            for jz in range(2):
                halves = []
                for half in range(2):
                    at = pl.multiple_of(((2 * kp + half) * 6 + 2 * pair + jz) * 16, 16)
                    parts = [ref[n, pl.ds(at, 16), :] for ref in (own, rc) for n in range(4)]
                    halves.append(jnp.concatenate(parts, axis=0))
                res.append(dot(kxm, jnp.concatenate(halves, axis=1)))
            for r in range(8):
                both = jnp.concatenate([res[0][r * 24 : (r + 1) * 24], res[1][r * 24 : (r + 1) * 24]], axis=0)
                ax[r, pair * 48 : pair * 48 + 48, pl.ds(pl.multiple_of(kp * 256, 256), 256)] = both.astype(bf16)
        return carry

    lax.fori_loop(0, 4, x_stage, 0)
    for r in range(8):
        for half in range(2):
            ay[r, half, 144:192, :] = jnp.zeros((48, 128), f32)
    fetch.wait()

    first_half = iota((128, 128), 1) < 64

    def y_stage(r, carry):
        acc = jnp.zeros((144, 256), f32)
        for kp in range(4):
            tiles = []
            for k in (2 * kp, 2 * kp + 1):
                block = (gy & 4) + k if k < 4 else k - (gy & 4)
                at = pl.multiple_of(128 * (8 + gy - block), 128)
                after, before = strip[r, :, pl.ds(at + 128, 128)], strip[r, :, pl.ds(at - 128, 128)]
                ends = jnp.where(first_half, after, before)
                tiles.append(jnp.concatenate([strip[r, :, pl.ds(at, 128)], ends], axis=1))
            acc = acc + dot(ax[r, :, kp * 256 : (kp + 1) * 256], jnp.concatenate(tiles, axis=0))
        for half in range(2):
            ay[r, half, 0:144, :] = acc[:, 128 * half : 128 * half + 128]
        return carry

    lax.fori_loop(0, 8, y_stage, 0, unroll=2)
    w = wz[...]
    lane = iota((64, 128), 1)
    rims = jnp.zeros((64, 128), f32)
    for a in range(18):
        halves = [
            jnp.concatenate([ay[r, half, pl.ds(a, 8, stride=24), :] for r in range(8)], axis=0).astype(bf16)
            for half in range(2)
        ]
        col = jnp.concatenate(halves, axis=1)
        o = dot(w, jnp.concatenate([col, col, col], axis=0))
        rims = jnp.where(lane // 2 == a, pltpu.roll(o[:, 128:], 2 * a + 1, 1), rims)
        for d in range(8):
            out[d, a * 6 : a * 6 + 6, :] = o[d * 8 : d * 8 + 6, :128]
    for d in range(8):
        out[d, 108:114, :] = rims[d * 8 : d * 8 + 6]
        values = out[d, 0:114, :]
        peak = jnp.max(jnp.abs(values), axis=0, keepdims=True)
        code = jnp.ceil(16.0 * jnp.log2(jnp.maximum(peak, 1e-30)))
        scaled = values * (SCALE * jnp.exp2(code * -0.0625))
        scaled = jnp.concatenate([scaled, jnp.broadcast_to(code, (6, 128))], axis=0)
        packed[d] = jnp.round(scaled).astype(i32).astype(jnp.int16)


def sum_kernel(parts, out):
    total = jnp.zeros((114, 128), f32)
    for d in range(8):
        values = parts[d].astype(i32).astype(f32)
        total = total + values[0:114] * (jnp.exp2(values[114:115] * 0.0625) * (1.0 / SCALE))
    out[0:114] = total
    out[114:120] = jnp.zeros((6, 128), f32)


def weights_kernel(mag, own_low, own_high, z_low, z_high, stiff, sat, fields, aa):
    m0, hh, wx, wy, wz, ss = parts_of(fields)
    gx, gy, gz = (lax.axis_index(n) for n in ("gx", "gy", "gz"))
    row, col = iota((40, 384), 0), iota((40, 384), 1)
    inside = ((row < 32) | ((row < 36) & (gx < 7)) | ((row >= 36) & (gx > 0))) & (
        (col < 256) | ((col < 320) & (gy < 7)) | ((col >= 320) & (gy > 0))
    )
    unpacked = [unpack_rims(ref) for ref in (z_low, own_low, own_high, z_high)]
    for p in range(10):
        z = p - 3
        if z < 0:
            chunks, at, ok = unpacked[0], p * 4, gz > 0
        elif z > 3:
            chunks, at, ok = unpacked[3], (z - 4) * 4, gz < 7
        elif z < 3:
            chunks, at, ok = unpacked[1], z * 4, gz >= 0
        else:
            chunks, at, ok = unpacked[2], 8, gz >= 0
        whole = [jnp.concatenate([v[40 * (at + c) : 40 * (at + c) + 40] for v in chunks], axis=1) for c in range(4)]
        for c in range(3):
            m0[c, p] = whole[c]
            if 0 <= z < 4:
                m0[c, p, 0:32, 0:256] = mag[c, z]
        ids = whole[3].astype(i32)
        aa[p] = jnp.where(inside & ok, lookup(ids, stiff), 0.0)
        ss[p] = (2.0 * TIME_STEP) / lookup(ids, sat)

    def weight(u, v):
        den = u + v
        return 2.0 * u * v / jnp.where(den > 0.0, den, 1.0)

    for p in range(10):
        here = aa[p]
        if 1 <= p <= 8:
            wx[p] = weight(here, pltpu.roll(here, 39, 0))
            wy[p] = weight(here, pltpu.roll(here, 383, 1))
        if p < 9:
            wz[p] = weight(here, aa[p + 1])

    fz = [wz[0] * (m0[c, 1] - m0[c, 0]) for c in range(3)]
    for p in range(1, 9):
        for c in range(3):
            total, fz[c] = exchange(m0, wx, wy, wz, c, p, fz[c])
            hh[c, p - 1] = total * ss[p]


def exchange(src, wx, wy, wz, c, p, below):
    m = src[c, p]
    flux = wx[p] * (pltpu.roll(m, 39, 0) - m)
    total = flux - pltpu.roll(flux, 1, 0)
    flux = wy[p] * (pltpu.roll(m, 383, 1) - m)
    total = total + (flux - pltpu.roll(flux, 1, 1))
    up = wz[p] * (src[c, p + 1] - m)
    return total + (up - below), up


def substeps_kernel(
    fields_hbm, d_own, d_low, d_high, state_out, demag_out, fields, m1, m2, fz, field, rows, sems
):
    m0, hh, wx, wy, wz, ss = parts_of(fields)
    spans = ((1, 8), (11, 8), (21, 8), (30, 24), (56, 6), (66, 6), (75, 7), (86, 6))
    cuts = [pl.ds(first, count) for first, count in spans]
    fetches = [pltpu.make_async_copy(fields_hbm.at[c], fields.at[c], sems.at[n]) for n, c in enumerate(cuts)]
    for fetch in fetches:
        fetch.start()
    for q in range(6):
        demag_out[q // 3, q % 3] = d_own[pl.ds(6 + q, 16, stride=6), :]
    lane24, row24 = iota((24, 128), 1), iota((24, 128), 0)
    coarse_x = jnp.where(row24 == 17, 0, row24 + 1)
    sources = [(d_low, 3), (d_own, 0), (d_own, 3), (d_high, 0)]
    for level in range(4):
        ref, first = sources[level]
        for i in range(3):
            top, q = (level * 3 + i) * 24, first + i
            rows[top : top + 16, 0:128] = ref[pl.ds(6 + q, 16, stride=6), :]
            ends = jnp.where(row24[0:8] == 0, ref[102 + q : 103 + q, :], ref[q : q + 1, :])
            rows[top + 16 : top + 24, 0:128] = ends
            rim = jnp.broadcast_to(ref[108 + q : 109 + q, :], (24, 128))
            rows[top : top + 24, 128:256] = jnp.where(lane24 // 2 == coarse_x, rim, 0.0)
    x = rows[...]
    hi = x.astype(bf16)
    lo = (x - hi.astype(f32)).astype(bf16)
    a, b = iota((256, 256), 0) % 128, iota((256, 256), 1)
    wide = one_hot(b // 2 == a)
    a, b = iota((256, 128), 0) % 128, iota((256, 128), 1)
    ends = one_hot(((a % 2 == 1) & (b < 2)) | ((a % 2 == 0) & (b >= 126)))
    block = dot(jnp.concatenate([hi[:, :128], lo[:, :128]], axis=1), wide) * TIME_STEP
    sides = dot(jnp.concatenate([hi[:, 128:], lo[:, 128:]], axis=1), ends) * TIME_STEP
    row8 = iota((8, 128), 0)
    for g in range(12):
        for q in range(3):
            v = block[g * 24 : (g + 1) * 24, q * 128 : (q + 1) * 128] if q < 2 else sides[g * 24 : (g + 1) * 24]
            field[g, q, pl.ds(0, 16, stride=2), :] = v[0:16]
            field[g, q, pl.ds(1, 16, stride=2), :] = v[0:16]
            field[g, q, 32:40, :] = jnp.where(row8 < 2, v[16:17], jnp.where(row8 >= 6, v[17:18], 0.0))
    for step in range(3):
        src, dst = ((m0, m1), (m1, m2), (m2, None))[step]
        if step < 2:
            for fetch in (fetches[:4], fetches[4:])[step]:
                fetch.wait()
        first, last = step + 1, 8 - step

        def plane(p, carry):
            m = [src[c, p] for c in range(3)]
            level = (p - 1) // 2
            h = []
            for c in range(3):
                if step == 0:
                    total = hh[c, p - 1]
                else:
                    total, up = exchange(src, wx, wy, wz, c, p, fz[c])
                    fz[c] = up
                    total = total * ss[p]
                h.append(total + jnp.concatenate([field[level * 3 + c, q] for q in range(3)], axis=1))
            t = [m[1] * h[2] - m[2] * h[1], m[2] * h[0] - m[0] * h[2], m[0] * h[1] - m[1] * h[0]]
            u = [m[1] * t[2] - m[2] * t[1], m[2] * t[0] - m[0] * t[2], m[0] * t[1] - m[1] * t[0]]
            raw = [m[c] - (t[c] + DAMPING * u[c]) for c in range(3)]
            scale = lax.rsqrt(jnp.maximum(raw[0] * raw[0] + raw[1] * raw[1] + raw[2] * raw[2], 1e-30))
            for c in range(3):
                if step < 2:
                    dst[c, p] = raw[c] * scale
                else:
                    state_out[c, p - 3] = (raw[c] * scale)[0:32, 0:256]
            return carry

        if step:
            for c in range(3):
                fz[c] = wz[first - 1] * (src[c, first] - src[c, first - 1])
        lax.fori_loop(first, last + 1, plane, 0)


def swap(value, axis, bit):
    return lax.ppermute(value, axis, [(i, i ^ bit) for i in range(8)])


def step(magnet, grains, stiffness_table, saturation_table, kernel_x, kernel_y, kernel_z, mixing):
    shape = jax.ShapeDtypeStruct
    up = [(i, i + 1) for i in range(7)]
    down = [(i + 1, i) for i in range(7)]
    big = (10, 40, 384)
    (pay,) = call(
        coarse_kernel,
        shape((128, 128), bf16),
        [VM, VM, SM],
        [pltpu.VMEM((6, 32, 256), f32)],
        20_000_000,
        600_000,
    )(magnet, grains, saturation_table)
    other = swap(pay, "gy", 4)
    edges, cells, block = call(
        block_kernel,
        [shape((2, 48, 256), f32), shape((512, 256), bf16), shape((4, 256, 128), bf16)],
        [VM] * 3,
        (),
        1_000_000,
        1_500_000,
        16 << 20,
    )(magnet, grains, pay)
    strip, kx, wz = call(
        toeplitz_kernel,
        [shape((8, 128, 2176), bf16), shape((192, 128), f32), shape((64, 192), bf16)],
        [VM, VM, VM, SM],
        [pltpu.VMEM((8, 2176), f32), pltpu.VMEM((8, 128, 2176), bf16), pltpu.SemaphoreType.DMA((8,))],
        20_000_000,
        5_000_000,
        FULL - 14_000_000,
        [HB, VM, VM],
    )(kernel_x, kernel_y, kernel_z, mixing.transpose(1, 2, 0))
    (pay,) = call(pair_kernel, shape((4, 256, 128), bf16), [VM] * 2, (), 1000, 400_000, 8 << 20, None, {0: 0})(block, other)
    groups = [[0, 1, 2, 3], [4, 5, 6, 7]]
    gathered = lax.all_to_all(pay, "gy", 0, 0, tiled=True, axis_index_groups=groups)
    pay, face_a, rim = call(
        faces_kernel,
        [shape((4, 912, 128), bf16), shape((144, 128), bf16), shape((512, 128), bf16)],
        [VM] * 2,
        [pltpu.VMEM((48, 128), f32)] * 2,
        1_000_000,
        1_000_000,
        8 << 20,
    )(gathered, edges)
    groups = [[0, 2, 4, 6], [1, 3, 5, 7]]
    gathered = lax.all_to_all(pay, "gx", 0, 0, tiled=True, axis_index_groups=groups)
    near = swap(face_a, "gx", 1)
    rc = swap(gathered, "gx", 1)
    own_low, own_high = call(
        rims_kernel,
        [shape((992, 128), bf16)] * 2,
        [VM] * 4,
        [pltpu.VMEM((3, 672, 128), f32), pltpu.VMEM((144, 128), f32), pltpu.VMEM((144, 128), f32)],
        1_000_000,
        2_000_000,
        12 << 20,
    )(cells, rim, near, rc)
    z_low = lax.ppermute(own_high, "gz", up)
    z_high = lax.ppermute(own_low, "gz", down)
    (parts,) = call(
        stages_kernel,
        shape((8, 120, 128), jnp.int16),
        [VM, VM, VM, HB, VM],
        [pltpu.VMEM((8, 144, 1024), bf16), pltpu.VMEM((8, 2, 192, 128), f32), pltpu.VMEM((8, 120, 128), f32)]
        + [pltpu.VMEM((8, 128, 2176), bf16), pltpu.SemaphoreType.DMA],
        2_000_000_000,
        10_000_000,
        FULL - (16 << 20),
    )(gathered, rc, kx, strip, wz)
    parts = lax.all_to_all(parts, "gz", 0, 0, tiled=True)
    (fields,) = call(
        weights_kernel,
        shape((94, 40, 384), f32),
        [VM] * 5 + [SM] * 2,
        [pltpu.VMEM(big, f32)],
        20_000_000,
        5_000_000,
    )(magnet, own_low, own_high, z_low, z_high, stiffness_table, saturation_table)
    (d_own,) = call(sum_kernel, shape((120, 128), f32), [VM], (), 100_000, 300_000, 8 << 20)(parts)
    d_low = lax.ppermute(d_own, "gz", up)
    d_high = lax.ppermute(d_own, "gz", down)
    state, demag = call(
        substeps_kernel,
        [shape((3, 4, 32, 256), f32), shape((2, 3, 16, 128), f32)],
        [HB] + [VM] * 3,
        [pltpu.VMEM((94, 40, 384), f32)]
        + [pltpu.VMEM((3,) + big, f32)] * 2
        + [pltpu.VMEM((3, 40, 384), f32), pltpu.VMEM((12, 3, 40, 128), f32)]
        + [pltpu.VMEM((288, 256), f32), pltpu.SemaphoreType.DMA((8,))],
        50_000_000,
        5_000_000,
        FULL - 14_000_000,
    )(fields, d_own, d_low, d_high)
    return (state, demag)


def solution(mesh):
    in_specs = (P(None, "gz", "gx", "gy"), P("gz", "gx", "gy"), P(), P(), P(), P(), P(), P())
    out_specs = (P(None, "gz", "gx", "gy"), P("gz", None, "gx", "gy"))
    return jax.shard_map(step, mesh=mesh, in_specs=in_specs, out_specs=out_specs, check_vma=False)
```

```python
import jax
import jax.numpy as jnp
from jax import lax
from jax.experimental import pallas as pl
from jax.experimental.pallas import tpu as pltpu
from jax.sharding import PartitionSpec as P


f32, bf16, i32 = jnp.float32, jnp.bfloat16, jnp.int32
VM = pl.BlockSpec(memory_space=pltpu.VMEM)
SM = pl.BlockSpec(memory_space=pltpu.SMEM)
HB = pl.BlockSpec(memory_space=pltpu.MemorySpace.HBM)
TIME_STEP = 0.02
DAMPING = 0.3
SCALE = 32000.0
FULL = 67_043_328
FAR = [(pl.ds(a, n), pl.ds(b, n)) for a, b, n in ((56, 0, 6), (66, 6, 6), (75, 12, 7), (86, 19, 6))]


def iota(shape, dim):
    return lax.broadcasted_iota(i32, shape, dim)


def one_hot(condition):
    return jnp.where(condition, 1.0, 0.0).astype(bf16)


def dot(a, b, dims=((1,), (0,))):
    return lax.dot_general(a, b, (dims, ((), ())), preferred_element_type=f32)


class Planes:
    def __init__(self, ref, base, inner=0):
        self.ref, self.base, self.inner = ref, base, inner

    def key(self, k):
        k = k if isinstance(k, tuple) else (k,)
        if self.inner:
            return (self.base + k[0] * self.inner + k[1],) + k[2:]
        return (self.base + k[0],) + k[1:]

    def __getitem__(self, k):
        return self.ref[self.key(k)]

    def __setitem__(self, k, value):
        self.ref[self.key(k)] = value


def parts_of(ref):
    layout = ((0, 10), (30, 8), (54, 0), (64, 0), (74, 0), (84, 0))
    return [Planes(ref, base, inner) for base, inner in layout]


def lookup(ids, table):
    bits = [(ids & (1 << k)) != 0 for k in range(4)]
    level = [table[k] for k in range(16)]
    for bit in bits:
        level = [jnp.where(bit, level[2 * k + 1], level[2 * k]) for k in range(len(level) // 2)]
    return level[0]


def call(body, out_shape, in_specs, scratch=(), flops=0, nbytes=0, vmem=None, out_specs=None, alias={}):
    outs = out_shape if isinstance(out_shape, list) else [out_shape]
    result = pl.pallas_call(
        body,
        out_shape=outs,
        in_specs=in_specs,
        out_specs=out_specs or [VM] * len(outs),
        scratch_shapes=list(scratch),
        input_output_aliases=alias,
        compiler_params=pltpu.CompilerParams(vmem_limit_bytes=vmem),
        cost_estimate=pl.CostEstimate(flops=flops, bytes_accessed=nbytes, transcendentals=0),
    )
    return result


def coarse_kernel(mag, grains, sat, out, scr):
    for a in range(2):
        s0 = lookup(grains[2 * a], sat)
        s1 = lookup(grains[2 * a + 1], sat)
        for j in range(3):
            scr[j * 2 + a] = s0 * mag[j, 2 * a] + s1 * mag[j, 2 * a + 1]
    pick = one_hot(iota((256, 128), 0) == 2 * iota((256, 128), 1))
    rows = []
    for p in range(6):
        s = scr[p].reshape(16, 2, 256)
        s = s[:, 0, :] + s[:, 1, :]
        s = s + pltpu.roll(s, 255, 1)
        rows.append((s * 0.125).astype(bf16))
    coarse = dot(jnp.concatenate(rows, axis=0), pick).astype(bf16)
    cells = [mag[j].reshape(128, 256).astype(bf16) for j in range(3)]
    cells.append(grains[...].reshape(128, 256).astype(f32).astype(bf16))
    cells = jnp.concatenate(cells, axis=0)
    k, lane = iota((8, 256), 0), iota((8, 256), 1)
    edge = one_hot(((k < 3) & (lane == k)) | ((k >= 4) & (k < 7) & (lane == 249 + k)))
    faces = dot(edge, cells, ((1,), (1,)))
    faces = jnp.concatenate([faces[:, 128 * q : 128 * (q + 1)] for q in range(4)], axis=0).astype(bf16)
    out[0:96, :] = coarse
    out[96:128, :] = faces


def block_kernel(mag, grains, own, edges, cells, out):
    for n in range(4):
        out[n, 0:128, :] = own[...]
        out[n, 128:256, :] = own[...]
    for c in range(4):
        for z in range(4):
            at = c * 4 + z
            plane = mag[c, z] if c < 3 else grains[z].astype(f32)
            edges[0, 3 * at : 3 * at + 3, :] = plane[0:3]
            edges[1, 3 * at : 3 * at + 3, :] = plane[29:32]
            cells[32 * at : 32 * at + 32, :] = plane.astype(bf16)


def pair_kernel(block, other, out):
    for n in range(4):
        out[n, 128:256, :] = other[...]


def toeplitz_kernel(kernel_x, kernel_y, kernel_z, mixing, strip_hbm, kx_out, wz_out, kyp, strip, sems):
    gx, gz = lax.axis_index("gx"), lax.axis_index("gz")
    kyp[...] = jnp.zeros_like(kyp)
    kyp[:, 0:2048] = kernel_y[...].astype(f32)

    def send(r):
        return pltpu.make_async_copy(strip.at[r], strip_hbm.at[r], sems.at[r])

    def one(r, carry):
        row = jnp.broadcast_to(kyp[pl.ds(r, 1), :], (128, 2176))
        strip[pl.ds(r, 1)] = pltpu.roll(row, 0, 1, stride=1, stride_axis=0).astype(bf16)[None]
        send(r).start()
        return carry

    lax.fori_loop(0, 8, one, 0)
    mirror = one_hot(iota((256, 256), 0) + iota((256, 256), 1) == 255)
    kxr = dot(kernel_x[...], mirror)
    row, col = iota((64, 32), 0), iota((64, 32), 1)
    level = 2 * (row // 8) + jnp.where(row % 8 >= 3, 1, 0) + 16 - 2 * gz
    row, col8 = iota((8, 64), 0), iota((8, 64), 1)
    total = jnp.zeros((64, 64), f32)
    for zl in range(2):
        per_rank = dot(one_hot(col == level - zl), kernel_z[...], ((1,), (1,)))
        total = total + dot(per_rank.astype(bf16), one_hot((col8 // 8 == row) & (col8 % 8 < 6) & (col8 % 2 == zl)))
    row, col = iota((64, 64), 0), iota((64, 64), 1)
    i_of = jnp.where(row % 8 < 6, row % 8 % 3, 3)
    rj_of = col // 2
    mix = jnp.zeros((64, 64), f32)
    for i in range(3):
        line = jnp.zeros((1, 64), f32)
        for r in range(8):
            for j in range(3):
                line = jnp.where(rj_of[0:1] == r * 4 + j, mixing[i, j, r], line)
        mix = jnp.where(i_of == i, line, mix)
    w = mix * total
    hi = w.astype(bf16)
    rest = w - hi.astype(f32)
    mid = rest.astype(bf16)
    wz_out[:, 0:64] = hi
    wz_out[:, 64:128] = mid
    wz_out[:, 128:192] = (rest - mid.astype(f32)).astype(bf16)

    lane = iota((24, 256), 1)
    for r in range(8):
        row = pltpu.roll(jnp.broadcast_to(kxr[r : r + 1, :], (24, 256)), 0, 1, stride=1, stride_axis=0)
        total = jnp.zeros((24, 256), f32)
        for l in range(8):
            block = 2 * (l % 4) + ((gx & 1) if l < 4 else 1 - (gx & 1))
            shift = (16 * l + 16 * (gx - block) + 128 + 512) & 255
            total = jnp.where(lane // 16 == l, pltpu.roll(row, shift, 1), total)
        kx_out[r * 24 : (r + 1) * 24, :] = total[:, :128]
    for r in range(8):
        send(r).wait()


def faces_kernel(gathered, edges, pay, face_a, rim, low, high):
    gx, gy = lax.axis_index("gx"), lax.axis_index("gy")
    y = gy & 3

    def faces(n, row):
        rows = gathered[n, row : row + 32, :].astype(f32)
        return jnp.concatenate([rows[8 * q : 8 * (q + 1)] for q in range(4)], axis=1)

    right = jnp.where(gy == 3, faces(0, 224), faces(jnp.minimum(y + 1, 3), 96))
    left = jnp.where(gy == 4, faces(3, 224), faces(jnp.maximum(y - 1, 0), 96))
    sel = jnp.where(iota((8, 512), 0) < 4, right, left)
    k, lane = iota((8, 128), 0), iota((8, 128), 1)
    put = one_hot(((k < 3) & (lane == k)) | ((k >= 4) & (k < 7) & (lane == 121 + k)))
    unpacked = dot(sel.astype(bf16), put, ((0,), (0,)))
    rim[...] = unpacked.astype(bf16)
    for n in range(16):
        low[3 * n : 3 * n + 3] = unpacked[32 * n : 32 * n + 3]
        high[3 * n : 3 * n + 3] = unpacked[32 * n + 29 : 32 * n + 32]
    odd = (gx & 1) == 1
    to_b = [jnp.where(odd, edges[1], edges[0]).astype(bf16), jnp.where(odd, high[...], low[...]).astype(bf16)]
    to_a = [jnp.where(odd, edges[0], edges[1]).astype(bf16), jnp.where(odd, low[...], high[...]).astype(bf16)]
    face_a[0:48, :] = to_a[0][:, :128]
    face_a[48:96, :] = to_a[0][:, 128:]
    face_a[96:144, :] = to_a[1]
    for n in range(4):
        for k in range(4):
            pay[n, k * 96 : (k + 1) * 96, :] = gathered[k, 0:96, :]
            pay[n, (k + 4) * 96 : (k + 5) * 96, :] = gathered[k, 128:224, :]
        pay[n, 768:816, :] = to_b[0][:, :128]
        pay[n, 816:864, :] = to_b[0][:, 128:]
        pay[n, 864:912, :] = to_b[1]


def rims_kernel(cells, rim, near, rc, low_out, high_out, scr, fa, fb):
    gx = lax.axis_index("gx")
    even = (gx & 1) == 0
    chip = gx // 2
    a = near[...].astype(f32)
    b = rc[jnp.where(even, jnp.maximum(chip - 1, 0), jnp.minimum(chip + 1, 3)), 768:912, :].astype(f32)
    fa[...] = jnp.where(even, a, b)
    fb[...] = jnp.where(even, b, a)
    scr[2, 640:672, :] = jnp.zeros((32, 128), f32)
    for z in range(4):
        for c in range(4):
            plane, top, at = (c * 4 + z) * 32, (z * 4 + c) * 40, (c * 4 + z) * 3
            for q in range(3):
                if q < 2:
                    scr[q, top : top + 32] = cells[plane : plane + 32, q * 128 : (q + 1) * 128].astype(f32)
                else:
                    scr[q, top : top + 32] = rim[plane : plane + 32, :].astype(f32)
                scr[q, top + 32 : top + 40] = jnp.zeros((8, 128), f32)
                scr[q, top + 32 : top + 35] = fa[q * 48 + at : q * 48 + at + 3, :]
                scr[q, top + 37 : top + 40] = fb[q * 48 + at : q * 48 + at + 3, :]
    for out, first in ((low_out, 0), (high_out, 160)):
        for q in range(2):
            out[q * 480 : (q + 1) * 480, :] = scr[q, first : first + 480].astype(bf16)
        ends = dot(rim_lanes(), scr[2, first : first + 512].astype(bf16), ((1,), (1,)))
        ends = jnp.concatenate([ends[:, 128 * n : 128 * (n + 1)] for n in range(4)], axis=0)
        out[960:992, :] = ends.astype(bf16)


def rim_lanes():
    k, lane = iota((8, 128), 0), iota((8, 128), 1)
    return one_hot(((k < 3) & (lane == k)) | ((k >= 4) & (k < 7) & (lane == 121 + k)))


def unpack_rims(ref):
    ends = ref[960:992, :].astype(f32)
    ends = jnp.concatenate([ends[8 * n : 8 * (n + 1)] for n in range(4)], axis=1)
    ends = dot(ends.astype(bf16), rim_lanes(), ((0,), (0,)))
    return [ref[0:480, :].astype(f32), ref[480:960, :].astype(f32), ends]


def stages_kernel(own, rc, kx, strip_hbm, wz, packed, ax, ay, out, strip, sem):
    gy = lax.axis_index("gy")
    kxm = kx[...].astype(bf16)
    fetch = pltpu.make_async_copy(strip_hbm, strip, sem)
    fetch.start()

    def x_stage(kp, carry):
        for pair in range(3):
            res = []
            for jz in range(2):
                halves = []
                for half in range(2):
                    at = pl.multiple_of(((2 * kp + half) * 6 + 2 * pair + jz) * 16, 16)
                    parts = [ref[n, pl.ds(at, 16), :] for ref in (own, rc) for n in range(4)]
                    halves.append(jnp.concatenate(parts, axis=0))
                res.append(dot(kxm, jnp.concatenate(halves, axis=1)))
            for r in range(8):
                both = jnp.concatenate([res[0][r * 24 : (r + 1) * 24], res[1][r * 24 : (r + 1) * 24]], axis=0)
                ax[r, pair * 48 : pair * 48 + 48, pl.ds(pl.multiple_of(kp * 256, 256), 256)] = both.astype(bf16)
        return carry

    lax.fori_loop(0, 4, x_stage, 0)
    for r in range(8):
        for half in range(2):
            ay[r, half, 144:192, :] = jnp.zeros((48, 128), f32)
    fetch.wait()

    first_half = iota((128, 128), 1) < 64

    def y_stage(r, carry):
        acc = jnp.zeros((144, 256), f32)
        for kp in range(4):
            tiles = []
            for k in (2 * kp, 2 * kp + 1):
                block = (gy & 4) + k if k < 4 else k - (gy & 4)
                at = pl.multiple_of(128 * (8 + gy - block), 128)
                after, before = strip[r, :, pl.ds(at + 128, 128)], strip[r, :, pl.ds(at - 128, 128)]
                ends = jnp.where(first_half, after, before)
                tiles.append(jnp.concatenate([strip[r, :, pl.ds(at, 128)], ends], axis=1))
            acc = acc + dot(ax[r, :, kp * 256 : (kp + 1) * 256], jnp.concatenate(tiles, axis=0))
        for half in range(2):
            ay[r, half, 0:144, :] = acc[:, 128 * half : 128 * half + 128]
        return carry

    lax.fori_loop(0, 8, y_stage, 0, unroll=2)
    w = wz[...]
    lane = iota((64, 128), 1)
    rims = jnp.zeros((64, 128), f32)
    for a in range(18):
        halves = [
            jnp.concatenate([ay[r, half, pl.ds(a, 8, stride=24), :] for r in range(8)], axis=0).astype(bf16)
            for half in range(2)
        ]
        col = jnp.concatenate(halves, axis=1)
        o = dot(w, jnp.concatenate([col, col, col], axis=0))
        rims = jnp.where(lane // 2 == a, pltpu.roll(o[:, 128:], 2 * a + 1, 1), rims)
        for d in range(8):
            out[d, a * 6 : a * 6 + 6, :] = o[d * 8 : d * 8 + 6, :128]
    for d in range(8):
        out[d, 108:114, :] = rims[d * 8 : d * 8 + 6]
        values = out[d, 0:114, :]
        peak = jnp.max(jnp.abs(values), axis=0, keepdims=True)
        code = jnp.ceil(16.0 * jnp.log2(jnp.maximum(peak, 1e-30)))
        scaled = values * (SCALE * jnp.exp2(code * -0.0625))
        scaled = jnp.concatenate([scaled, jnp.broadcast_to(code, (6, 128))], axis=0)
        packed[d] = jnp.round(scaled).astype(i32).astype(jnp.int16)


def sum_kernel(parts, out):
    total = jnp.zeros((114, 128), f32)
    for d in range(8):
        values = parts[d].astype(i32).astype(f32)
        total = total + values[0:114] * (jnp.exp2(values[114:115] * 0.0625) * (1.0 / SCALE))
    out[0:114] = total
    out[114:120] = jnp.zeros((6, 128), f32)


def weights_kernel(mag, own_low, own_high, z_low, z_high, stiff, sat, near, far_hbm, fields, aa, sems):
    m0, _, wx, wy, wz, ss = parts_of(fields)
    gx, gy, gz = (lax.axis_index(n) for n in ("gx", "gy", "gz"))
    row, col = iota((40, 384), 0), iota((40, 384), 1)
    inside = ((row < 32) | ((row < 36) & (gx < 7)) | ((row >= 36) & (gx > 0))) & (
        (col < 256) | ((col < 320) & (gy < 7)) | ((col >= 320) & (gy > 0))
    )
    unpacked = [unpack_rims(ref) for ref in (z_low, own_low, own_high, z_high)]
    for p in range(10):
        z = p - 3
        if z < 0:
            chunks, at, ok = unpacked[0], p * 4, gz > 0
        elif z > 3:
            chunks, at, ok = unpacked[3], (z - 4) * 4, gz < 7
        elif z < 3:
            chunks, at, ok = unpacked[1], z * 4, gz >= 0
        else:
            chunks, at, ok = unpacked[2], 8, gz >= 0
        whole = [jnp.concatenate([v[40 * (at + c) : 40 * (at + c) + 40] for v in chunks], axis=1) for c in range(4)]
        for c in range(3):
            m0[c, p] = whole[c]
            if 0 <= z < 4:
                m0[c, p, 0:32, 0:256] = mag[c, z]
        ids = whole[3].astype(i32)
        aa[p] = jnp.where(inside & ok, lookup(ids, stiff), 0.0)
        ss[p] = (2.0 * TIME_STEP) / lookup(ids, sat)

    def weight(u, v):
        den = u + v
        return 2.0 * u * v / jnp.where(den > 0.0, den, 1.0)

    for p in range(10):
        here = aa[p]
        if 1 <= p <= 8:
            wx[p] = weight(here, pltpu.roll(here, 39, 0))
            wy[p] = weight(here, pltpu.roll(here, 383, 1))
        if p < 9:
            wz[p] = weight(here, aa[p + 1])

    copies = [pltpu.make_async_copy(fields.at[a], far_hbm.at[b], sems.at[n]) for n, (a, b) in enumerate(FAR)]
    for copy in copies:
        copy.start()
    fz = [wz[0] * (m0[c, 1] - m0[c, 0]) for c in range(3)]
    for p in range(1, 9):
        for c in range(3):
            total, fz[c] = exchange(m0, wx, wy, wz, c, p, fz[c])
            near[24 + c * 8 + p - 1] = total * ss[p]
            near[c * 8 + p - 1] = m0[c, p]
    for copy in copies:
        copy.wait()


def exchange(src, wx, wy, wz, c, p, below):
    m = src[c, p]
    flux = wx[p] * (pltpu.roll(m, 39, 0) - m)
    total = flux - pltpu.roll(flux, 1, 0)
    flux = wy[p] * (pltpu.roll(m, 383, 1) - m)
    total = total + (flux - pltpu.roll(flux, 1, 1))
    up = wz[p] * (src[c, p + 1] - m)
    return total + (up - below), up


def substeps_kernel(
    near, far_hbm, d_own, d_low, d_high, state_out, demag_out, far, m1, m2, fz, field, rows, sem
):
    m0, hh = Planes(near, -1, 8), Planes(near, 24, 8)
    wx, wy, wz, ss = (Planes(far, base) for base in (-2, 4, 11, 17))
    fetch = pltpu.make_async_copy(far_hbm, far, sem)
    fetch.start()
    for q in range(6):
        demag_out[q // 3, q % 3] = d_own[pl.ds(6 + q, 16, stride=6), :]
    lane24, row24 = iota((24, 128), 1), iota((24, 128), 0)
    coarse_x = jnp.where(row24 == 17, 0, row24 + 1)
    sources = [(d_low, 3), (d_own, 0), (d_own, 3), (d_high, 0)]
    for level in range(4):
        ref, first = sources[level]
        for i in range(3):
            top, q = (level * 3 + i) * 24, first + i
            rows[top : top + 16, 0:128] = ref[pl.ds(6 + q, 16, stride=6), :]
            ends = jnp.where(row24[0:8] == 0, ref[102 + q : 103 + q, :], ref[q : q + 1, :])
            rows[top + 16 : top + 24, 0:128] = ends
            rim = jnp.broadcast_to(ref[108 + q : 109 + q, :], (24, 128))
            rows[top : top + 24, 128:256] = jnp.where(lane24 // 2 == coarse_x, rim, 0.0)
    x = rows[...]
    hi = x.astype(bf16)
    lo = (x - hi.astype(f32)).astype(bf16)
    a, b = iota((256, 256), 0) % 128, iota((256, 256), 1)
    wide = one_hot(b // 2 == a)
    a, b = iota((256, 128), 0) % 128, iota((256, 128), 1)
    ends = one_hot(((a % 2 == 1) & (b < 2)) | ((a % 2 == 0) & (b >= 126)))
    block = dot(jnp.concatenate([hi[:, :128], lo[:, :128]], axis=1), wide) * TIME_STEP
    sides = dot(jnp.concatenate([hi[:, 128:], lo[:, 128:]], axis=1), ends) * TIME_STEP
    row8 = iota((8, 128), 0)
    for g in range(12):
        for q in range(3):
            v = block[g * 24 : (g + 1) * 24, q * 128 : (q + 1) * 128] if q < 2 else sides[g * 24 : (g + 1) * 24]
            field[g, q, pl.ds(0, 16, stride=2), :] = v[0:16]
            field[g, q, pl.ds(1, 16, stride=2), :] = v[0:16]
            field[g, q, 32:40, :] = jnp.where(row8 < 2, v[16:17], jnp.where(row8 >= 6, v[17:18], 0.0))
    for step in range(3):
        src, dst = ((m0, m1), (m1, m2), (m2, None))[step]
        if step == 1:
            fetch.wait()
        first, last = step + 1, 8 - step

        def plane(p, carry):
            m = [src[c, p] for c in range(3)]
            level = (p - 1) // 2
            h = []
            for c in range(3):
                if step == 0:
                    total = hh[c, p - 1]
                else:
                    total, up = exchange(src, wx, wy, wz, c, p, fz[c])
                    fz[c] = up
                    total = total * ss[p]
                h.append(total + jnp.concatenate([field[level * 3 + c, q] for q in range(3)], axis=1))
            t = [m[1] * h[2] - m[2] * h[1], m[2] * h[0] - m[0] * h[2], m[0] * h[1] - m[1] * h[0]]
            u = [m[1] * t[2] - m[2] * t[1], m[2] * t[0] - m[0] * t[2], m[0] * t[1] - m[1] * t[0]]
            raw = [m[c] - (t[c] + DAMPING * u[c]) for c in range(3)]
            scale = lax.rsqrt(jnp.maximum(raw[0] * raw[0] + raw[1] * raw[1] + raw[2] * raw[2], 1e-30))
            for c in range(3):
                if step < 2:
                    dst[c, p] = raw[c] * scale
                else:
                    state_out[c, p - 3] = (raw[c] * scale)[0:32, 0:256]
            return carry

        if step:
            for c in range(3):
                fz[c] = wz[first - 1] * (src[c, first] - src[c, first - 1])
        lax.fori_loop(first, last + 1, plane, 0)


def swap(value, axis, bit):
    return lax.ppermute(value, axis, [(i, i ^ bit) for i in range(8)])


def step(magnet, grains, stiffness_table, saturation_table, kernel_x, kernel_y, kernel_z, mixing):
    shape = jax.ShapeDtypeStruct
    up = [(i, i + 1) for i in range(7)]
    down = [(i + 1, i) for i in range(7)]
    big = (10, 40, 384)
    (pay,) = call(
        coarse_kernel,
        shape((128, 128), bf16),
        [VM, VM, SM],
        [pltpu.VMEM((6, 32, 256), f32)],
        20_000_000,
        600_000,
    )(magnet, grains, saturation_table)
    other = swap(pay, "gy", 4)
    edges, cells, block = call(
        block_kernel,
        [shape((2, 48, 256), f32), shape((512, 256), bf16), shape((4, 256, 128), bf16)],
        [VM] * 3,
        (),
        1_000_000,
        1_500_000,
        16 << 20,
    )(magnet, grains, pay)
    strip, kx, wz = call(
        toeplitz_kernel,
        [shape((8, 128, 2176), bf16), shape((192, 128), f32), shape((64, 192), bf16)],
        [VM, VM, VM, SM],
        [pltpu.VMEM((8, 2176), f32), pltpu.VMEM((8, 128, 2176), bf16), pltpu.SemaphoreType.DMA((8,))],
        20_000_000,
        5_000_000,
        FULL - 14_000_000,
        [HB, VM, VM],
    )(kernel_x, kernel_y, kernel_z, mixing.transpose(1, 2, 0))
    (pay,) = call(pair_kernel, shape((4, 256, 128), bf16), [VM] * 2, (), 1000, 400_000, 8 << 20, None, {0: 0})(block, other)
    groups = [[0, 1, 2, 3], [4, 5, 6, 7]]
    gathered = lax.all_to_all(pay, "gy", 0, 0, tiled=True, axis_index_groups=groups)
    pay, face_a, rim = call(
        faces_kernel,
        [shape((4, 912, 128), bf16), shape((144, 128), bf16), shape((512, 128), bf16)],
        [VM] * 2,
        [pltpu.VMEM((48, 128), f32)] * 2,
        1_000_000,
        1_000_000,
        8 << 20,
    )(gathered, edges)
    groups = [[0, 2, 4, 6], [1, 3, 5, 7]]
    gathered = lax.all_to_all(pay, "gx", 0, 0, tiled=True, axis_index_groups=groups)
    near = swap(face_a, "gx", 1)
    rc = swap(gathered, "gx", 1)
    own_low, own_high = call(
        rims_kernel,
        [shape((992, 128), bf16)] * 2,
        [VM] * 4,
        [pltpu.VMEM((3, 672, 128), f32), pltpu.VMEM((144, 128), f32), pltpu.VMEM((144, 128), f32)],
        1_000_000,
        2_000_000,
        12 << 20,
    )(cells, rim, near, rc)
    z_low = lax.ppermute(own_high, "gz", up)
    z_high = lax.ppermute(own_low, "gz", down)
    (parts,) = call(
        stages_kernel,
        shape((8, 120, 128), jnp.int16),
        [VM, VM, VM, HB, VM],
        [pltpu.VMEM((8, 144, 1024), bf16), pltpu.VMEM((8, 2, 192, 128), f32), pltpu.VMEM((8, 120, 128), f32)]
        + [pltpu.VMEM((8, 128, 2176), bf16), pltpu.SemaphoreType.DMA],
        2_000_000_000,
        10_000_000,
        FULL - (16 << 20),
    )(gathered, rc, kx, strip, wz)
    parts = lax.all_to_all(parts, "gz", 0, 0, tiled=True)
    near_fields, far_fields = call(
        weights_kernel,
        [shape((48, 40, 384), f32), shape((25, 40, 384), f32)],
        [VM] * 5 + [SM] * 2,
        [pltpu.VMEM((94, 40, 384), f32), pltpu.VMEM(big, f32), pltpu.SemaphoreType.DMA((4,))],
        20_000_000,
        5_000_000,
        FULL - 15_000_000,
        [VM, HB],
    )(magnet, own_low, own_high, z_low, z_high, stiffness_table, saturation_table)
    (d_own,) = call(sum_kernel, shape((120, 128), f32), [VM], (), 100_000, 300_000, 8 << 20)(parts)
    d_low = lax.ppermute(d_own, "gz", up)
    d_high = lax.ppermute(d_own, "gz", down)
    state, demag = call(
        substeps_kernel,
        [shape((3, 4, 32, 256), f32), shape((2, 3, 16, 128), f32)],
        [VM, HB] + [VM] * 3,
        [pltpu.VMEM((25, 40, 384), f32)]
        + [pltpu.VMEM((3,) + big, f32)] * 2
        + [pltpu.VMEM((3, 40, 384), f32), pltpu.VMEM((12, 3, 40, 128), f32)]
        + [pltpu.VMEM((288, 256), f32), pltpu.SemaphoreType.DMA],
        50_000_000,
        5_000_000,
        FULL - 15_000_000,
    )(near_fields, far_fields, d_own, d_low, d_high)
    return (state, demag)


def solution(mesh):
    in_specs = (P(None, "gz", "gx", "gy"), P("gz", "gx", "gy"), P(), P(), P(), P(), P(), P())
    out_specs = (P(None, "gz", "gx", "gy"), P("gz", None, "gx", "gy"))
    return jax.shard_map(step, mesh=mesh, in_specs=in_specs, out_specs=out_specs, check_vma=False)
```

```python
import jax
import jax.numpy as jnp
from jax import lax
from jax.experimental import pallas as pl
from jax.experimental.pallas import tpu as pltpu
from jax.sharding import PartitionSpec as P


f32, bf16, i32 = jnp.float32, jnp.bfloat16, jnp.int32
VM = pl.BlockSpec(memory_space=pltpu.VMEM)
SM = pl.BlockSpec(memory_space=pltpu.SMEM)
HB = pl.BlockSpec(memory_space=pltpu.MemorySpace.HBM)
TIME_STEP = 0.02
DAMPING = 0.3
SCALE = 32000.0
FULL = 67_043_328


def iota(shape, dim):
    return lax.broadcasted_iota(i32, shape, dim)


def one_hot(condition):
    return jnp.where(condition, 1.0, 0.0).astype(bf16)


def dot(a, b, dims=((1,), (0,))):
    return lax.dot_general(a, b, (dims, ((), ())), preferred_element_type=f32)


class Planes:
    def __init__(self, ref, base, inner=0):
        self.ref, self.base, self.inner = ref, base, inner

    def key(self, k):
        k = k if isinstance(k, tuple) else (k,)
        if self.inner:
            return (self.base + k[0] * self.inner + k[1],) + k[2:]
        return (self.base + k[0],) + k[1:]

    def __getitem__(self, k):
        return self.ref[self.key(k)]

    def __setitem__(self, k, value):
        self.ref[self.key(k)] = value


def parts_of(ref):
    layout = ((0, 10), (30, 8), (54, 0), (64, 0), (74, 0), (84, 0))
    return [Planes(ref, base, inner) for base, inner in layout]


def lookup(ids, table):
    bits = [(ids & (1 << k)) != 0 for k in range(4)]
    level = [table[k] for k in range(16)]
    for bit in bits:
        level = [jnp.where(bit, level[2 * k + 1], level[2 * k]) for k in range(len(level) // 2)]
    return level[0]


def call(body, out_shape, in_specs, scratch=(), flops=0, nbytes=0, vmem=None, alias={}):
    outs = out_shape if isinstance(out_shape, list) else [out_shape]
    result = pl.pallas_call(
        body,
        out_shape=outs,
        in_specs=in_specs,
        out_specs=[VM] * len(outs),
        scratch_shapes=list(scratch),
        input_output_aliases=alias,
        compiler_params=pltpu.CompilerParams(vmem_limit_bytes=vmem),
        cost_estimate=pl.CostEstimate(flops=flops, bytes_accessed=nbytes, transcendentals=0),
    )
    return result


def coarse_kernel(mag, grains, sat, out, scr):
    for a in range(2):
        s0 = lookup(grains[2 * a], sat)
        s1 = lookup(grains[2 * a + 1], sat)
        for j in range(3):
            scr[j * 2 + a] = s0 * mag[j, 2 * a] + s1 * mag[j, 2 * a + 1]
    pick = one_hot(iota((256, 128), 0) == 2 * iota((256, 128), 1))
    rows = []
    for p in range(6):
        s = scr[p].reshape(16, 2, 256)
        s = s[:, 0, :] + s[:, 1, :]
        s = s + pltpu.roll(s, 255, 1)
        rows.append((s * 0.125).astype(bf16))
    coarse = dot(jnp.concatenate(rows, axis=0), pick).astype(bf16)
    cells = [mag[j].reshape(128, 256).astype(bf16) for j in range(3)]
    cells.append(grains[...].reshape(128, 256).astype(f32).astype(bf16))
    cells = jnp.concatenate(cells, axis=0)
    k, lane = iota((8, 256), 0), iota((8, 256), 1)
    edge = one_hot(((k < 3) & (lane == k)) | ((k >= 4) & (k < 7) & (lane == 249 + k)))
    faces = dot(edge, cells, ((1,), (1,)))
    faces = jnp.concatenate([faces[:, 128 * q : 128 * (q + 1)] for q in range(4)], axis=0).astype(bf16)
    out[0:96, :] = coarse
    out[96:128, :] = faces


def block_kernel(mag, grains, own, edges, cells, out):
    for n in range(4):
        out[n, 0:128, :] = own[...]
        out[n, 128:256, :] = own[...]
    for c in range(4):
        for z in range(4):
            at = c * 4 + z
            plane = mag[c, z] if c < 3 else grains[z].astype(f32)
            edges[0, 3 * at : 3 * at + 3, :] = plane[0:3]
            edges[1, 3 * at : 3 * at + 3, :] = plane[29:32]
            cells[32 * at : 32 * at + 32, :] = plane.astype(bf16)


def pair_kernel(block, other, out):
    for n in range(4):
        out[n, 128:256, :] = other[...]


def toeplitz_kernel(kernel_x, kernel_y, kernel_z, mixing, strip, kx_out, wz_out, kyp):
    gx, gz = lax.axis_index("gx"), lax.axis_index("gz")
    kyp[...] = jnp.zeros_like(kyp)
    kyp[:, 0:2048] = kernel_y[...].astype(f32)
    mirror = one_hot(iota((256, 256), 0) + iota((256, 256), 1) == 255)
    kxr = dot(kernel_x[...], mirror)
    row, col = iota((64, 32), 0), iota((64, 32), 1)
    level = 2 * (row // 8) + jnp.where(row % 8 >= 3, 1, 0) + 16 - 2 * gz
    row, col8 = iota((8, 64), 0), iota((8, 64), 1)
    total = jnp.zeros((64, 64), f32)
    for zl in range(2):
        per_rank = dot(one_hot(col == level - zl), kernel_z[...], ((1,), (1,)))
        total = total + dot(per_rank.astype(bf16), one_hot((col8 // 8 == row) & (col8 % 8 < 6) & (col8 % 2 == zl)))
    row, col = iota((64, 64), 0), iota((64, 64), 1)
    i_of = jnp.where(row % 8 < 6, row % 8 % 3, 3)
    rj_of = col // 2
    mix = jnp.zeros((64, 64), f32)
    for i in range(3):
        line = jnp.zeros((1, 64), f32)
        for r in range(8):
            for j in range(3):
                line = jnp.where(rj_of[0:1] == r * 4 + j, mixing[i, j, r], line)
        mix = jnp.where(i_of == i, line, mix)
    w = mix * total
    hi = w.astype(bf16)
    rest = w - hi.astype(f32)
    mid = rest.astype(bf16)
    wz_out[:, 0:64] = hi
    wz_out[:, 64:128] = mid
    wz_out[:, 128:192] = (rest - mid.astype(f32)).astype(bf16)

    def one(r, carry):
        row = jnp.broadcast_to(kyp[pl.ds(r, 1), :], (128, 2176))
        strip[pl.ds(r, 1)] = pltpu.roll(row, 0, 1, stride=1, stride_axis=0).astype(bf16)[None]
        return carry

    lax.fori_loop(0, 8, one, 0)
    lane = iota((24, 256), 1)
    for r in range(8):
        row = pltpu.roll(jnp.broadcast_to(kxr[r : r + 1, :], (24, 256)), 0, 1, stride=1, stride_axis=0)
        total = jnp.zeros((24, 256), f32)
        for l in range(8):
            block = 2 * (l % 4) + ((gx & 1) if l < 4 else 1 - (gx & 1))
            shift = (16 * l + 16 * (gx - block) + 128 + 512) & 255
            total = jnp.where(lane // 16 == l, pltpu.roll(row, shift, 1), total)
        kx_out[r * 24 : (r + 1) * 24, :] = total[:, :128]


def faces_kernel(gathered, edges, pay, face_a, rim, low, high):
    gx, gy = lax.axis_index("gx"), lax.axis_index("gy")
    y = gy & 3

    def faces(n, row):
        rows = gathered[n, row : row + 32, :].astype(f32)
        return jnp.concatenate([rows[8 * q : 8 * (q + 1)] for q in range(4)], axis=1)

    right = jnp.where(gy == 3, faces(0, 224), faces(jnp.minimum(y + 1, 3), 96))
    left = jnp.where(gy == 4, faces(3, 224), faces(jnp.maximum(y - 1, 0), 96))
    sel = jnp.where(iota((8, 512), 0) < 4, right, left)
    k, lane = iota((8, 128), 0), iota((8, 128), 1)
    put = one_hot(((k < 3) & (lane == k)) | ((k >= 4) & (k < 7) & (lane == 121 + k)))
    unpacked = dot(sel.astype(bf16), put, ((0,), (0,)))
    rim[...] = unpacked.astype(bf16)
    for n in range(16):
        low[3 * n : 3 * n + 3] = unpacked[32 * n : 32 * n + 3]
        high[3 * n : 3 * n + 3] = unpacked[32 * n + 29 : 32 * n + 32]
    odd = (gx & 1) == 1
    to_b = [jnp.where(odd, edges[1], edges[0]).astype(bf16), jnp.where(odd, high[...], low[...]).astype(bf16)]
    to_a = [jnp.where(odd, edges[0], edges[1]).astype(bf16), jnp.where(odd, low[...], high[...]).astype(bf16)]
    face_a[0:48, :] = to_a[0][:, :128]
    face_a[48:96, :] = to_a[0][:, 128:]
    face_a[96:144, :] = to_a[1]
    for n in range(4):
        for k in range(4):
            pay[n, k * 96 : (k + 1) * 96, :] = gathered[k, 0:96, :]
            pay[n, (k + 4) * 96 : (k + 5) * 96, :] = gathered[k, 128:224, :]
        pay[n, 768:816, :] = to_b[0][:, :128]
        pay[n, 816:864, :] = to_b[0][:, 128:]
        pay[n, 864:912, :] = to_b[1]


def rims_kernel(cells, rim, near, rc, low_out, high_out, scr, fa, fb):
    gx = lax.axis_index("gx")
    even = (gx & 1) == 0
    chip = gx // 2
    a = near[...].astype(f32)
    b = rc[jnp.where(even, jnp.maximum(chip - 1, 0), jnp.minimum(chip + 1, 3)), 768:912, :].astype(f32)
    fa[...] = jnp.where(even, a, b)
    fb[...] = jnp.where(even, b, a)
    for z in range(4):
        for c in range(4):
            plane = (c * 4 + z) * 32
            scr[0:32, 0:256] = cells[plane : plane + 32, :].astype(f32)
            scr[0:32, 256:384] = rim[plane : plane + 32, :].astype(f32)
            scr[32:40, :] = jnp.zeros((8, 384), f32)
            for q in range(3):
                at = q * 48 + (c * 4 + z) * 3
                scr[32:35, q * 128 : (q + 1) * 128] = fa[at : at + 3, :]
                scr[37:40, q * 128 : (q + 1) * 128] = fb[at : at + 3, :]
            whole = scr[...].astype(bf16)
            if z < 3:
                low_out[z * 4 + c] = whole
            if z > 0:
                high_out[(z - 1) * 4 + c] = whole


def stages_kernel(own, rc, kx, strip_hbm, wz, packed, ax, ay, out, strip, sem):
    gy = lax.axis_index("gy")
    kxm = kx[...].astype(bf16)
    fetch = pltpu.make_async_copy(strip_hbm, strip, sem)
    fetch.start()

    def x_stage(kp, carry):
        for pair in range(3):
            res = []
            for jz in range(2):
                halves = []
                for half in range(2):
                    at = pl.multiple_of(((2 * kp + half) * 6 + 2 * pair + jz) * 16, 16)
                    parts = [ref[n, pl.ds(at, 16), :] for ref in (own, rc) for n in range(4)]
                    halves.append(jnp.concatenate(parts, axis=0))
                res.append(dot(kxm, jnp.concatenate(halves, axis=1)))
            for r in range(8):
                both = jnp.concatenate([res[0][r * 24 : (r + 1) * 24], res[1][r * 24 : (r + 1) * 24]], axis=0)
                ax[r, pair * 48 : pair * 48 + 48, pl.ds(pl.multiple_of(kp * 256, 256), 256)] = both.astype(bf16)
        return carry

    lax.fori_loop(0, 4, x_stage, 0)
    for r in range(8):
        for half in range(2):
            ay[r, half, 144:192, :] = jnp.zeros((48, 128), f32)
    fetch.wait()

    first_half = iota((128, 128), 1) < 64

    def y_stage(r, carry):
        acc = jnp.zeros((144, 256), f32)
        for kp in range(4):
            tiles = []
            for k in (2 * kp, 2 * kp + 1):
                block = (gy & 4) + k if k < 4 else k - (gy & 4)
                at = pl.multiple_of(128 * (8 + gy - block), 128)
                after, before = strip[r, :, pl.ds(at + 128, 128)], strip[r, :, pl.ds(at - 128, 128)]
                ends = jnp.where(first_half, after, before)
                tiles.append(jnp.concatenate([strip[r, :, pl.ds(at, 128)], ends], axis=1))
            acc = acc + dot(ax[r, :, kp * 256 : (kp + 1) * 256], jnp.concatenate(tiles, axis=0))
        for half in range(2):
            ay[r, half, 0:144, :] = acc[:, 128 * half : 128 * half + 128]
        return carry

    lax.fori_loop(0, 8, y_stage, 0, unroll=2)
    w = wz[...]
    lane = iota((64, 128), 1)
    rims = jnp.zeros((64, 128), f32)
    for a in range(18):
        halves = [
            jnp.concatenate([ay[r, half, pl.ds(a, 8, stride=24), :] for r in range(8)], axis=0).astype(bf16)
            for half in range(2)
        ]
        col = jnp.concatenate(halves, axis=1)
        o = dot(w, jnp.concatenate([col, col, col], axis=0))
        rims = jnp.where(lane // 2 == a, pltpu.roll(o[:, 128:], 2 * a + 1, 1), rims)
        for d in range(8):
            out[d, a * 6 : a * 6 + 6, :] = o[d * 8 : d * 8 + 6, :128]
    for d in range(8):
        out[d, 108:114, :] = rims[d * 8 : d * 8 + 6]
        values = out[d, 0:114, :]
        peak = jnp.max(jnp.abs(values), axis=0, keepdims=True)
        code = jnp.ceil(16.0 * jnp.log2(jnp.maximum(peak, 1e-30)))
        scaled = values * (SCALE * jnp.exp2(code * -0.0625))
        scaled = jnp.concatenate([scaled, jnp.broadcast_to(code, (6, 128))], axis=0)
        packed[d] = jnp.round(scaled).astype(i32).astype(jnp.int16)


def sum_kernel(parts, out):
    total = jnp.zeros((114, 128), f32)
    for d in range(8):
        values = parts[d].astype(i32).astype(f32)
        total = total + values[0:114] * (jnp.exp2(values[114:115] * 0.0625) * (1.0 / SCALE))
    out[0:114] = total
    out[114:120] = jnp.zeros((6, 128), f32)


def weights_kernel(mag, own_low, own_high, z_low, z_high, stiff, sat, fields, aa):
    m0, hh, wx, wy, wz, ss = parts_of(fields)
    gx, gy, gz = (lax.axis_index(n) for n in ("gx", "gy", "gz"))
    row, col = iota((40, 384), 0), iota((40, 384), 1)
    inside = ((row < 32) | ((row < 36) & (gx < 7)) | ((row >= 36) & (gx > 0))) & (
        (col < 256) | ((col < 320) & (gy < 7)) | ((col >= 320) & (gy > 0))
    )
    for p in range(10):
        z = p - 3
        if z < 0:
            whole = [z_low[p * 4 + c].astype(f32) for c in range(4)]
            ok = gz > 0
        elif z > 3:
            whole = [z_high[(z - 4) * 4 + c].astype(f32) for c in range(4)]
            ok = gz < 7
        else:
            ref, at = (own_low, z * 4) if z < 3 else (own_high, 8)
            whole = [ref[at + c].astype(f32) for c in range(4)]
            ok = gz >= 0
        for c in range(3):
            m0[c, p] = whole[c]
            if 0 <= z < 4:
                m0[c, p, 0:32, 0:256] = mag[c, z]
        ids = whole[3].astype(i32)
        aa[p] = jnp.where(inside & ok, lookup(ids, stiff), 0.0)
        ss[p] = (2.0 * TIME_STEP) / lookup(ids, sat)

    def weight(u, v):
        den = u + v
        return 2.0 * u * v / jnp.where(den > 0.0, den, 1.0)

    for p in range(10):
        here = aa[p]
        if 1 <= p <= 8:
            wx[p] = weight(here, pltpu.roll(here, 39, 0))
            wy[p] = weight(here, pltpu.roll(here, 383, 1))
        if p < 9:
            wz[p] = weight(here, aa[p + 1])

    fz = [wz[0] * (m0[c, 1] - m0[c, 0]) for c in range(3)]
    for p in range(1, 9):
        for c in range(3):
            total, fz[c] = exchange(m0, wx, wy, wz, c, p, fz[c])
            hh[c, p - 1] = total * ss[p]


def exchange(src, wx, wy, wz, c, p, below):
    m = src[c, p]
    flux = wx[p] * (pltpu.roll(m, 39, 0) - m)
    total = flux - pltpu.roll(flux, 1, 0)
    flux = wy[p] * (pltpu.roll(m, 383, 1) - m)
    total = total + (flux - pltpu.roll(flux, 1, 1))
    up = wz[p] * (src[c, p + 1] - m)
    return total + (up - below), up


def substeps_kernel(
    fields_hbm, d_own, d_low, d_high, state_out, demag_out, fields, m1, m2, fz, field, rows, sems
):
    m0, hh, wx, wy, wz, ss = parts_of(fields)
    spans = ((1, 8), (11, 8), (21, 8), (30, 24), (56, 6), (66, 6), (75, 7), (86, 6))
    cuts = [pl.ds(first, count) for first, count in spans]
    fetches = [pltpu.make_async_copy(fields_hbm.at[c], fields.at[c], sems.at[n]) for n, c in enumerate(cuts)]
    for fetch in fetches:
        fetch.start()
    for q in range(6):
        demag_out[q // 3, q % 3] = d_own[pl.ds(6 + q, 16, stride=6), :]
    lane24, row24 = iota((24, 128), 1), iota((24, 128), 0)
    coarse_x = jnp.where(row24 == 17, 0, row24 + 1)
    sources = [(d_low, 3), (d_own, 0), (d_own, 3), (d_high, 0)]
    for level in range(4):
        ref, first = sources[level]
        for i in range(3):
            top, q = (level * 3 + i) * 24, first + i
            rows[top : top + 16, 0:128] = ref[pl.ds(6 + q, 16, stride=6), :]
            ends = jnp.where(row24[0:8] == 0, ref[102 + q : 103 + q, :], ref[q : q + 1, :])
            rows[top + 16 : top + 24, 0:128] = ends
            rim = jnp.broadcast_to(ref[108 + q : 109 + q, :], (24, 128))
            rows[top : top + 24, 128:256] = jnp.where(lane24 // 2 == coarse_x, rim, 0.0)
    x = rows[...]
    hi = x.astype(bf16)
    lo = (x - hi.astype(f32)).astype(bf16)
    a, b = iota((256, 256), 0) % 128, iota((256, 256), 1)
    wide = one_hot(b // 2 == a)
    a, b = iota((256, 128), 0) % 128, iota((256, 128), 1)
    ends = one_hot(((a % 2 == 1) & (b < 2)) | ((a % 2 == 0) & (b >= 126)))
    block = dot(jnp.concatenate([hi[:, :128], lo[:, :128]], axis=1), wide) * TIME_STEP
    sides = dot(jnp.concatenate([hi[:, 128:], lo[:, 128:]], axis=1), ends) * TIME_STEP
    row8 = iota((8, 128), 0)
    for g in range(12):
        for q in range(3):
            v = block[g * 24 : (g + 1) * 24, q * 128 : (q + 1) * 128] if q < 2 else sides[g * 24 : (g + 1) * 24]
            field[g, q, pl.ds(0, 16, stride=2), :] = v[0:16]
            field[g, q, pl.ds(1, 16, stride=2), :] = v[0:16]
            field[g, q, 32:40, :] = jnp.where(row8 < 2, v[16:17], jnp.where(row8 >= 6, v[17:18], 0.0))
    for step in range(3):
        src, dst = ((m0, m1), (m1, m2), (m2, None))[step]
        if step < 2:
            for fetch in (fetches[:4], fetches[4:])[step]:
                fetch.wait()
        first, last = step + 1, 8 - step

        def plane(p, carry):
            m = [src[c, p] for c in range(3)]
            level = (p - 1) // 2
            h = []
            for c in range(3):
                if step == 0:
                    total = hh[c, p - 1]
                else:
                    total, up = exchange(src, wx, wy, wz, c, p, fz[c])
                    fz[c] = up
                    total = total * ss[p]
                h.append(total + jnp.concatenate([field[level * 3 + c, q] for q in range(3)], axis=1))
            t = [m[1] * h[2] - m[2] * h[1], m[2] * h[0] - m[0] * h[2], m[0] * h[1] - m[1] * h[0]]
            u = [m[1] * t[2] - m[2] * t[1], m[2] * t[0] - m[0] * t[2], m[0] * t[1] - m[1] * t[0]]
            raw = [m[c] - (t[c] + DAMPING * u[c]) for c in range(3)]
            scale = lax.rsqrt(jnp.maximum(raw[0] * raw[0] + raw[1] * raw[1] + raw[2] * raw[2], 1e-30))
            for c in range(3):
                if step < 2:
                    dst[c, p] = raw[c] * scale
                else:
                    state_out[c, p - 3] = (raw[c] * scale)[0:32, 0:256]
            return carry

        if step:
            for c in range(3):
                fz[c] = wz[first - 1] * (src[c, first] - src[c, first - 1])
        lax.fori_loop(first, last + 1, plane, 0)


def swap(value, axis, bit):
    return lax.ppermute(value, axis, [(i, i ^ bit) for i in range(8)])


def step(magnet, grains, stiffness_table, saturation_table, kernel_x, kernel_y, kernel_z, mixing):
    shape = jax.ShapeDtypeStruct
    up = [(i, i + 1) for i in range(7)]
    down = [(i + 1, i) for i in range(7)]
    big = (10, 40, 384)
    (pay,) = call(
        coarse_kernel,
        shape((128, 128), bf16),
        [VM, VM, SM],
        [pltpu.VMEM((6, 32, 256), f32)],
        20_000_000,
        600_000,
    )(magnet, grains, saturation_table)
    other = swap(pay, "gy", 4)
    edges, cells, block = call(
        block_kernel,
        [shape((2, 48, 256), f32), shape((512, 256), bf16), shape((4, 256, 128), bf16)],
        [VM] * 3,
        (),
        1_000_000,
        1_500_000,
        16 << 20,
    )(magnet, grains, pay)
    strip, kx, wz = call(
        toeplitz_kernel,
        [shape((8, 128, 2176), bf16), shape((192, 128), f32), shape((64, 192), bf16)],
        [VM, VM, VM, SM],
        [pltpu.VMEM((8, 2176), f32)],
        20_000_000,
        5_000_000,
        FULL - 14_000_000,
    )(kernel_x, kernel_y, kernel_z, mixing.transpose(1, 2, 0))
    (pay,) = call(pair_kernel, shape((4, 256, 128), bf16), [VM] * 2, (), 1000, 400_000, 8 << 20, {0: 0})(block, other)
    groups = [[0, 1, 2, 3], [4, 5, 6, 7]]
    gathered = lax.all_to_all(pay, "gy", 0, 0, tiled=True, axis_index_groups=groups)
    pay, face_a, rim = call(
        faces_kernel,
        [shape((4, 912, 128), bf16), shape((144, 128), bf16), shape((512, 128), bf16)],
        [VM] * 2,
        [pltpu.VMEM((48, 128), f32)] * 2,
        1_000_000,
        1_000_000,
        8 << 20,
    )(gathered, edges)
    groups = [[0, 2, 4, 6], [1, 3, 5, 7]]
    gathered = lax.all_to_all(pay, "gx", 0, 0, tiled=True, axis_index_groups=groups)
    near = swap(face_a, "gx", 1)
    rc = swap(gathered, "gx", 1)
    own_low, own_high = call(
        rims_kernel,
        [shape((12, 40, 384), bf16)] * 2,
        [VM] * 4,
        [pltpu.VMEM((40, 384), f32), pltpu.VMEM((144, 128), f32), pltpu.VMEM((144, 128), f32)],
        1_000_000,
        2_000_000,
        12 << 20,
    )(cells, rim, near, rc)
    z_low = lax.ppermute(own_high, "gz", up)
    z_high = lax.ppermute(own_low, "gz", down)
    (parts,) = call(
        stages_kernel,
        shape((8, 120, 128), jnp.int16),
        [VM, VM, VM, HB, VM],
        [pltpu.VMEM((8, 144, 1024), bf16), pltpu.VMEM((8, 2, 192, 128), f32), pltpu.VMEM((8, 120, 128), f32)]
        + [pltpu.VMEM((8, 128, 2176), bf16), pltpu.SemaphoreType.DMA],
        2_000_000_000,
        10_000_000,
        FULL - (16 << 20),
    )(gathered, rc, kx, strip, wz)
    parts = lax.all_to_all(parts, "gz", 0, 0, tiled=True)
    (fields,) = call(
        weights_kernel,
        shape((94, 40, 384), f32),
        [VM] * 5 + [SM] * 2,
        [pltpu.VMEM(big, f32)],
        20_000_000,
        5_000_000,
    )(magnet, own_low, own_high, z_low, z_high, stiffness_table, saturation_table)
    (d_own,) = call(sum_kernel, shape((120, 128), f32), [VM], (), 100_000, 300_000, 8 << 20)(parts)
    d_low = lax.ppermute(d_own, "gz", up)
    d_high = lax.ppermute(d_own, "gz", down)
    state, demag = call(
        substeps_kernel,
        [shape((3, 4, 32, 256), f32), shape((2, 3, 16, 128), f32)],
        [HB] + [VM] * 3,
        [pltpu.VMEM((94, 40, 384), f32)]
        + [pltpu.VMEM((3,) + big, f32)] * 2
        + [pltpu.VMEM((3, 40, 384), f32), pltpu.VMEM((12, 3, 40, 128), f32)]
        + [pltpu.VMEM((288, 256), f32), pltpu.SemaphoreType.DMA((8,))],
        50_000_000,
        5_000_000,
        FULL - 14_000_000,
    )(fields, d_own, d_low, d_high)
    return (state, demag)


def solution(mesh):
    in_specs = (P(None, "gz", "gx", "gy"), P("gz", "gx", "gy"), P(), P(), P(), P(), P(), P())
    out_specs = (P(None, "gz", "gx", "gy"), P("gz", None, "gx", "gy"))
    return jax.shard_map(step, mesh=mesh, in_specs=in_specs, out_specs=out_specs, check_vma=False)
```
